128 devices in a mesh: dp: 64 (over z, y, x), fsdp: 2 (over core).
Axes of the slice: x: 4, y: 4, z: 4, core: 2. Of those that a mesh axis runs over, the one named last changes fastest.
Arguments:
- mel_panels: bfloat16 [8192, 10240], P(('dp', 'fsdp')), may hold values from -6 to 6
- frames: int32 [8192], P(('dp', 'fsdp')), may hold values from 0 to 128, as said below
- target: int32 [8192], P(('dp', 'fsdp')), may hold values from 0 to 63, as said below
- conv_first: bfloat16 [9, 256], P(None, 'fsdp'), may hold values from -2 to 2
- depth_a: bfloat16 [9, 256], P(None, 'fsdp'), may hold values from -3 to 3
- point_a: bfloat16 [256, 256], P(None, 'fsdp'), may hold values from -0.5 to 0.5
- depth_b: bfloat16 [9, 256], P(None, 'fsdp'), may hold values from -3 to 3
- point_b: bfloat16 [256, 256], P(None, 'fsdp'), may hold values from -0.5 to 0.5
- linear_weight: bfloat16 [2560, 1024], P(None, 'fsdp'), may hold values from -0.15625 to 0.15625
- norm_gain: bfloat16 [1024], P('fsdp'), may hold values from 0.099609375 to 1.8984375
- up_weight: bfloat16 [1024, 2048], P(None, 'fsdp'), may hold values from -0.1875 to 0.1875
- depth_kernel: bfloat16 [9, 1024], P(None, 'fsdp'), may hold values from -2 to 2
- conv_gain: bfloat16 [1024], P('fsdp'), may hold values from 0.099609375 to 1.8984375
- down_weight: bfloat16 [1024, 1024], P('fsdp'), may hold values from -0.1875 to 0.1875
- cotangent: bfloat16 [65536, 1024], P(('dp', 'fsdp')), may hold values from -6 to 6
Outputs:
- layer_out: bfloat16 [65536, 1024], P(('dp', 'fsdp'))
- grad_input: bfloat16 [65536, 1024], P(('dp', 'fsdp'))
- grad_down: float32 [1024, 1024], P('fsdp')
The draws below stay inside these ranges and needn't reach their ends.
Inputs may be any that keep to these rules, and one draw needn't show every extreme that they name: The slots of one loader are those of one index of dp and fsdp. A live slot holds a panel of 8 * m frames with 8 * m >= 32; frames = 0 marks an empty slot. Every device receives exactly 32 panels from the loaders of its own fsdp index, at most one from any loader, and one of them has 128 frames. `target`: only live slots are sent.
All inputs are finite; a program needn't handle non-finite values.
Results may differ from the reference program's by a relative error of at most 0.017.
Values may be sent and summed in bfloat16 or wider, within the bound.
A program may use at most 192 MiB of HBM per device.

```python
import jax
import jax.numpy as jnp
from jax import lax

MELS = 80
CH = 256
D = 1024
KER = 9
PANEL = 128
U_DEV = 32
U_LOAD = 64
SUBF = 10
ROWS_DEV = 512
PANELS = 8192
ROWS = 65536
N_DP = 64
N_FSDP = 2


def assign_panels(key):
    subkeys = jax.random.split(jax.random.fold_in(key, 11), 5)
    half_groups = N_DP // 2
    offsets = 2 * jax.random.permutation(subkeys[0], half_groups)[:U_DEV]
    parity = jax.random.randint(subkeys[1], (N_FSDP, N_DP), 0, 2)
    draws_len = 8 * jax.random.randint(subkeys[2], (N_FSDP, N_DP, U_DEV), max(PANEL // 32, 1), PANEL // 8 + 1)
    first_slot = jnp.arange(U_DEV)[None, None, :] == 0
    panel_len = jnp.where(first_slot, PANEL, draws_len)
    destinations = jnp.arange(N_DP)
    source = (destinations[None, :, None] + offsets[None, None, :] + parity[:, :, None]) % N_DP
    hit_table = source[:, None, :, :] == destinations[None, :, None, None]
    flat_hits = hit_table.reshape(N_FSDP, N_DP, N_DP * U_DEV).astype(jnp.int32)
    rank_table = jnp.cumsum(flat_hits, axis=2) - 1
    slot_ids = jnp.arange(U_LOAD)
    match_table = (rank_table[:, :, None, :] == slot_ids[None, None, :, None]) & (flat_hits[:, :, None, :] > 0)
    dest_of = jnp.broadcast_to(destinations[:, None], (N_DP, U_DEV)).reshape(-1)
    len_of = panel_len.reshape(N_FSDP, N_DP * U_DEV)
    filled = jnp.any(match_table, axis=3)
    fill_target = jnp.sum(jnp.where(match_table, dest_of[None, None, None, :], 0), axis=3)
    fill_len = jnp.sum(jnp.where(match_table, len_of[:, None, None, :], 0), axis=3)
    spare_dest = jax.random.randint(subkeys[3], (N_FSDP, N_DP, U_LOAD), 0, N_DP)
    targets = jnp.where(filled, fill_target, spare_dest)
    lengths = jnp.where(filled, fill_len, 0)
    scores = jax.random.randint(subkeys[4], (N_FSDP, N_DP, U_LOAD), 0, 1 << 20) * U_LOAD + slot_ids
    shuffle = jnp.argsort(scores, axis=2)
    targets = jnp.take_along_axis(targets, shuffle, axis=2)
    lengths = jnp.take_along_axis(lengths, shuffle, axis=2)
    targets = jnp.transpose(targets, (1, 0, 2)).reshape(-1).astype(jnp.int32)
    lengths = jnp.transpose(lengths, (1, 0, 2)).reshape(-1).astype(jnp.int32)
    return (targets, lengths)


def draw_frames(key, part):
    return assign_panels(key)[1]


def draw_target(key, part):
    return assign_panels(key)[0]


def levels(rng, shape, cuts, least, top_value):
    loudness, own = 1.0, jax.random.fold_in(rng, 6)
    for dim, blocks in cuts:
        steps = jnp.exp(jax.random.uniform(jax.random.fold_in(own, dim), (blocks,), jnp.float32, least / len(cuts), top_value / len(cuts)))
        loudness = loudness * jnp.repeat(steps, shape[dim] // blocks).reshape([-1 if axis == dim else 1 for axis in range(len(shape))])
    return loudness


def noise(rng, extent, scale, bound, cuts=(), kind=jnp.bfloat16):
    entries = jax.random.normal(rng, extent, jnp.float32) * scale
    if len(cuts) > 0:
        entries = levels(rng, extent, cuts, -0.22, 0.18) * entries
    return jnp.clip(entries, min=-bound, max=bound).astype(kind)


def setup_inputs(seed: int = 0) -> dict:
    splits = jax.random.split(jax.random.key(seed), 16)
    mel_panels = noise(splits[0], (PANELS, PANEL * MELS), 1.0, 6.0, ((0, 128),))
    frames = draw_frames(jax.random.fold_in(splits[15], 71), 0)
    target = draw_target(jax.random.fold_in(splits[15], 71), 0)
    conv_first = noise(splits[3], (9, CH), 9 ** -0.5, 2.0, ((1, 2),))
    depth_a = noise(splits[4], (9, CH), 4 ** -0.5, 3.0, ((1, 2),))
    point_a = noise(splits[5], (CH, CH), (CH // 2) ** -0.5, 0.5, ((1, 2),))
    depth_b = noise(splits[6], (9, CH), 4 ** -0.5, 3.0, ((1, 2),))
    point_b = noise(splits[7], (CH, CH), (CH // 2) ** -0.5, 0.5, ((1, 2),))
    linear_weight = noise(splits[8], (SUBF * CH, D), (SUBF * CH // 2) ** -0.5, 0.15625, ((1, 2),))
    norm_gain = jnp.clip(1.0 + 0.18 * jax.random.normal(splits[9], (D,), jnp.float32), 0.099609375, 1.8984375).astype(jnp.bfloat16)
    up_weight = noise(splits[10], (D, 2 * D), D ** -0.5, 0.1875, ((1, 2),))
    depth_kernel = noise(splits[11], (KER, D), KER ** -0.5, 2.0, ((1, 2),))
    conv_gain = jnp.clip(1.0 + 0.18 * jax.random.normal(splits[12], (D,), jnp.float32), 0.099609375, 1.8984375).astype(jnp.bfloat16)
    down_weight = noise(splits[13], (D, D), D ** -0.5, 0.1875, ((0, 2),))
    cotangent = noise(splits[14], (ROWS, D), 1.0, 6.0, ((0, 128),))
    return {"mel_panels": mel_panels, "frames": frames, "target": target, "conv_first": conv_first, "depth_a": depth_a, "point_a": point_a, "depth_b": depth_b, "point_b": point_b, "linear_weight": linear_weight, "norm_gain": norm_gain, "up_weight": up_weight, "depth_kernel": depth_kernel, "conv_gain": conv_gain, "down_weight": down_weight, "cotangent": cotangent}


EPSILON = 1e-05

def first_section(masked, weights):
    height = masked.shape[1] // 2
    breadth = masked.shape[2] // 2
    padded = jnp.pad(masked, ((0, 0), (1, 1), (1, 1)))
    summed = jnp.zeros((masked.shape[0], height, breadth, weights.shape[1]), jnp.float32)
    for i in range(3):
        for j in range(3):
            window = padded[:, i:i + 2 * height:2, j:j + 2 * breadth:2].astype(jnp.float32)
            summed = summed + window[:, :, :, None] * weights[3 * i + j].astype(jnp.float32)
    return jnp.maximum(summed, 0.0).astype(jnp.bfloat16)

def depth_stride(source, weights):
    height = source.shape[1] // 2
    breadth = source.shape[2] // 2
    padded = jnp.pad(source, ((0, 0), (1, 1), (1, 1), (0, 0)))
    summed = jnp.zeros((source.shape[0], height, breadth, source.shape[3]), jnp.float32)
    for i in range(3):
        for j in range(3):
            window = padded[:, i:i + 2 * height:2, j:j + 2 * breadth:2, :].astype(jnp.float32)
            summed = summed + window * weights[3 * i + j].astype(jnp.float32)
    return summed.astype(jnp.bfloat16)

def point_relu(spread, weights):
    shape_in = spread.shape
    mapped = jnp.dot(spread.reshape(-1, shape_in[3]), weights, preferred_element_type=jnp.float32)
    return jnp.maximum(mapped, 0.0).astype(jnp.bfloat16).reshape(shape_in[:3] + (weights.shape[1],))

def subsample(block_panels, block_lengths, conv_first, depth_a, point_a, depth_b, point_b):
    number = block_panels.shape[0]
    frames_in = block_panels.reshape(number, PANEL, MELS)
    inside = jnp.arange(PANEL)[None, :] < block_lengths[:, None]
    masked = jnp.where(inside[:, :, None], frames_in, jnp.zeros_like(frames_in))
    first = first_section(masked, conv_first)
    second = point_relu(depth_stride(first, depth_a), point_a)
    fourth = point_relu(depth_stride(second, depth_b), point_b)
    return fourth.reshape(number * fourth.shape[1], fourth.shape[2] * fourth.shape[3])

def depth_forward(gated, kernel, span):
    groups_in = gated.shape[0] // span
    half_width = kernel.shape[0] // 2
    shaped = jnp.pad(gated.reshape(groups_in, span, -1), ((0, 0), (half_width, half_width), (0, 0)))
    summed = jnp.zeros((groups_in, span, gated.shape[1]), jnp.float32)
    for k in range(kernel.shape[0]):
        summed = summed + shaped[:, k:k + span].astype(jnp.float32) * kernel[k].astype(jnp.float32)
    return summed.reshape(gated.shape[0], -1)

def depth_backward(upstream, kernel, span):
    groups_in = upstream.shape[0] // span
    half_width = kernel.shape[0] // 2
    shaped = jnp.pad(upstream.reshape(groups_in, span, -1), ((0, 0), (half_width, half_width), (0, 0)))
    summed = jnp.zeros((groups_in, span, upstream.shape[1]), jnp.float32)
    for k in range(kernel.shape[0]):
        offset = 2 * half_width - k
        summed = summed + shaped[:, offset:offset + span] * kernel[k].astype(jnp.float32)
    return summed.reshape(upstream.shape[0], -1)

def module_pass(features, keep, cotangent, norm_gain, up_weight, depth_kernel, conv_gain, down_weight, span):
    width = features.shape[1]
    values = features.astype(jnp.float32)
    centred = values - lax.optimization_barrier(jnp.mean(values, axis=1, keepdims=True))
    scale_one = lax.rsqrt(lax.optimization_barrier(jnp.mean(centred * centred, axis=1, keepdims=True)) + EPSILON)
    standard = centred * scale_one
    normed = (standard * norm_gain.astype(jnp.float32)).astype(jnp.bfloat16)
    projected = jnp.dot(normed, up_weight, preferred_element_type=jnp.float32)
    value_half = projected[:, :width]
    gate_half = jax.nn.sigmoid(projected[:, width:])
    row_keep = keep[:, None]
    gated = (row_keep * value_half * gate_half).astype(jnp.bfloat16)
    depthwise = depth_forward(gated, depth_kernel, span)
    centred_two = depthwise - lax.optimization_barrier(jnp.mean(depthwise, axis=1, keepdims=True))
    scale_two = lax.rsqrt(lax.optimization_barrier(jnp.mean(centred_two * centred_two, axis=1, keepdims=True)) + EPSILON)
    standard_two = centred_two * scale_two
    active = standard_two * conv_gain.astype(jnp.float32)
    swish_gate = jax.nn.sigmoid(active)
    hidden = (active * swish_gate).astype(jnp.bfloat16)
    mixed = jnp.dot(hidden, down_weight, preferred_element_type=jnp.float32)
    layer_out = (row_keep * (values + mixed)).astype(jnp.bfloat16)
    back_out = jnp.where(row_keep > 0, cotangent, jnp.zeros_like(cotangent))
    back_hidden = lax.dot_general(back_out, down_weight, (((1,), (1,)), ((), ())), preferred_element_type=jnp.float32)
    back_active = back_hidden * (swish_gate + active * swish_gate * (1.0 - swish_gate))
    gain_back = back_active * conv_gain.astype(jnp.float32)
    back_depth = scale_two * (gain_back - lax.optimization_barrier(jnp.mean(gain_back, axis=1, keepdims=True)) - standard_two * lax.optimization_barrier(jnp.mean(gain_back * standard_two, axis=1, keepdims=True)))
    back_gated = row_keep * depth_backward(back_depth, depth_kernel, span)
    back_proj = jnp.concatenate([back_gated * gate_half, back_gated * value_half * gate_half * (1.0 - gate_half)], axis=1).astype(jnp.bfloat16)
    back_normed = lax.dot_general(back_proj, up_weight, (((1,), (1,)), ((), ())), preferred_element_type=jnp.float32)
    gain_front = back_normed * norm_gain.astype(jnp.float32)
    back_input = scale_one * (gain_front - lax.optimization_barrier(jnp.mean(gain_front, axis=1, keepdims=True)) - standard * lax.optimization_barrier(jnp.mean(gain_front * standard, axis=1, keepdims=True)))
    grad_input = (back_out.astype(jnp.float32) + back_input).astype(jnp.bfloat16)
    return (layer_out, grad_input, hidden, back_out)

def reference(mel_panels, frames, target, conv_first, depth_a, point_a, depth_b, point_b, linear_weight, norm_gain, up_weight, depth_kernel, conv_gain, down_weight, cotangent):
    width_all = PANEL * MELS
    grouped_mel = mel_panels.reshape(N_DP, N_FSDP, U_LOAD, width_all)
    grouped_frames = frames.reshape(N_DP, N_FSDP, U_LOAD)
    grouped_target = target.reshape(N_DP, N_FSDP, U_LOAD)
    flat_index = jnp.arange(N_DP * U_LOAD, dtype=jnp.int32)
    destinations = jnp.arange(N_DP, dtype=jnp.int32)
    places = jnp.arange(U_DEV, dtype=jnp.int32)
    panel_parts = []
    length_parts = []
    for j in range(N_FSDP):
        frame_row = grouped_frames[:, j].reshape(-1)
        target_row = grouped_target[:, j].reshape(-1)
        flags = ((target_row[None, :] == destinations[:, None]) & (frame_row[None, :] > 0)).astype(jnp.int32)
        rank_table = (jnp.cumsum(flags, axis=1) - 1).astype(jnp.int32)
        match_table = (rank_table[:, None, :] == places[None, :, None]) & (flags[:, None, :] > 0)
        source = lax.optimization_barrier(jnp.sum(jnp.where(match_table, flat_index[None, None, :], 0), axis=2)).astype(jnp.int32)
        loader_pool = grouped_mel[:, j].reshape(N_DP * U_LOAD, width_all)
        panel_parts.append(loader_pool[source])
        length_parts.append(frame_row[source])
    panels = jnp.stack(panel_parts, axis=1).reshape(-1, width_all)
    lengths = jnp.stack(length_parts, axis=1).reshape(-1).astype(jnp.int32)
    per_block = 16
    blocks = panels.shape[0] // per_block

    def sub_block(block_args):
        flat_rows = subsample(block_args[0], block_args[1], conv_first, depth_a, point_a, depth_b, point_b)
        return jnp.dot(flat_rows, linear_weight, preferred_element_type=jnp.float32).astype(jnp.bfloat16)
    features = lax.map(sub_block, (panels.reshape(blocks, per_block, width_all), lengths.reshape(blocks, per_block))).reshape(ROWS, D)
    span = PANEL // 8
    keep = (jnp.arange(span)[None, :] < (lengths // 8)[:, None]).reshape(-1).astype(jnp.float32)
    devices = N_DP * N_FSDP

    def one_device(carry, device_args):
        layer_out, grad_input, hidden, back_out = module_pass(device_args[0], device_args[1], device_args[2], norm_gain, up_weight, depth_kernel, conv_gain, down_weight, span)
        contrib = lax.dot_general(hidden, back_out, (((0,), (0,)), ((), ())), preferred_element_type=jnp.float32)
        return (carry + contrib, (layer_out, grad_input))
    summed, (layers, grads) = lax.scan(one_device, jnp.zeros((D, D), jnp.float32), (features.reshape(devices, ROWS_DEV, D), keep.reshape(devices, ROWS_DEV), cotangent.reshape(devices, ROWS_DEV, D)))
    grad_down = summed / jnp.sqrt(jnp.float32(ROWS))
    return (layers.reshape(ROWS, D), grads.reshape(ROWS, D), grad_down)
```

```python
import functools
import math

import jax
import jax.numpy as jnp
from jax import lax
from jax.experimental import pallas as pl
from jax.experimental.pallas import tpu as pltpu
from jax.sharding import PartitionSpec as P

MELS = 80
PANEL = 128
EPSILON = 1e-05
SPAN = 16
GROUP = 8 * MELS
N_DP = 64
U_DEV = 32
ROWS = U_DEV * SPAN
D = 1024
CH = 256
HALF = CH // 2
MARK = 64.0
MESH = pl.DeviceIdType.MESH
VMEM_SPEC = pl.BlockSpec(memory_space=pltpu.VMEM)
ANY_SPEC = pl.BlockSpec(memory_space=pl.ANY)
BF = jnp.bfloat16
F32 = jnp.float32


def iota(shape, dim):
    return lax.broadcasted_iota(jnp.int32, shape, dim)


def dot(a, b):
    return jnp.dot(a, b, preferred_element_type=F32)


def shifted_peer(me, step):
    x = (me + step) % 4
    y = (me // 4 + step // 4) % 4
    z = (me // 16 + step // 16) % 4
    return z * 16 + y * 4 + x


N_SMALL = 8
N_BIG = 3


def exchange_kernel(*refs):
    frames, target, mel = refs[:3]
    small = refs[3 : 3 + N_SMALL]
    big = refs[11:14]
    windows, keep_out, band_out = refs[14:17]
    small_full = refs[17 : 17 + N_SMALL]
    big_other = refs[25:28]
    flat, outgoing, incoming = refs[28:31]
    small_other = refs[31 : 31 + N_SMALL]
    small_send, small_recv, big_send, big_recv, send_sem, recv_sem = refs[39:]

    me = lax.axis_index("dp")
    core = lax.axis_index("fsdp")
    other = 1 - core
    barrier = pltpu.get_barrier_semaphore()
    pl.semaphore_signal(barrier, inc=1, device_id=(me, other), device_id_type=MESH)

    def greet(step, carry):
        pl.semaphore_signal(
            barrier, inc=1, device_id=(shifted_peer(me, step), core), device_id_type=MESH
        )
        return carry

    lax.fori_loop(1, N_DP, greet, 0)

    picks = (target[...] == iota((N_DP, 64), 0)) & (frames[...] > 0)
    length = jnp.sum(jnp.where(picks, frames[...], 0), axis=1, keepdims=True)
    chosen = jnp.where(picks, 1.0, 0.0).astype(BF)
    for g in range(SPAN):
        rows = dot(chosen, mel[:, g * GROUP : (g + 1) * GROUP])
        rows = jnp.where(length > 8 * g, rows, MARK)
        for k in range(GROUP // 128):
            flat[k, pl.ds(g, N_DP, stride=SPAN), :] = rows[:, k * 128 : (k + 1) * 128]
    for k in range(GROUP // 128):
        outgoing[:, :, k * 128 : (k + 1) * 128] = flat[k].reshape(N_DP, SPAN, 128).astype(BF)

    pl.semaphore_wait(barrier, N_DP)

    partner = []
    for k in range(N_SMALL):
        copy = pltpu.make_async_remote_copy(
            src_ref=small[k],
            dst_ref=small_other[k],
            send_sem=small_send.at[k],
            recv_sem=small_recv.at[k],
            device_id=(me, other),
            device_id_type=MESH,
        )
        copy.start()
        partner.append(copy)

    def send(step, carry):
        pltpu.make_async_remote_copy(
            src_ref=outgoing.at[shifted_peer(me, step)],
            dst_ref=incoming.at[me],
            send_sem=send_sem,
            recv_sem=recv_sem,
            device_id=(shifted_peer(me, step), core),
            device_id_type=MESH,
        ).start()
        return carry

    lax.fori_loop(1, N_DP, send, 0)
    for k in range(N_BIG):
        copy = pltpu.make_async_remote_copy(
            src_ref=big[k],
            dst_ref=big_other[k],
            send_sem=big_send.at[k],
            recv_sem=big_recv.at[k],
            device_id=(me, other),
            device_id_type=MESH,
        )
        copy.start()
        partner.append(copy)
    incoming[pl.ds(me, 1)] = outgoing[pl.ds(me, 1)]

    for k in range(N_SMALL):
        partner[k].wait()
        width = small[k].shape[1]
        small_full[k][:, pl.ds(pl.multiple_of(core * width, 128), width)] = small[k][...]
        small_full[k][:, pl.ds(pl.multiple_of(other * width, 128), width)] = small_other[k][...]

    taps = small_full[0][...]
    row = iota((256, 9), 0)
    tap = iota((256, 9), 1)
    base = row - 80 * (tap // 3) - tap % 3 + 1

    def band(f, carry):
        b = base + (tap % 3) - 1
        hit = (base == 2 * f) & (b >= 0) & (b < MELS)
        column = dot(jnp.where(hit, 1.0, 0.0).astype(BF), taps)
        band_out[:, pl.ds(pl.multiple_of(f * CH, CH), CH)] = column.astype(BF)
        return carry

    lax.fori_loop(0, MELS // 2, band, 0)

    sent = outgoing.at[pl.ds(0, N_DP - 1)]
    got = incoming.at[pl.ds(0, N_DP - 1)]
    pltpu.make_async_copy(got, got, recv_sem).wait()

    total = N_DP * SPAN
    panels = incoming[...].reshape(total, GROUP)
    first_lane = jnp.where(iota((8, GROUP), 1) == 0, 1.0, 0.0).astype(BF)
    heads = lax.dot_general(
        first_lane, panels, (((1,), (1,)), ((), ())), preferred_element_type=F32
    )
    live_row = jnp.where(heads < MARK / 2, 1.0, 0.0).astype(BF)
    pick_heads = jnp.where(iota((total, 64), 0) == SPAN * iota((total, 64), 1), 1.0, 0.0)
    present = dot(live_row, pick_heads.astype(BF)).astype(BF)
    before = jnp.where(iota((64, 64), 0) < iota((64, 64), 1), 1.0, 0.0).astype(BF)
    place = dot(present, before).astype(BF)
    spread = jnp.where(iota((64, total), 1) // SPAN == iota((64, total), 0), 1.0, 0.0).astype(BF)
    present_row = dot(present, spread)[:1]
    place_row = dot(place, spread)[:1].astype(jnp.int32)
    goal = jnp.where(
        present_row > 0.5, (iota((1, total), 1) % SPAN) * U_DEV + place_row, -1
    )
    move = jnp.where(iota((ROWS, total), 0) == goal, 1.0, 0.0).astype(BF)
    x = dot(move, panels)
    keep = x[:, :1] < MARK / 2
    x = jnp.where(keep, x, 0.0)
    keep_out[...] = jnp.broadcast_to(jnp.where(keep, 1.0, 0.0), (ROWS, 128))

    late = jnp.concatenate([jnp.zeros((U_DEV, 128), F32), x[: ROWS - U_DEV, 512:]], axis=0)
    late = pltpu.roll(late, 80, 1)
    now = pltpu.roll(x[:, :256], 80, 1)
    lanes = iota((ROWS, 128), 1)
    w0 = jnp.concatenate([jnp.where(lanes < 80, late, now[:, :128]), now[:, 128:]], axis=1)
    windows[0:ROWS] = w0.astype(BF)
    windows[ROWS : 2 * ROWS] = pltpu.roll(x[:, :384], 384 - 80, 1)[:, :256].astype(BF)
    windows[2 * ROWS : 3 * ROWS] = pltpu.roll(x[:, 128:512], 384 - 112, 1)[:, :256].astype(BF)
    windows[3 * ROWS : 4 * ROWS] = pltpu.roll(x[:, 384:], 256 - 16, 1).astype(BF)

    pltpu.make_async_copy(sent, sent, send_sem).wait()
    for k in range(N_SMALL, N_SMALL + N_BIG):
        partner[k].wait()


def exchange(frames, target, mel, small, big):
    small_full = [jax.ShapeDtypeStruct((a.shape[0], 2 * a.shape[1]), BF) for a in small]
    shapes = [
        jax.ShapeDtypeStruct((4 * ROWS, 256), BF),
        jax.ShapeDtypeStruct((ROWS, 128), F32),
        jax.ShapeDtypeStruct((256, MELS // 2 * CH), BF),
        *small_full,
        *[jax.ShapeDtypeStruct(a.shape, BF) for a in big],
    ]
    out = pl.pallas_call(
        exchange_kernel,
        out_shape=shapes,
        in_specs=[VMEM_SPEC] * (3 + N_SMALL) + [ANY_SPEC] * N_BIG,
        out_specs=[VMEM_SPEC] * (3 + N_SMALL) + [ANY_SPEC] * N_BIG,
        scratch_shapes=[
            pltpu.VMEM((GROUP // 128, N_DP * SPAN, 128), F32),
            pltpu.VMEM((N_DP, SPAN, GROUP), BF),
            pltpu.VMEM((N_DP, SPAN, GROUP), BF),
            *[pltpu.VMEM(a.shape, BF) for a in small],
            pltpu.SemaphoreType.DMA((N_SMALL,)),
            pltpu.SemaphoreType.DMA((N_SMALL,)),
            pltpu.SemaphoreType.DMA((N_BIG,)),
            pltpu.SemaphoreType.DMA((N_BIG,)),
            pltpu.SemaphoreType.DMA,
            pltpu.SemaphoreType.DMA,
        ],
        compiler_params=pltpu.CompilerParams(
            collective_id=0, has_side_effects=True, vmem_limit_bytes=48 << 20
        ),
        name="exchange",
    )(frames, target, mel, *small, *big)
    return out[0], out[1], out[2], out[3 : 3 + N_SMALL], out[3 + N_SMALL :]


CHUNK = 64
PAD = U_DEV


def depth_rows(load, taps, r):
    total = None
    for i in range(3):
        for j in range(3):
            term = load(i, j, r) * taps[3 * i + j]
            total = term if total is None else total + term
    return total


def subsample_kernel(
    windows, band, depth_a, point_a, depth_b, point_b, linear_own, linear_other, out,
    first, spread_a, second, spread_b, fourth, linear, sems
):
    core = lax.axis_index("fsdp")
    width = D // 2
    loads = [
        pltpu.make_async_copy(
            linear_own, linear.at[:, pl.ds(pl.multiple_of(core * width, width), width)], sems.at[0]
        ),
        pltpu.make_async_copy(
            linear_other,
            linear.at[:, pl.ds(pl.multiple_of((1 - core) * width, width), width)],
            sems.at[1],
        ),
    ]
    for copy in loads:
        copy.start()
    first[:, 0] = jnp.zeros((4, PAD + ROWS, CH), BF)
    second[:, 0] = jnp.zeros((2, PAD + ROWS, CH), BF)
    for col in range(1, 5):
        first[3, col, 0:PAD] = jnp.zeros((PAD, CH), BF)
    for col in range(1, 3):
        second[1, col, 0:PAD] = jnp.zeros((PAD, CH), BF)
    taps_a = [jnp.broadcast_to(depth_a[k : k + 1], (CHUNK, CH)) for k in range(9)]
    taps_b = [jnp.broadcast_to(depth_b[k : k + 1], (CHUNK, CH)) for k in range(9)]

    def step(n, carry):
        for t in range(4):
            x = windows[t * ROWS : (t + 1) * ROWS]
            for f in range(4):
                w = band[:, pl.ds(pl.multiple_of(n * 4 * CH + f * CH, CH), CH)]
                first[t, 1 + f, PAD : PAD + ROWS] = jnp.maximum(dot(x, w), 0.0).astype(BF)
        for t2 in range(2):
            for f2 in range(2):

                def load(i, j, r):
                    t = 2 * t2 + i - 1
                    if t < 0:
                        return first[3, 2 * f2 + j, r : r + CHUNK]
                    return first[t, 2 * f2 + j, PAD + r : PAD + r + CHUNK]

                for r in range(0, ROWS, CHUNK):
                    spread_a[r : r + CHUNK] = depth_rows(load, taps_a, r)
                mapped = dot(spread_a[...], point_a[...])
                second[t2, 1 + f2, PAD : PAD + ROWS] = jnp.maximum(mapped, 0.0).astype(BF)

        def load_b(i, j, r):
            if i == 0:
                return second[1, j, r : r + CHUNK]
            return second[i - 1, j, PAD + r : PAD + r + CHUNK]

        for r in range(0, ROWS, CHUNK):
            spread_b[r : r + CHUNK] = depth_rows(load_b, taps_b, r)
        mapped = dot(spread_b[...], point_b[...])
        fourth[:, pl.ds(pl.multiple_of(n * CH, CH), CH)] = jnp.maximum(mapped, 0.0).astype(BF)
        for t in range(4):
            first[t, 0] = first[t, 4]
        for t2 in range(2):
            second[t2, 0] = second[t2, 2]
        return carry

    lax.fori_loop(0, 10, step, 0)
    for copy in loads:
        copy.wait()
    out[...] = dot(fourth[...], linear[...]).astype(BF)


def subsample(windows, band, depth_a, point_a, depth_b, point_b, linear_own, linear_other):
    return pl.pallas_call(
        subsample_kernel,
        out_shape=jax.ShapeDtypeStruct((ROWS, D), BF),
        in_specs=[VMEM_SPEC] * 6 + [ANY_SPEC] * 2,
        out_specs=VMEM_SPEC,
        scratch_shapes=[
            pltpu.VMEM((4, 5, PAD + ROWS, CH), BF),
            pltpu.VMEM((ROWS, CH), BF),
            pltpu.VMEM((2, 3, PAD + ROWS, CH), BF),
            pltpu.VMEM((ROWS, CH), BF),
            pltpu.VMEM((ROWS, 10 * CH), BF),
            pltpu.VMEM((10 * CH, D), BF),
            pltpu.SemaphoreType.DMA((2,)),
        ],
        compiler_params=pltpu.CompilerParams(vmem_limit_bytes=56 << 20),
        name="subsample",
    )(windows, band, depth_a, point_a, depth_b, point_b, linear_own, linear_other)


def in_blocks(value, dim, size):
    before, after = (value.shape[:dim], value.shape[dim + 1 :])
    return jnp.moveaxis(value.reshape(*before, size, -1, *after), dim, 0)


def sent_and_summed(value, axis, dim):
    size = lax.axis_size(axis)
    tiles = lax.all_to_all(in_blocks(value, dim, size), axis, 0, 0, tiled=True)
    return jnp.sum(tiles.astype(jnp.float32), axis=0)


def depth_forward(gated, kernel, span):
    groups_in = gated.shape[0] // span
    half_width = kernel.shape[0] // 2
    shaped = jnp.pad(gated.reshape(groups_in, span, -1), ((0, 0), (half_width, half_width), (0, 0)))
    summed = jnp.zeros((groups_in, span, gated.shape[1]), jnp.float32)
    for k in range(kernel.shape[0]):
        summed = summed + shaped[:, k : k + span].astype(jnp.float32) * kernel[k].astype(
            jnp.float32
        )
    return summed.reshape(gated.shape[0], -1)


def depth_backward(upstream, kernel, span):
    groups_in = upstream.shape[0] // span
    half_width = kernel.shape[0] // 2
    shaped = jnp.pad(
        upstream.reshape(groups_in, span, -1), ((0, 0), (half_width, half_width), (0, 0))
    )
    summed = jnp.zeros((groups_in, span, upstream.shape[1]), jnp.float32)
    for k in range(kernel.shape[0]):
        offset = 2 * half_width - k
        summed = summed + shaped[:, offset : offset + span] * kernel[k].astype(jnp.float32)
    return summed.reshape(upstream.shape[0], -1)


def module_pass(
    features, keep, cotangent, norm_gain, up_weight, depth_kernel, conv_gain, down_weight, span
):
    width = features.shape[1]
    values = features.astype(jnp.float32)
    centred = values - jnp.mean(values, axis=1, keepdims=True)
    scale_one = lax.rsqrt(jnp.mean(centred * centred, axis=1, keepdims=True) + EPSILON)
    standard = centred * scale_one
    normed = (standard * norm_gain.astype(jnp.float32)).astype(jnp.bfloat16)
    projected = jnp.dot(normed, up_weight, preferred_element_type=jnp.float32)
    value_half = projected[:, :width]
    gate_half = jax.nn.sigmoid(projected[:, width:])
    row_keep = keep[:, None]
    gated = (row_keep * value_half * gate_half).astype(jnp.bfloat16)
    depthwise = depth_forward(gated, depth_kernel, span)
    centred_two = depthwise - jnp.mean(depthwise, axis=1, keepdims=True)
    scale_two = lax.rsqrt(jnp.mean(centred_two * centred_two, axis=1, keepdims=True) + EPSILON)
    standard_two = centred_two * scale_two
    active = standard_two * conv_gain.astype(jnp.float32)
    swish_gate = jax.nn.sigmoid(active)
    hidden = (active * swish_gate).astype(jnp.bfloat16)
    mixed = jnp.dot(hidden, down_weight, preferred_element_type=jnp.float32)
    layer_out = (row_keep * (values + mixed)).astype(jnp.bfloat16)
    back_out = jnp.where(row_keep > 0, cotangent, jnp.zeros_like(cotangent))
    back_hidden = lax.dot_general(
        back_out, down_weight, (((1,), (1,)), ((), ())), preferred_element_type=jnp.float32
    )
    back_active = back_hidden * (swish_gate + active * swish_gate * (1.0 - swish_gate))
    gain_back = back_active * conv_gain.astype(jnp.float32)
    back_depth = scale_two * (
        gain_back
        - jnp.mean(gain_back, axis=1, keepdims=True)
        - standard_two * jnp.mean(gain_back * standard_two, axis=1, keepdims=True)
    )
    back_gated = row_keep * depth_backward(back_depth, depth_kernel, span)
    back_proj = jnp.concatenate(
        [back_gated * gate_half, back_gated * value_half * gate_half * (1.0 - gate_half)], axis=1
    ).astype(jnp.bfloat16)
    back_normed = lax.dot_general(
        back_proj, up_weight, (((1,), (1,)), ((), ())), preferred_element_type=jnp.float32
    )
    gain_front = back_normed * norm_gain.astype(jnp.float32)
    back_input = scale_one * (
        gain_front
        - jnp.mean(gain_front, axis=1, keepdims=True)
        - standard * jnp.mean(gain_front * standard, axis=1, keepdims=True)
    )
    grad_input = (back_out.astype(jnp.float32) + back_input).astype(jnp.bfloat16)
    return (layer_out, grad_input, hidden, back_out)


def by_panel(rows):
    return rows.reshape(SPAN, U_DEV, -1).transpose(1, 0, 2).reshape(ROWS, -1)


def joined(own, other, dim):
    order = lax.axis_index("fsdp") == 0
    first = jnp.where(order, own, other)
    last = jnp.where(order, other, own)
    return jnp.concatenate([first, last], axis=dim)


def local(
    mel_panels,
    frames,
    target,
    conv_first,
    depth_a,
    point_a,
    depth_b,
    point_b,
    linear_weight,
    norm_gain,
    up_weight,
    depth_kernel,
    conv_gain,
    down_weight,
    cotangent,
):
    small = (
        conv_first,
        depth_a,
        point_a,
        depth_b,
        point_b,
        norm_gain[None],
        depth_kernel,
        conv_gain[None],
    )
    big = (linear_weight, up_weight, down_weight)
    windows, keep, band, full, other = exchange(frames[None], target[None], mel_panels, small, big)
    features = subsample(windows, band, *full[1:5], linear_weight, other[0])
    features = by_panel(features)
    keep = by_panel(keep)[:, 0]
    layer_out, grad_input, hidden, back_out = module_pass(
        features,
        keep,
        cotangent,
        full[5][0],
        joined(up_weight, other[1], 1),
        full[6],
        full[7][0],
        joined(down_weight, other[2], 0),
        SPAN,
    )
    local_rows = sent_and_summed(
        lax.dot_general(
            hidden, back_out, (((0,), (0,)), ((), ())), preferred_element_type=jnp.float32
        ).astype(jnp.bfloat16),
        "fsdp",
        0,
    )
    summed = lax.psum(local_rows, "dp")
    grad_down = summed / jnp.sqrt(jnp.float32(ROWS * N_DP * 2))
    return (layer_out, grad_input, grad_down)


def solution(mesh):
    placed = (
        P(("dp", "fsdp"), None),
        P(("dp", "fsdp")),
        P(("dp", "fsdp")),
        P(None, "fsdp"),
        P(None, "fsdp"),
        P(None, "fsdp"),
        P(None, "fsdp"),
        P(None, "fsdp"),
        P(None, "fsdp"),
        P("fsdp"),
        P(None, "fsdp"),
        P(None, "fsdp"),
        P("fsdp"),
        P("fsdp", None),
        P(("dp", "fsdp"), None),
    )
    return jax.shard_map(
        local,
        mesh=mesh,
        in_specs=placed,
        out_specs=(P(("dp", "fsdp"), None), P(("dp", "fsdp"), None), P("fsdp", None)),
        check_vma=False,
    )
```

```python
import functools
import math

import jax
import jax.numpy as jnp
from jax import lax
from jax.experimental import pallas as pl
from jax.experimental.pallas import tpu as pltpu
from jax.sharding import PartitionSpec as P

MELS = 80
PANEL = 128
EPSILON = 1e-05
SPAN = 16
GROUP = 8 * MELS
N_DP = 64
U_DEV = 32
ROWS = U_DEV * SPAN
D = 1024
CH = 256
HALF = CH // 2
MARK = 64.0
MESH = pl.DeviceIdType.MESH
VMEM_SPEC = pl.BlockSpec(memory_space=pltpu.VMEM)
ANY_SPEC = pl.BlockSpec(memory_space=pl.ANY)
BF = jnp.bfloat16
F32 = jnp.float32


def iota(shape, dim):
    return lax.broadcasted_iota(jnp.int32, shape, dim)


def dot(a, b):
    return jnp.dot(a, b, preferred_element_type=F32)


def shifted_peer(me, step):
    x = (me + step) % 4
    y = (me // 4 + step // 4) % 4
    z = (me // 16 + step // 16) % 4
    return z * 16 + y * 4 + x


N_SMALL = 8
N_BIG = 3


def exchange_kernel(*refs):
    frames, target, mel = refs[:3]
    small = refs[3 : 3 + N_SMALL]
    big = refs[11:14]
    windows, keep_out, band_out = refs[14:17]
    small_full = refs[17 : 17 + N_SMALL]
    big_other = refs[25:28]
    flat, outgoing, incoming = refs[28:31]
    small_other = refs[31 : 31 + N_SMALL]
    small_send, small_recv, big_send, big_recv, send_sem, recv_sem = refs[39:]

    me = lax.axis_index("dp")
    core = lax.axis_index("fsdp")
    other = 1 - core
    barrier = pltpu.get_barrier_semaphore()
    pl.semaphore_signal(barrier, inc=1, device_id=(me, other), device_id_type=MESH)

    def greet(step, carry):
        pl.semaphore_signal(
            barrier, inc=1, device_id=(shifted_peer(me, step), core), device_id_type=MESH
        )
        return carry

    lax.fori_loop(1, N_DP, greet, 0)

    picks = (target[...] == iota((N_DP, 64), 0)) & (frames[...] > 0)
    length = jnp.sum(jnp.where(picks, frames[...], 0), axis=1, keepdims=True)
    chosen = jnp.where(picks, 1.0, 0.0).astype(BF)
    for g in range(SPAN):
        rows = dot(chosen, mel[:, g * GROUP : (g + 1) * GROUP])
        rows = jnp.where(length > 8 * g, rows, MARK)
        for k in range(GROUP // 128):
            flat[k, pl.ds(g, N_DP, stride=SPAN), :] = rows[:, k * 128 : (k + 1) * 128]
    for k in range(GROUP // 128):
        outgoing[:, :, k * 128 : (k + 1) * 128] = flat[k].reshape(N_DP, SPAN, 128).astype(BF)

    pl.semaphore_wait(barrier, N_DP)

    partner = []
    for k in range(N_SMALL):
        copy = pltpu.make_async_remote_copy(
            src_ref=small[k],
            dst_ref=small_other[k],
            send_sem=small_send.at[k],
            recv_sem=small_recv.at[k],
            device_id=(me, other),
            device_id_type=MESH,
        )
        copy.start()
        partner.append(copy)

    def send(step, carry):
        pltpu.make_async_remote_copy(
            src_ref=outgoing.at[shifted_peer(me, step)],
            dst_ref=incoming.at[me],
            send_sem=send_sem,
            recv_sem=recv_sem,
            device_id=(shifted_peer(me, step), core),
            device_id_type=MESH,
        ).start()
        return carry

    lax.fori_loop(1, N_DP, send, 0)
    for k in range(N_BIG):
        copy = pltpu.make_async_remote_copy(
            src_ref=big[k],
            dst_ref=big_other[k],
            send_sem=big_send.at[k],
            recv_sem=big_recv.at[k],
            device_id=(me, other),
            device_id_type=MESH,
        )
        copy.start()
        partner.append(copy)
    incoming[pl.ds(me, 1)] = outgoing[pl.ds(me, 1)]

    for k in range(N_SMALL):
        partner[k].wait()
        width = small[k].shape[1]
        small_full[k][:, pl.ds(pl.multiple_of(core * width, 128), width)] = small[k][...]
        small_full[k][:, pl.ds(pl.multiple_of(other * width, 128), width)] = small_other[k][...]

    taps = small_full[0][...]
    row = iota((256, 9), 0)
    tap = iota((256, 9), 1)
    base = row - 80 * (tap // 3) - tap % 3 + 1

    def band(f, carry):
        b = base + (tap % 3) - 1
        hit = (base == 2 * f) & (b >= 0) & (b < MELS)
        column = dot(jnp.where(hit, 1.0, 0.0).astype(BF), taps)
        band_out[:, pl.ds(pl.multiple_of(f * CH, CH), CH)] = column.astype(BF)
        return carry

    lax.fori_loop(0, MELS // 2, band, 0)

    sent = outgoing.at[pl.ds(0, N_DP - 1)]
    got = incoming.at[pl.ds(0, N_DP - 1)]
    pltpu.make_async_copy(got, got, recv_sem).wait()

    total = N_DP * SPAN
    panels = incoming[...].reshape(total, GROUP)
    first_lane = jnp.where(iota((8, GROUP), 1) == 0, 1.0, 0.0).astype(BF)
    heads = lax.dot_general(
        first_lane, panels, (((1,), (1,)), ((), ())), preferred_element_type=F32
    )
    live_row = jnp.where(heads < MARK / 2, 1.0, 0.0).astype(BF)
    pick_heads = jnp.where(iota((total, 64), 0) == SPAN * iota((total, 64), 1), 1.0, 0.0)
    present = dot(live_row, pick_heads.astype(BF)).astype(BF)
    before = jnp.where(iota((64, 64), 0) < iota((64, 64), 1), 1.0, 0.0).astype(BF)
    place = dot(present, before).astype(BF)
    spread = jnp.where(iota((64, total), 1) // SPAN == iota((64, total), 0), 1.0, 0.0).astype(BF)
    present_row = dot(present, spread)[:1]
    place_row = dot(place, spread)[:1].astype(jnp.int32)
    goal = jnp.where(
        present_row > 0.5, (iota((1, total), 1) % SPAN) * U_DEV + place_row, -1
    )
    move = jnp.where(iota((ROWS, total), 0) == goal, 1.0, 0.0).astype(BF)
    x = dot(move, panels)
    keep = x[:, :1] < MARK / 2
    x = jnp.where(keep, x, 0.0)
    keep_out[...] = jnp.broadcast_to(jnp.where(keep, 1.0, 0.0), (ROWS, 128))

    late = jnp.concatenate([jnp.zeros((U_DEV, 128), F32), x[: ROWS - U_DEV, 512:]], axis=0)
    late = pltpu.roll(late, 80, 1)
    now = pltpu.roll(x[:, :256], 80, 1)
    lanes = iota((ROWS, 128), 1)
    w0 = jnp.concatenate([jnp.where(lanes < 80, late, now[:, :128]), now[:, 128:]], axis=1)
    windows[0:ROWS] = w0.astype(BF)
    windows[ROWS : 2 * ROWS] = pltpu.roll(x[:, :384], 384 - 80, 1)[:, :256].astype(BF)
    windows[2 * ROWS : 3 * ROWS] = pltpu.roll(x[:, 128:512], 384 - 112, 1)[:, :256].astype(BF)
    windows[3 * ROWS : 4 * ROWS] = pltpu.roll(x[:, 384:], 256 - 16, 1).astype(BF)

    pltpu.make_async_copy(sent, sent, send_sem).wait()
    for k in range(N_SMALL, N_SMALL + N_BIG):
        partner[k].wait()


def exchange(frames, target, mel, small, big):
    small_full = [jax.ShapeDtypeStruct((a.shape[0], 2 * a.shape[1]), BF) for a in small]
    shapes = [
        jax.ShapeDtypeStruct((4 * ROWS, 256), BF),
        jax.ShapeDtypeStruct((ROWS, 128), F32),
        jax.ShapeDtypeStruct((256, MELS // 2 * CH), BF),
        *small_full,
        *[jax.ShapeDtypeStruct(a.shape, BF) for a in big],
    ]
    out = pl.pallas_call(
        exchange_kernel,
        out_shape=shapes,
        in_specs=[VMEM_SPEC] * (3 + N_SMALL) + [ANY_SPEC] * N_BIG,
        out_specs=[VMEM_SPEC] * (3 + N_SMALL) + [ANY_SPEC] * N_BIG,
        scratch_shapes=[
            pltpu.VMEM((GROUP // 128, N_DP * SPAN, 128), F32),
            pltpu.VMEM((N_DP, SPAN, GROUP), BF),
            pltpu.VMEM((N_DP, SPAN, GROUP), BF),
            *[pltpu.VMEM(a.shape, BF) for a in small],
            pltpu.SemaphoreType.DMA((N_SMALL,)),
            pltpu.SemaphoreType.DMA((N_SMALL,)),
            pltpu.SemaphoreType.DMA((N_BIG,)),
            pltpu.SemaphoreType.DMA((N_BIG,)),
            pltpu.SemaphoreType.DMA,
            pltpu.SemaphoreType.DMA,
        ],
        compiler_params=pltpu.CompilerParams(
            collective_id=0, has_side_effects=True, vmem_limit_bytes=48 << 20
        ),
        name="exchange",
    )(frames, target, mel, *small, *big)
    return out[0], out[1], out[2], out[3 : 3 + N_SMALL], out[3 + N_SMALL :]


CHUNK = 64
PAD = U_DEV


def depth_rows(load, taps, r):
    total = None
    for i in range(3):
        for j in range(3):
            term = load(i, j, r) * taps[3 * i + j]
            total = term if total is None else total + term
    return total


def subsample_kernel(
    windows, band, depth_a, point_a, depth_b, point_b, linear_own, linear_other, out,
    first, spread_a, second, spread_b, fourth, linear, sems
):
    core = lax.axis_index("fsdp")
    width = D // 2
    loads = [
        pltpu.make_async_copy(
            linear_own, linear.at[:, pl.ds(pl.multiple_of(core * width, width), width)], sems.at[0]
        ),
        pltpu.make_async_copy(
            linear_other,
            linear.at[:, pl.ds(pl.multiple_of((1 - core) * width, width), width)],
            sems.at[1],
        ),
    ]
    for copy in loads:
        copy.start()
    first[:, 0] = jnp.zeros((4, PAD + ROWS, CH), BF)
    second[:, 0] = jnp.zeros((2, PAD + ROWS, CH), BF)
    for col in range(1, 5):
        first[3, col, 0:PAD] = jnp.zeros((PAD, CH), BF)
    for col in range(1, 3):
        second[1, col, 0:PAD] = jnp.zeros((PAD, CH), BF)
    taps_a = [jnp.broadcast_to(depth_a[k : k + 1], (CHUNK, CH)) for k in range(9)]
    taps_b = [jnp.broadcast_to(depth_b[k : k + 1], (CHUNK, CH)) for k in range(9)]

    def step(n, carry):
        for t in range(4):
            x = windows[t * ROWS : (t + 1) * ROWS]
            for f in range(4):
                w = band[:, pl.ds(pl.multiple_of(n * 4 * CH + f * CH, CH), CH)]
                first[t, 1 + f, PAD : PAD + ROWS] = jnp.maximum(dot(x, w), 0.0).astype(BF)
        for t2 in range(2):
            for f2 in range(2):

                def load(i, j, r):
                    t = 2 * t2 + i - 1
                    if t < 0:
                        return first[3, 2 * f2 + j, r : r + CHUNK]
                    return first[t, 2 * f2 + j, PAD + r : PAD + r + CHUNK]

                for r in range(0, ROWS, CHUNK):
                    spread_a[r : r + CHUNK] = depth_rows(load, taps_a, r)
                mapped = dot(spread_a[...], point_a[...])
                second[t2, 1 + f2, PAD : PAD + ROWS] = jnp.maximum(mapped, 0.0).astype(BF)

        def load_b(i, j, r):
            if i == 0:
                return second[1, j, r : r + CHUNK]
            return second[i - 1, j, PAD + r : PAD + r + CHUNK]

        for r in range(0, ROWS, CHUNK):
            spread_b[r : r + CHUNK] = depth_rows(load_b, taps_b, r)
        mapped = dot(spread_b[...], point_b[...])
        fourth[:, pl.ds(pl.multiple_of(n * CH, CH), CH)] = jnp.maximum(mapped, 0.0).astype(BF)
        for t in range(4):
            first[t, 0] = first[t, 4]
        for t2 in range(2):
            second[t2, 0] = second[t2, 2]
        return carry

    lax.fori_loop(0, 10, step, 0)
    for copy in loads:
        copy.wait()
    out[...] = dot(fourth[...], linear[...]).astype(BF)


def subsample(windows, band, depth_a, point_a, depth_b, point_b, linear_own, linear_other):
    return pl.pallas_call(
        subsample_kernel,
        out_shape=jax.ShapeDtypeStruct((ROWS, D), BF),
        in_specs=[VMEM_SPEC] * 6 + [ANY_SPEC] * 2,
        out_specs=VMEM_SPEC,
        scratch_shapes=[
            pltpu.VMEM((4, 5, PAD + ROWS, CH), BF),
            pltpu.VMEM((ROWS, CH), BF),
            pltpu.VMEM((2, 3, PAD + ROWS, CH), BF),
            pltpu.VMEM((ROWS, CH), BF),
            pltpu.VMEM((ROWS, 10 * CH), BF),
            pltpu.VMEM((10 * CH, D), BF),
            pltpu.SemaphoreType.DMA((2,)),
        ],
        compiler_params=pltpu.CompilerParams(vmem_limit_bytes=56 << 20),
        name="subsample",
    )(windows, band, depth_a, point_a, depth_b, point_b, linear_own, linear_other)


def dot_t(a, b):
    return lax.dot_general(a, b, (((1,), (1,)), ((), ())), preferred_element_type=F32)


def dot_rows(a, b):
    return lax.dot_general(a, b, (((0,), (0,)), ((), ())), preferred_element_type=F32)


def row_mean(x):
    return jnp.sum(x, axis=1, keepdims=True) * (1.0 / D)


KER = 9
BORDER = KER // 2 * U_DEV
HALF_D = D // 2
N_TILE = 256


def lane_tile(n, start=0):
    return pl.ds(pl.multiple_of(start + n * N_TILE, N_TILE), N_TILE)


def module_kernel(
    features, keep, cotangent, norm_gain, depth_kernel, conv_gain,
    up_own, up_other, down_own, down_other,
    layer_out, grad_input, grad_down,
    up, down, normed, stats, gate_a, gate_b, gated, standard_two, slope, hidden, back_out,
    grad_own, to_partner, from_partner, part, parts, mine, shared, big, back_depth, back_proj,
    load_sems, partner_send, partner_recv, send_sems, recv_sems,
):
    me = lax.axis_index("dp")
    core = lax.axis_index("fsdp")
    other = 1 - core
    barrier = pltpu.get_barrier_semaphore()
    pl.semaphore_signal(barrier, inc=1, device_id=(me, other), device_id_type=MESH)

    def greet(step, carry):
        pl.semaphore_signal(
            barrier, inc=1, device_id=(shifted_peer(me, step), core), device_id_type=MESH
        )
        return carry

    lax.fori_loop(1, N_DP, greet, 0)

    def part_of(which, width):
        return pl.ds(pl.multiple_of(which * width, width), width)

    loads = [
        pltpu.make_async_copy(up_own, up.at[:, part_of(core, D)], load_sems.at[0]),
        pltpu.make_async_copy(up_other, up.at[:, part_of(other, D)], load_sems.at[1]),
        pltpu.make_async_copy(down_own, down.at[part_of(core, HALF_D)], load_sems.at[2]),
        pltpu.make_async_copy(down_other, down.at[part_of(other, HALF_D)], load_sems.at[3]),
    ]
    for copy in loads:
        copy.start()

    def rows_of(g, shift=0):
        return pl.ds(pl.multiple_of((g + shift) * U_DEV, U_DEV), U_DEV)

    gain_one = norm_gain[...].astype(F32)
    gain_two = conv_gain[...].astype(F32)

    def norm_rows(g, carry):
        values = features[rows_of(g)].astype(F32)
        mean = row_mean(values)
        centred = values - mean
        scale = lax.rsqrt(row_mean(centred * centred) + EPSILON)
        normed[rows_of(g)] = (centred * scale * gain_one).astype(BF)
        stats[0, rows_of(g)] = jnp.broadcast_to(mean, (U_DEV, 128))
        stats[1, rows_of(g)] = jnp.broadcast_to(scale, (U_DEV, 128))
        return carry

    lax.fori_loop(0, SPAN, norm_rows, 0)
    gated[0:BORDER] = jnp.zeros((BORDER, D), BF)
    gated[BORDER + ROWS :] = jnp.zeros((BORDER, D), BF)
    back_depth[0:BORDER] = jnp.zeros((BORDER, D), F32)
    back_depth[BORDER + ROWS :] = jnp.zeros((BORDER, D), F32)

    out_row = iota((ROWS, ROWS), 0)
    in_row = iota((ROWS, ROWS), 1)
    to_groups = jnp.where(in_row == (out_row % U_DEV) * SPAN + out_row // U_DEV, 1.0, 0.0)
    to_groups = to_groups.astype(BF)
    to_panels = jnp.where(in_row == (out_row % SPAN) * U_DEV + out_row // SPAN, 1.0, 0.0)
    to_panels = to_panels.astype(BF)

    loads[0].wait()
    loads[1].wait()

    def project(n, carry):
        value = dot(normed[...], up[:, lane_tile(n)])
        gate = jax.nn.sigmoid(dot(normed[...], up[:, lane_tile(n, D)]))
        both = value * gate
        gate_a[:, lane_tile(n)] = gate
        gate_b[:, lane_tile(n)] = both * (1.0 - gate)
        gated[BORDER : BORDER + ROWS, lane_tile(n)] = (keep[:, :1] * both).astype(BF)
        moved = dot(to_groups, cotangent[:, lane_tile(n)])
        back_out[:, lane_tile(n)] = jnp.where(keep[:, :1] > 0, moved, 0.0).astype(BF)
        return carry

    lax.fori_loop(0, D // N_TILE, project, 0)

    def conv_rows(g, carry):
        summed = None
        for k in range(KER):
            tap = depth_kernel[k : k + 1].astype(F32)
            term = gated[rows_of(g, k)].astype(F32) * tap
            summed = term if summed is None else summed + term
        centred = summed - row_mean(summed)
        scale = lax.rsqrt(row_mean(centred * centred) + EPSILON)
        standard = centred * scale
        active = standard * gain_two
        swish = jax.nn.sigmoid(active)
        act = active * swish
        hidden[rows_of(g)] = act.astype(BF)
        standard_two[rows_of(g)] = standard
        slope[rows_of(g)] = (swish + act * (1.0 - swish)) * gain_two
        stats[2, rows_of(g)] = jnp.broadcast_to(scale, (U_DEV, 128))
        return carry

    lax.fori_loop(0, SPAN, conv_rows, 0)

    def grad_rows(which, n):
        mine_rows = hidden[:, part_of(which, HALF_D)]
        return dot_rows(mine_rows, back_out[:, lane_tile(n)])

    def partner_grad(n, carry):
        to_partner[:, lane_tile(n)] = grad_rows(other, n).astype(BF)
        return carry

    lax.fori_loop(0, D // N_TILE, partner_grad, 0)
    pl.semaphore_wait(barrier, N_DP)
    swap = pltpu.make_async_remote_copy(
        src_ref=to_partner,
        dst_ref=from_partner,
        send_sem=partner_send,
        recv_sem=partner_recv,
        device_id=(me, other),
        device_id_type=MESH,
    )
    swap.start()

    def own_grad(n, carry):
        grad_own[:, lane_tile(n)] = grad_rows(core, n)
        return carry

    lax.fori_loop(0, D // N_TILE, own_grad, 0)
    loads[2].wait()
    loads[3].wait()
    swap.wait()

    def add_partner(n, carry):
        rows = pl.ds(pl.multiple_of(n * 64, 64), 64)
        part[rows] = (grad_own[rows] + from_partner[rows].astype(F32)).astype(BF)
        return carry

    lax.fori_loop(0, HALF_D // 64, add_partner, 0)

    def piece(ref, c):
        return ref.at[
            pl.ds(pl.multiple_of(c // 2 * SPAN, SPAN), SPAN),
            pl.ds(pl.multiple_of(c % 2 * HALF_D, HALF_D), HALF_D),
        ]

    def scatter(step, carry):
        peer = shifted_peer(me, step)
        pltpu.make_async_remote_copy(
            src_ref=piece(part, peer),
            dst_ref=parts.at[me],
            send_sem=send_sems.at[0],
            recv_sem=recv_sems.at[0],
            device_id=(peer, core),
            device_id_type=MESH,
        ).start()
        return carry

    lax.fori_loop(1, N_DP, scatter, 0)
    parts[pl.ds(me, 1)] = piece(part, me)[...][None]

    def output(n, carry):
        mixed = dot(hidden[...], down[:, lane_tile(n)])
        total = features[:, lane_tile(n)].astype(F32) + mixed
        total = (keep[:, :1] * total).astype(BF)
        layer_out[:, lane_tile(n)] = dot(to_panels, total).astype(BF)
        return carry

    lax.fori_loop(0, D // N_TILE, output, 0)

    def back_hidden(n, carry):
        rows = down[pl.ds(pl.multiple_of(n * N_TILE, N_TILE), N_TILE)]
        big[:, lane_tile(n)] = dot_t(back_out[...], rows)
        return carry

    lax.fori_loop(0, D // N_TILE, back_hidden, 0)

    def back_norm(g, carry):
        error = big[rows_of(g)] * slope[rows_of(g)]
        standard = standard_two[rows_of(g)]
        inner = error - row_mean(error) - standard * row_mean(error * standard)
        back_depth[rows_of(g, KER // 2)] = stats[2, rows_of(g), :1] * inner
        return carry

    lax.fori_loop(0, SPAN, back_norm, 0)

    def back_conv(g, carry):
        summed = None
        for k in range(KER):
            tap = depth_kernel[k : k + 1].astype(F32)
            term = back_depth[rows_of(g, KER - 1 - k)] * tap
            summed = term if summed is None else summed + term
        summed = keep[rows_of(g), :1] * summed
        back_proj[rows_of(g), 0:D] = (summed * gate_a[rows_of(g)]).astype(BF)
        back_proj[rows_of(g), D : 2 * D] = (summed * gate_b[rows_of(g)]).astype(BF)
        return carry

    lax.fori_loop(0, SPAN, back_conv, 0)

    def await_all(ref, sem):
        block = ref.at[pl.ds(0, N_DP - 1)]
        pltpu.make_async_copy(block, block, sem).wait()

    await_all(parts, recv_sems.at[0])
    total = parts[0].astype(F32)
    for k in range(1, N_DP):
        total = total + parts[k].astype(F32)
    mine[...] = (total * (1.0 / math.sqrt(ROWS * N_DP * 2))).astype(BF)

    def spread_mine(step, carry):
        pltpu.make_async_remote_copy(
            src_ref=mine,
            dst_ref=shared.at[me],
            send_sem=send_sems.at[1],
            recv_sem=recv_sems.at[1],
            device_id=(shifted_peer(me, step), core),
            device_id_type=MESH,
        ).start()
        return carry

    lax.fori_loop(1, N_DP, spread_mine, 0)
    shared[pl.ds(me, 1)] = mine[...][None]

    def back_up(n, carry):
        rows = up[pl.ds(pl.multiple_of(n * N_TILE, N_TILE), N_TILE)]
        big[:, lane_tile(n)] = dot_t(back_proj[...], rows)
        return carry

    lax.fori_loop(0, D // N_TILE, back_up, 0)

    def back_first(g, carry):
        front = big[rows_of(g)] * gain_one
        scale = stats[1, rows_of(g), :1]
        standard = (features[rows_of(g)].astype(F32) - stats[0, rows_of(g), :1]) * scale
        inner = front - row_mean(front) - standard * row_mean(front * standard)
        normed[rows_of(g)] = (back_out[rows_of(g)].astype(F32) + scale * inner).astype(BF)
        return carry

    lax.fori_loop(0, SPAN, back_first, 0)

    def reorder(n, carry):
        grad_input[:, lane_tile(n)] = dot(to_panels, normed[:, lane_tile(n)]).astype(BF)
        return carry

    lax.fori_loop(0, D // N_TILE, reorder, 0)
    await_all(shared, recv_sems.at[1])

    def place(c, carry):
        piece(grad_down, c)[...] = shared[c].astype(F32)
        return carry

    lax.fori_loop(0, N_DP, place, 0)
    await_all(parts, send_sems.at[0])
    await_all(shared, send_sems.at[1])


def module(features, keep, cotangent, norm_gain, depth_kernel, conv_gain, ups, downs):
    rows = (ROWS, D)
    return pl.pallas_call(
        module_kernel,
        out_shape=[
            jax.ShapeDtypeStruct(rows, BF),
            jax.ShapeDtypeStruct(rows, BF),
            jax.ShapeDtypeStruct((HALF_D, D), F32),
        ],
        in_specs=[VMEM_SPEC] * 6 + [ANY_SPEC] * 4,
        out_specs=[VMEM_SPEC] * 3,
        scratch_shapes=[
            pltpu.VMEM((D, 2 * D), BF),
            pltpu.VMEM((D, D), BF),
            pltpu.VMEM(rows, BF),
            pltpu.VMEM((3, ROWS, 128), F32),
            pltpu.VMEM(rows, F32),
            pltpu.VMEM(rows, F32),
            pltpu.VMEM((ROWS + 2 * BORDER, D), BF),
            pltpu.VMEM(rows, F32),
            pltpu.VMEM(rows, F32),
            pltpu.VMEM(rows, BF),
            pltpu.VMEM(rows, BF),
            pltpu.VMEM((HALF_D, D), F32),
            pltpu.VMEM((HALF_D, D), BF),
            pltpu.VMEM((HALF_D, D), BF),
            pltpu.VMEM((HALF_D, D), BF),
            pltpu.VMEM((N_DP, SPAN, HALF_D), BF),
            pltpu.VMEM((SPAN, HALF_D), BF),
            pltpu.VMEM((N_DP, SPAN, HALF_D), BF),
            pltpu.VMEM(rows, F32),
            pltpu.VMEM((ROWS + 2 * BORDER, D), F32),
            pltpu.VMEM((ROWS, 2 * D), BF),
            pltpu.SemaphoreType.DMA((4,)),
            pltpu.SemaphoreType.DMA,
            pltpu.SemaphoreType.DMA,
            pltpu.SemaphoreType.DMA((2,)),
            pltpu.SemaphoreType.DMA((2,)),
        ],
        compiler_params=pltpu.CompilerParams(
            collective_id=1, has_side_effects=True, vmem_limit_bytes=58 << 20
        ),
        name="module",
    )(features, keep, cotangent, norm_gain, depth_kernel, conv_gain, *ups, *downs)


def local(
    mel_panels,
    frames,
    target,
    conv_first,
    depth_a,
    point_a,
    depth_b,
    point_b,
    linear_weight,
    norm_gain,
    up_weight,
    depth_kernel,
    conv_gain,
    down_weight,
    cotangent,
):
    small = (
        conv_first,
        depth_a,
        point_a,
        depth_b,
        point_b,
        norm_gain[None],
        depth_kernel,
        conv_gain[None],
    )
    big = (linear_weight, up_weight, down_weight)
    windows, keep, band, full, other = exchange(frames[None], target[None], mel_panels, small, big)
    features = subsample(windows, band, *full[1:5], linear_weight, other[0])
    return module(
        features,
        keep,
        cotangent,
        full[5],
        full[6],
        full[7],
        (up_weight, other[1]),
        (down_weight, other[2]),
    )


def solution(mesh):
    placed = (
        P(("dp", "fsdp"), None),
        P(("dp", "fsdp")),
        P(("dp", "fsdp")),
        P(None, "fsdp"),
        P(None, "fsdp"),
        P(None, "fsdp"),
        P(None, "fsdp"),
        P(None, "fsdp"),
        P(None, "fsdp"),
        P("fsdp"),
        P(None, "fsdp"),
        P(None, "fsdp"),
        P("fsdp"),
        P("fsdp", None),
        P(("dp", "fsdp"), None),
    )
    return jax.shard_map(
        local,
        mesh=mesh,
        in_specs=placed,
        out_specs=(P(("dp", "fsdp"), None), P(("dp", "fsdp"), None), P("fsdp", None)),
        check_vma=False,
    )
```

```python
import functools
import math

import jax
import jax.numpy as jnp
from jax import lax
from jax.experimental import pallas as pl
from jax.experimental.pallas import tpu as pltpu
from jax.sharding import PartitionSpec as P

MELS = 80
PANEL = 128
EPSILON = 1e-05
SPAN = 16
GROUP = 8 * MELS
N_DP = 64
U_DEV = 32
ROWS = U_DEV * SPAN
D = 1024
CH = 256
HALF = CH // 2
MARK = 64.0
MESH = pl.DeviceIdType.MESH
VMEM_SPEC = pl.BlockSpec(memory_space=pltpu.VMEM)
ANY_SPEC = pl.BlockSpec(memory_space=pl.ANY)
BF = jnp.bfloat16
F32 = jnp.float32


def iota(shape, dim):
    return lax.broadcasted_iota(jnp.int32, shape, dim)


def dot(a, b):
    return jnp.dot(a, b, preferred_element_type=F32)


def shifted_peer(me, step):
    x = (me + step) % 4
    y = (me // 4 + step // 4) % 4
    z = (me // 16 + step // 16) % 4
    return z * 16 + y * 4 + x


N_SMALL = 8
N_BIG = 3


def exchange_kernel(*refs):
    frames, target, mel = refs[:3]
    small = refs[3 : 3 + N_SMALL]
    big = refs[11:14]
    windows, keep_out, band_out = refs[14:17]
    small_full = refs[17 : 17 + N_SMALL]
    big_other = refs[25:28]
    flat, outgoing, incoming = refs[28:31]
    small_other = refs[31 : 31 + N_SMALL]
    small_send, small_recv, big_send, big_recv, send_sem, recv_sem = refs[39:]

    me = lax.axis_index("dp")
    core = lax.axis_index("fsdp")
    other = 1 - core
    barrier = pltpu.get_barrier_semaphore()
    pl.semaphore_signal(barrier, inc=1, device_id=(me, other), device_id_type=MESH)

    def greet(step, carry):
        pl.semaphore_signal(
            barrier, inc=1, device_id=(shifted_peer(me, step), core), device_id_type=MESH
        )
        return carry

    lax.fori_loop(1, N_DP, greet, 0)

    picks = (target[...] == iota((N_DP, 64), 0)) & (frames[...] > 0)
    length = jnp.sum(jnp.where(picks, frames[...], 0), axis=1, keepdims=True)
    chosen = jnp.where(picks, 1.0, 0.0).astype(BF)
    for g in range(SPAN):
        rows = dot(chosen, mel[:, g * GROUP : (g + 1) * GROUP])
        rows = jnp.where(length > 8 * g, rows, MARK)
        for k in range(GROUP // 128):
            flat[k, pl.ds(g, N_DP, stride=SPAN), :] = rows[:, k * 128 : (k + 1) * 128]
    for k in range(GROUP // 128):
        outgoing[:, :, k * 128 : (k + 1) * 128] = flat[k].reshape(N_DP, SPAN, 128).astype(BF)

    pl.semaphore_wait(barrier, N_DP)

    partner = []
    for k in range(N_SMALL):
        copy = pltpu.make_async_remote_copy(
            src_ref=small[k],
            dst_ref=small_other[k],
            send_sem=small_send.at[k],
            recv_sem=small_recv.at[k],
            device_id=(me, other),
            device_id_type=MESH,
        )
        copy.start()
        partner.append(copy)

    def send(step, carry):
        pltpu.make_async_remote_copy(
            src_ref=outgoing.at[shifted_peer(me, step)],
            dst_ref=incoming.at[me],
            send_sem=send_sem,
            recv_sem=recv_sem,
            device_id=(shifted_peer(me, step), core),
            device_id_type=MESH,
        ).start()
        return carry

    lax.fori_loop(1, N_DP, send, 0)
    for k in range(N_BIG):
        copy = pltpu.make_async_remote_copy(
            src_ref=big[k],
            dst_ref=big_other[k],
            send_sem=big_send.at[k],
            recv_sem=big_recv.at[k],
            device_id=(me, other),
            device_id_type=MESH,
        )
        copy.start()
        partner.append(copy)
    incoming[pl.ds(me, 1)] = outgoing[pl.ds(me, 1)]

    for k in range(N_SMALL):
        partner[k].wait()
        width = small[k].shape[1]
        small_full[k][:, pl.ds(pl.multiple_of(core * width, 128), width)] = small[k][...]
        small_full[k][:, pl.ds(pl.multiple_of(other * width, 128), width)] = small_other[k][...]

    taps = small_full[0][...]
    row = iota((256, 9), 0)
    tap = iota((256, 9), 1)
    base = row - 80 * (tap // 3) - tap % 3 + 1

    def band(f, carry):
        b = base + (tap % 3) - 1
        hit = (base == 2 * f) & (b >= 0) & (b < MELS)
        column = dot(jnp.where(hit, 1.0, 0.0).astype(BF), taps)
        band_out[:, pl.ds(pl.multiple_of(f * CH, CH), CH)] = column.astype(BF)
        return carry

    lax.fori_loop(0, MELS // 2, band, 0)

    sent = outgoing.at[pl.ds(0, N_DP - 1)]
    got = incoming.at[pl.ds(0, N_DP - 1)]
    pltpu.make_async_copy(got, got, recv_sem).wait()

    total = N_DP * SPAN
    panels = incoming[...].reshape(total, GROUP)
    first_lane = jnp.where(iota((8, GROUP), 1) == 0, 1.0, 0.0).astype(BF)
    heads = lax.dot_general(
        first_lane, panels, (((1,), (1,)), ((), ())), preferred_element_type=F32
    )
    live_row = jnp.where(heads < MARK / 2, 1.0, 0.0).astype(BF)
    pick_heads = jnp.where(iota((total, 64), 0) == SPAN * iota((total, 64), 1), 1.0, 0.0)
    present = dot(live_row, pick_heads.astype(BF)).astype(BF)
    before = jnp.where(iota((64, 64), 0) < iota((64, 64), 1), 1.0, 0.0).astype(BF)
    place = dot(present, before).astype(BF)
    spread = jnp.where(iota((64, total), 1) // SPAN == iota((64, total), 0), 1.0, 0.0).astype(BF)
    present_row = dot(present, spread)[:1]
    place_row = dot(place, spread)[:1].astype(jnp.int32)
    goal = jnp.where(
        present_row > 0.5, (iota((1, total), 1) % SPAN) * U_DEV + place_row, -1
    )
    move = jnp.where(iota((ROWS, total), 0) == goal, 1.0, 0.0).astype(BF)
    x = dot(move, panels)
    keep = x[:, :1] < MARK / 2
    x = jnp.where(keep, x, 0.0)
    keep_out[...] = jnp.broadcast_to(jnp.where(keep, 1.0, 0.0), (ROWS, 128))

    late = jnp.concatenate([jnp.zeros((U_DEV, 128), F32), x[: ROWS - U_DEV, 512:]], axis=0)
    late = pltpu.roll(late, 80, 1)
    now = pltpu.roll(x[:, :256], 80, 1)
    lanes = iota((ROWS, 128), 1)
    w0 = jnp.concatenate([jnp.where(lanes < 80, late, now[:, :128]), now[:, 128:]], axis=1)
    windows[0:ROWS] = w0.astype(BF)
    windows[ROWS : 2 * ROWS] = pltpu.roll(x[:, :384], 384 - 80, 1)[:, :256].astype(BF)
    windows[2 * ROWS : 3 * ROWS] = pltpu.roll(x[:, 128:512], 384 - 112, 1)[:, :256].astype(BF)
    windows[3 * ROWS : 4 * ROWS] = pltpu.roll(x[:, 384:], 256 - 16, 1).astype(BF)

    pltpu.make_async_copy(sent, sent, send_sem).wait()
    for k in range(N_SMALL, N_SMALL + N_BIG):
        partner[k].wait()


def exchange(frames, target, mel, small, big):
    small_full = [jax.ShapeDtypeStruct((a.shape[0], 2 * a.shape[1]), BF) for a in small]
    shapes = [
        jax.ShapeDtypeStruct((4 * ROWS, 256), BF),
        jax.ShapeDtypeStruct((ROWS, 128), F32),
        jax.ShapeDtypeStruct((256, MELS // 2 * CH), BF),
        *small_full,
        *[jax.ShapeDtypeStruct(a.shape, BF) for a in big],
    ]
    out = pl.pallas_call(
        exchange_kernel,
        out_shape=shapes,
        in_specs=[VMEM_SPEC] * (3 + N_SMALL) + [ANY_SPEC] * N_BIG,
        out_specs=[VMEM_SPEC] * (3 + N_SMALL) + [ANY_SPEC] * N_BIG,
        scratch_shapes=[
            pltpu.VMEM((GROUP // 128, N_DP * SPAN, 128), F32),
            pltpu.VMEM((N_DP, SPAN, GROUP), BF),
            pltpu.VMEM((N_DP, SPAN, GROUP), BF),
            *[pltpu.VMEM(a.shape, BF) for a in small],
            pltpu.SemaphoreType.DMA((N_SMALL,)),
            pltpu.SemaphoreType.DMA((N_SMALL,)),
            pltpu.SemaphoreType.DMA((N_BIG,)),
            pltpu.SemaphoreType.DMA((N_BIG,)),
            pltpu.SemaphoreType.DMA,
            pltpu.SemaphoreType.DMA,
        ],
        compiler_params=pltpu.CompilerParams(
            collective_id=0, has_side_effects=True, vmem_limit_bytes=67043328
        ),
        name="exchange",
    )(frames, target, mel, *small, *big)
    return out[0], out[1], out[2], out[3 : 3 + N_SMALL], out[3 + N_SMALL :]


CHUNK = 64
PAD = U_DEV


def depth_rows(load, taps, r):
    total = None
    for i in range(3):
        for j in range(3):
            term = load(i, j, r) * taps[3 * i + j]
            total = term if total is None else total + term
    return total


def subsample_kernel(
    windows, band, depth_a, point_a, depth_b, point_b, linear_own, linear_other, out,
    first, spread_a, second, spread_b, fourth, linear, sems
):
    core = lax.axis_index("fsdp")
    width = D // 2
    loads = [
        pltpu.make_async_copy(
            linear_own, linear.at[:, pl.ds(pl.multiple_of(core * width, width), width)], sems.at[0]
        ),
        pltpu.make_async_copy(
            linear_other,
            linear.at[:, pl.ds(pl.multiple_of((1 - core) * width, width), width)],
            sems.at[1],
        ),
    ]
    for copy in loads:
        copy.start()
    first[:, 0] = jnp.zeros((4, PAD + ROWS, CH), BF)
    second[:, 0] = jnp.zeros((2, PAD + ROWS, CH), BF)
    for col in range(1, 5):
        first[3, col, 0:PAD] = jnp.zeros((PAD, CH), BF)
    for col in range(1, 3):
        second[1, col, 0:PAD] = jnp.zeros((PAD, CH), BF)
    taps_a = [jnp.broadcast_to(depth_a[k : k + 1], (CHUNK, CH)) for k in range(9)]
    taps_b = [jnp.broadcast_to(depth_b[k : k + 1], (CHUNK, CH)) for k in range(9)]

    def step(n, carry):
        for t in range(4):
            x = windows[t * ROWS : (t + 1) * ROWS]
            for f in range(4):
                w = band[:, pl.ds(pl.multiple_of(n * 4 * CH + f * CH, CH), CH)]
                first[t, 1 + f, PAD : PAD + ROWS] = jnp.maximum(dot(x, w), 0.0).astype(BF)
        for t2 in range(2):
            for f2 in range(2):

                def load(i, j, r):
                    t = 2 * t2 + i - 1
                    if t < 0:
                        return first[3, 2 * f2 + j, r : r + CHUNK]
                    return first[t, 2 * f2 + j, PAD + r : PAD + r + CHUNK]

                for r in range(0, ROWS, CHUNK):
                    spread_a[r : r + CHUNK] = depth_rows(load, taps_a, r)
                mapped = dot(spread_a[...], point_a[...])
                second[t2, 1 + f2, PAD : PAD + ROWS] = jnp.maximum(mapped, 0.0).astype(BF)

        def load_b(i, j, r):
            if i == 0:
                return second[1, j, r : r + CHUNK]
            return second[i - 1, j, PAD + r : PAD + r + CHUNK]

        for r in range(0, ROWS, CHUNK):
            spread_b[r : r + CHUNK] = depth_rows(load_b, taps_b, r)
        mapped = dot(spread_b[...], point_b[...])
        fourth[:, pl.ds(pl.multiple_of(n * CH, CH), CH)] = jnp.maximum(mapped, 0.0).astype(BF)
        for t in range(4):
            first[t, 0] = first[t, 4]
        for t2 in range(2):
            second[t2, 0] = second[t2, 2]
        return carry

    lax.fori_loop(0, 10, step, 0)
    for copy in loads:
        copy.wait()
    out[...] = dot(fourth[...], linear[...]).astype(BF)


def subsample(windows, band, depth_a, point_a, depth_b, point_b, linear_own, linear_other):
    return pl.pallas_call(
        subsample_kernel,
        out_shape=jax.ShapeDtypeStruct((ROWS, D), BF),
        in_specs=[VMEM_SPEC] * 6 + [ANY_SPEC] * 2,
        out_specs=VMEM_SPEC,
        scratch_shapes=[
            pltpu.VMEM((4, 5, PAD + ROWS, CH), BF),
            pltpu.VMEM((ROWS, CH), BF),
            pltpu.VMEM((2, 3, PAD + ROWS, CH), BF),
            pltpu.VMEM((ROWS, CH), BF),
            pltpu.VMEM((ROWS, 10 * CH), BF),
            pltpu.VMEM((10 * CH, D), BF),
            pltpu.SemaphoreType.DMA((2,)),
        ],
        compiler_params=pltpu.CompilerParams(vmem_limit_bytes=67043328),
        name="subsample",
    )(windows, band, depth_a, point_a, depth_b, point_b, linear_own, linear_other)


def dot_t(a, b):
    return lax.dot_general(a, b, (((1,), (1,)), ((), ())), preferred_element_type=F32)


def dot_rows(a, b):
    return lax.dot_general(a, b, (((0,), (0,)), ((), ())), preferred_element_type=F32)


def row_mean(x):
    return jnp.sum(x, axis=1, keepdims=True) * (1.0 / D)


KER = 9
BORDER = KER // 2 * U_DEV
HALF_D = D // 2
N_TILE = 256


def lane_tile(n, start=0):
    return pl.ds(pl.multiple_of(start + n * N_TILE, N_TILE), N_TILE)


def module_kernel(
    features, keep, cotangent, norm_gain, depth_kernel, conv_gain,
    up_own, up_other, down_own, down_other,
    layer_out, grad_input, grad_down,
    up, down, normed, stats, gate_a, gate_b, gated, standard_two, slope, hidden, back_out,
    grad_own, to_partner, from_partner, part, parts, mine, shared, big, back_depth, back_proj,
    load_sems, partner_send, partner_recv, send_sems, recv_sems,
):
    me = lax.axis_index("dp")
    core = lax.axis_index("fsdp")
    other = 1 - core
    barrier = pltpu.get_barrier_semaphore()
    pl.semaphore_signal(barrier, inc=1, device_id=(me, other), device_id_type=MESH)

    def greet(step, carry):
        pl.semaphore_signal(
            barrier, inc=1, device_id=(shifted_peer(me, step), core), device_id_type=MESH
        )
        return carry

    lax.fori_loop(1, N_DP, greet, 0)

    def part_of(which, width):
        return pl.ds(pl.multiple_of(which * width, width), width)

    loads = [
        pltpu.make_async_copy(up_own, up.at[:, part_of(core, D)], load_sems.at[0]),
        pltpu.make_async_copy(up_other, up.at[:, part_of(other, D)], load_sems.at[1]),
        pltpu.make_async_copy(down_own, down.at[part_of(core, HALF_D)], load_sems.at[2]),
        pltpu.make_async_copy(down_other, down.at[part_of(other, HALF_D)], load_sems.at[3]),
    ]
    for copy in loads:
        copy.start()

    def rows_of(g, shift=0):
        return pl.ds(pl.multiple_of((g + shift) * U_DEV, U_DEV), U_DEV)

    gain_one = norm_gain[...].astype(F32)
    gain_two = conv_gain[...].astype(F32)

    def norm_rows(g, carry):
        values = features[rows_of(g)].astype(F32)
        mean = row_mean(values)
        centred = values - mean
        scale = lax.rsqrt(row_mean(centred * centred) + EPSILON)
        normed[rows_of(g)] = (centred * scale * gain_one).astype(BF)
        stats[0, rows_of(g)] = jnp.broadcast_to(mean, (U_DEV, 128))
        stats[1, rows_of(g)] = jnp.broadcast_to(scale, (U_DEV, 128))
        return carry

    lax.fori_loop(0, SPAN, norm_rows, 0)
    gated[0:BORDER] = jnp.zeros((BORDER, D), BF)
    gated[BORDER + ROWS :] = jnp.zeros((BORDER, D), BF)
    back_depth[0:BORDER] = jnp.zeros((BORDER, D), F32)
    back_depth[BORDER + ROWS :] = jnp.zeros((BORDER, D), F32)

    out_row = iota((ROWS, ROWS), 0)
    in_row = iota((ROWS, ROWS), 1)
    to_groups = jnp.where(in_row == (out_row % U_DEV) * SPAN + out_row // U_DEV, 1.0, 0.0)
    to_groups = to_groups.astype(BF)
    to_panels = jnp.where(in_row == (out_row % SPAN) * U_DEV + out_row // SPAN, 1.0, 0.0)
    to_panels = to_panels.astype(BF)

    loads[0].wait()
    loads[1].wait()

    def project(n, carry):
        value = dot(normed[...], up[:, lane_tile(n)])
        gate = jax.nn.sigmoid(dot(normed[...], up[:, lane_tile(n, D)]))
        both = value * gate
        gate_a[:, lane_tile(n)] = gate
        gate_b[:, lane_tile(n)] = both * (1.0 - gate)
        gated[BORDER : BORDER + ROWS, lane_tile(n)] = (keep[:, :1] * both).astype(BF)
        moved = dot(to_groups, cotangent[:, lane_tile(n)])
        back_out[:, lane_tile(n)] = jnp.where(keep[:, :1] > 0, moved, 0.0).astype(BF)
        return carry

    lax.fori_loop(0, D // N_TILE, project, 0)

    def conv_rows(g, carry):
        summed = None
        for k in range(KER):
            tap = depth_kernel[k : k + 1].astype(F32)
            term = gated[rows_of(g, k)].astype(F32) * tap
            summed = term if summed is None else summed + term
        centred = summed - row_mean(summed)
        scale = lax.rsqrt(row_mean(centred * centred) + EPSILON)
        standard = centred * scale
        active = standard * gain_two
        swish = jax.nn.sigmoid(active)
        act = active * swish
        hidden[rows_of(g)] = act.astype(BF)
        standard_two[rows_of(g)] = standard
        slope[rows_of(g)] = (swish + act * (1.0 - swish)) * gain_two
        stats[2, rows_of(g)] = jnp.broadcast_to(scale, (U_DEV, 128))
        return carry

    lax.fori_loop(0, SPAN, conv_rows, 0)

    def grad_rows(which, n):
        mine_rows = hidden[:, part_of(which, HALF_D)]
        return dot_rows(mine_rows, back_out[:, lane_tile(n)])

    def partner_grad(n, carry):
        to_partner[:, lane_tile(n)] = grad_rows(other, n).astype(BF)
        return carry

    lax.fori_loop(0, D // N_TILE, partner_grad, 0)
    pl.semaphore_wait(barrier, N_DP)
    swap = pltpu.make_async_remote_copy(
        src_ref=to_partner,
        dst_ref=from_partner,
        send_sem=partner_send,
        recv_sem=partner_recv,
        device_id=(me, other),
        device_id_type=MESH,
    )
    swap.start()

    def own_grad(n, carry):
        grad_own[:, lane_tile(n)] = grad_rows(core, n)
        return carry

    lax.fori_loop(0, D // N_TILE, own_grad, 0)
    loads[2].wait()
    loads[3].wait()
    swap.wait()

    def add_partner(n, carry):
        rows = pl.ds(pl.multiple_of(n * 64, 64), 64)
        part[rows] = (grad_own[rows] + from_partner[rows].astype(F32)).astype(BF)
        return carry

    lax.fori_loop(0, HALF_D // 64, add_partner, 0)

    def piece(ref, c):
        return ref.at[
            pl.ds(pl.multiple_of(c // 2 * SPAN, SPAN), SPAN),
            pl.ds(pl.multiple_of(c % 2 * HALF_D, HALF_D), HALF_D),
        ]

    def scatter(step, carry):
        peer = shifted_peer(me, step)
        pltpu.make_async_remote_copy(
            src_ref=piece(part, peer),
            dst_ref=parts.at[me],
            send_sem=send_sems.at[0],
            recv_sem=recv_sems.at[0],
            device_id=(peer, core),
            device_id_type=MESH,
        ).start()
        return carry

    lax.fori_loop(1, N_DP, scatter, 0)
    parts[pl.ds(me, 1)] = piece(part, me)[...][None]

    def output(n, carry):
        mixed = dot(hidden[...], down[:, lane_tile(n)])
        total = features[:, lane_tile(n)].astype(F32) + mixed
        total = (keep[:, :1] * total).astype(BF)
        layer_out[:, lane_tile(n)] = dot(to_panels, total).astype(BF)
        return carry

    lax.fori_loop(0, D // N_TILE, output, 0)

    def back_hidden(n, carry):
        rows = down[pl.ds(pl.multiple_of(n * N_TILE, N_TILE), N_TILE)]
        big[:, lane_tile(n)] = dot_t(back_out[...], rows)
        return carry

    lax.fori_loop(0, D // N_TILE, back_hidden, 0)

    def back_norm(g, carry):
        error = big[rows_of(g)] * slope[rows_of(g)]
        standard = standard_two[rows_of(g)]
        inner = error - row_mean(error) - standard * row_mean(error * standard)
        back_depth[rows_of(g, KER // 2)] = stats[2, rows_of(g), :1] * inner
        return carry

    lax.fori_loop(0, SPAN, back_norm, 0)

    def back_conv(g, carry):
        summed = None
        for k in range(KER):
            tap = depth_kernel[k : k + 1].astype(F32)
            term = back_depth[rows_of(g, KER - 1 - k)] * tap
            summed = term if summed is None else summed + term
        summed = keep[rows_of(g), :1] * summed
        back_proj[rows_of(g), 0:D] = (summed * gate_a[rows_of(g)]).astype(BF)
        back_proj[rows_of(g), D : 2 * D] = (summed * gate_b[rows_of(g)]).astype(BF)
        return carry

    lax.fori_loop(0, SPAN, back_conv, 0)

    def await_all(ref, sem):
        block = ref.at[pl.ds(0, N_DP - 1)]
        pltpu.make_async_copy(block, block, sem).wait()

    await_all(parts, recv_sems.at[0])
    total = parts[0].astype(F32)
    for k in range(1, N_DP):
        total = total + parts[k].astype(F32)
    mine[...] = (total * (1.0 / math.sqrt(ROWS * N_DP * 2))).astype(BF)

    def spread_mine(step, carry):
        pltpu.make_async_remote_copy(
            src_ref=mine,
            dst_ref=shared.at[me],
            send_sem=send_sems.at[1],
            recv_sem=recv_sems.at[1],
            device_id=(shifted_peer(me, step), core),
            device_id_type=MESH,
        ).start()
        return carry

    lax.fori_loop(1, N_DP, spread_mine, 0)
    shared[pl.ds(me, 1)] = mine[...][None]

    def back_up(n, carry):
        rows = up[pl.ds(pl.multiple_of(n * N_TILE, N_TILE), N_TILE)]
        big[:, lane_tile(n)] = dot_t(back_proj[...], rows)
        return carry

    lax.fori_loop(0, D // N_TILE, back_up, 0)

    def back_first(g, carry):
        front = big[rows_of(g)] * gain_one
        scale = stats[1, rows_of(g), :1]
        standard = (features[rows_of(g)].astype(F32) - stats[0, rows_of(g), :1]) * scale
        inner = front - row_mean(front) - standard * row_mean(front * standard)
        normed[rows_of(g)] = (back_out[rows_of(g)].astype(F32) + scale * inner).astype(BF)
        return carry

    lax.fori_loop(0, SPAN, back_first, 0)

    def reorder(n, carry):
        grad_input[:, lane_tile(n)] = dot(to_panels, normed[:, lane_tile(n)]).astype(BF)
        return carry

    lax.fori_loop(0, D // N_TILE, reorder, 0)
    await_all(shared, recv_sems.at[1])

    def place(c, carry):
        piece(grad_down, c)[...] = shared[c].astype(F32)
        return carry

    lax.fori_loop(0, N_DP, place, 0)
    await_all(parts, send_sems.at[0])
    await_all(shared, send_sems.at[1])


def module(features, keep, cotangent, norm_gain, depth_kernel, conv_gain, ups, downs):
    rows = (ROWS, D)
    return pl.pallas_call(
        module_kernel,
        out_shape=[
            jax.ShapeDtypeStruct(rows, BF),
            jax.ShapeDtypeStruct(rows, BF),
            jax.ShapeDtypeStruct((HALF_D, D), F32),
        ],
        in_specs=[VMEM_SPEC] * 6 + [ANY_SPEC] * 4,
        out_specs=[VMEM_SPEC] * 3,
        scratch_shapes=[
            pltpu.VMEM((D, 2 * D), BF),
            pltpu.VMEM((D, D), BF),
            pltpu.VMEM(rows, BF),
            pltpu.VMEM((3, ROWS, 128), F32),
            pltpu.VMEM(rows, F32),
            pltpu.VMEM(rows, F32),
            pltpu.VMEM((ROWS + 2 * BORDER, D), BF),
            pltpu.VMEM(rows, F32),
            pltpu.VMEM(rows, F32),
            pltpu.VMEM(rows, BF),
            pltpu.VMEM(rows, BF),
            pltpu.VMEM((HALF_D, D), F32),
            pltpu.VMEM((HALF_D, D), BF),
            pltpu.VMEM((HALF_D, D), BF),
            pltpu.VMEM((HALF_D, D), BF),
            pltpu.VMEM((N_DP, SPAN, HALF_D), BF),
            pltpu.VMEM((SPAN, HALF_D), BF),
            pltpu.VMEM((N_DP, SPAN, HALF_D), BF),
            pltpu.VMEM(rows, F32),
            pltpu.VMEM((ROWS + 2 * BORDER, D), F32),
            pltpu.VMEM((ROWS, 2 * D), BF),
            pltpu.SemaphoreType.DMA((4,)),
            pltpu.SemaphoreType.DMA,
            pltpu.SemaphoreType.DMA,
            pltpu.SemaphoreType.DMA((2,)),
            pltpu.SemaphoreType.DMA((2,)),
        ],
        compiler_params=pltpu.CompilerParams(
            collective_id=1, has_side_effects=True, vmem_limit_bytes=67043328
        ),
        name="module",
    )(features, keep, cotangent, norm_gain, depth_kernel, conv_gain, *ups, *downs)


def local(
    mel_panels,
    frames,
    target,
    conv_first,
    depth_a,
    point_a,
    depth_b,
    point_b,
    linear_weight,
    norm_gain,
    up_weight,
    depth_kernel,
    conv_gain,
    down_weight,
    cotangent,
):
    small = (
        conv_first,
        depth_a,
        point_a,
        depth_b,
        point_b,
        norm_gain[None],
        depth_kernel,
        conv_gain[None],
    )
    big = (linear_weight, up_weight, down_weight)
    windows, keep, band, full, other = exchange(frames[None], target[None], mel_panels, small, big)
    features = subsample(windows, band, *full[1:5], linear_weight, other[0])
    return module(
        features,
        keep,
        cotangent,
        full[5],
        full[6],
        full[7],
        (up_weight, other[1]),
        (down_weight, other[2]),
    )


def solution(mesh):
    placed = (
        P(("dp", "fsdp"), None),
        P(("dp", "fsdp")),
        P(("dp", "fsdp")),
        P(None, "fsdp"),
        P(None, "fsdp"),
        P(None, "fsdp"),
        P(None, "fsdp"),
        P(None, "fsdp"),
        P(None, "fsdp"),
        P("fsdp"),
        P(None, "fsdp"),
        P(None, "fsdp"),
        P("fsdp"),
        P("fsdp", None),
        P(("dp", "fsdp"), None),
    )
    return jax.shard_map(
        local,
        mesh=mesh,
        in_specs=placed,
        out_specs=(P(("dp", "fsdp"), None), P(("dp", "fsdp"), None), P("fsdp", None)),
        check_vma=False,
    )
```

```python
import functools
import math

import jax
import jax.numpy as jnp
from jax import lax
from jax.experimental import pallas as pl
from jax.experimental.pallas import tpu as pltpu
from jax.sharding import PartitionSpec as P

MELS = 80
PANEL = 128
EPSILON = 1e-05
SPAN = 16
GROUP = 8 * MELS
N_DP = 64
U_DEV = 32
ROWS = U_DEV * SPAN
D = 1024
CH = 256
HALF = CH // 2
MARK = 64.0
MESH = pl.DeviceIdType.MESH
VMEM_SPEC = pl.BlockSpec(memory_space=pltpu.VMEM)
ANY_SPEC = pl.BlockSpec(memory_space=pl.ANY)
BF = jnp.bfloat16
F32 = jnp.float32


def iota(shape, dim):
    return lax.broadcasted_iota(jnp.int32, shape, dim)


def dot(a, b):
    return jnp.dot(a, b, preferred_element_type=F32)


def shifted_peer(me, step):
    x = (me + step) % 4
    y = (me // 4 + step // 4) % 4
    z = (me // 16 + step // 16) % 4
    return z * 16 + y * 4 + x


N_SMALL = 7
N_BIG = 3


def exchange_kernel(*refs):
    frames, target, mel = refs[:3]
    small = refs[3 : 3 + N_SMALL]
    big = refs[10:13]
    windows, keep_out, band_out = refs[13:16]
    small_full = refs[16 : 16 + N_SMALL]
    big_other = refs[23:26]
    flat, outgoing, incoming, band_in = refs[26:30]
    small_other = refs[30 : 30 + N_SMALL]
    small_send, small_recv, big_send, big_recv, send_sem, recv_sem, band_sem = refs[37:]

    me = lax.axis_index("dp")
    core = lax.axis_index("fsdp")
    other = 1 - core
    barrier = pltpu.get_barrier_semaphore()
    pl.semaphore_signal(barrier, inc=1, device_id=(me, other), device_id_type=MESH)

    def greet(step, carry):
        pl.semaphore_signal(
            barrier, inc=1, device_id=(shifted_peer(me, step), core), device_id_type=MESH
        )
        return carry

    lax.fori_loop(1, N_DP, greet, 0)

    picks = (target[...] == iota((N_DP, 64), 0)) & (frames[...] > 0)
    length = jnp.sum(jnp.where(picks, frames[...], 0), axis=1, keepdims=True)
    chosen = jnp.where(picks, 1.0, 0.0).astype(BF)
    for g in range(SPAN):
        rows = dot(chosen, mel[:, g * GROUP : (g + 1) * GROUP])
        rows = jnp.where(length > 8 * g, rows, MARK)
        for k in range(GROUP // 128):
            flat[k, pl.ds(g, N_DP, stride=SPAN), :] = rows[:, k * 128 : (k + 1) * 128]
    for k in range(GROUP // 128):
        outgoing[:, :, k * 128 : (k + 1) * 128] = flat[k].reshape(N_DP, SPAN, 128).astype(BF)

    pl.semaphore_wait(barrier, N_DP)

    partner = []
    for k in range(N_SMALL):
        copy = pltpu.make_async_remote_copy(
            src_ref=small[k],
            dst_ref=small_other[k],
            send_sem=small_send.at[k],
            recv_sem=small_recv.at[k],
            device_id=(me, other),
            device_id_type=MESH,
        )
        copy.start()
        partner.append(copy)

    def send(step, carry):
        pltpu.make_async_remote_copy(
            src_ref=outgoing.at[shifted_peer(me, step)],
            dst_ref=incoming.at[me],
            send_sem=send_sem,
            recv_sem=recv_sem,
            device_id=(shifted_peer(me, step), core),
            device_id_type=MESH,
        ).start()
        return carry

    lax.fori_loop(1, N_DP, send, 0)
    for k in range(N_BIG):
        copy = pltpu.make_async_remote_copy(
            src_ref=big[k],
            dst_ref=big_other[k],
            send_sem=big_send.at[k],
            recv_sem=big_recv.at[k],
            device_id=(me, other),
            device_id_type=MESH,
        )
        copy.start()
        partner.append(copy)
    incoming[pl.ds(me, 1)] = outgoing[pl.ds(me, 1)]

    for k in range(N_SMALL):
        partner[k].wait()
        width = small[k].shape[1]
        small_full[k][:, pl.ds(pl.multiple_of(core * width, 128), width)] = small[k][...]
        small_full[k][:, pl.ds(pl.multiple_of(other * width, 128), width)] = small_other[k][...]

    taps = small_full[0][...]
    row = iota((256, 9), 0)
    tap = iota((256, 9), 1)
    base = row - 80 * (tap // 3) - tap % 3 + 1

    def band(f, carry):
        b = base + (tap % 3) - 1
        hit = (base == 2 * f) & (b >= 0) & (b < MELS)
        column = dot(jnp.where(hit, 1.0, 0.0).astype(BF), taps)
        band_in[:, pl.ds(pl.multiple_of(f * CH, CH), CH)] = column.astype(BF)
        return carry

    lax.fori_loop(0, MELS // 2, band, 0)
    band_copy = pltpu.make_async_copy(band_in, band_out, band_sem)
    band_copy.start()

    sent = outgoing.at[pl.ds(0, N_DP - 1)]
    got = incoming.at[pl.ds(0, N_DP - 1)]
    pltpu.make_async_copy(got, got, recv_sem).wait()

    total = N_DP * SPAN
    panels = incoming[...].reshape(total, GROUP)
    first_lane = jnp.where(iota((8, GROUP), 1) == 0, 1.0, 0.0).astype(BF)
    heads = lax.dot_general(
        first_lane, panels, (((1,), (1,)), ((), ())), preferred_element_type=F32
    )
    live_row = jnp.where(heads < MARK / 2, 1.0, 0.0).astype(BF)
    pick_heads = jnp.where(iota((total, 64), 0) == SPAN * iota((total, 64), 1), 1.0, 0.0)
    present = dot(live_row, pick_heads.astype(BF)).astype(BF)
    before = jnp.where(iota((64, 64), 0) < iota((64, 64), 1), 1.0, 0.0).astype(BF)
    place = dot(present, before).astype(BF)
    spread = jnp.where(iota((64, total), 1) // SPAN == iota((64, total), 0), 1.0, 0.0).astype(BF)
    present_row = dot(present, spread)[:1]
    place_row = dot(place, spread)[:1].astype(jnp.int32)
    goal = jnp.where(
        present_row > 0.5, (iota((1, total), 1) % SPAN) * U_DEV + place_row, -1
    )
    move = jnp.where(iota((ROWS, total), 0) == goal, 1.0, 0.0).astype(BF)
    x = dot(move, panels)
    keep = x[:, :1] < MARK / 2
    x = jnp.where(keep, x, 0.0)
    keep_out[...] = jnp.broadcast_to(jnp.where(keep, 1.0, 0.0), (ROWS, 128))

    late = jnp.concatenate([jnp.zeros((U_DEV, 128), F32), x[: ROWS - U_DEV, 512:]], axis=0)
    late = pltpu.roll(late, 80, 1)
    now = pltpu.roll(x[:, :256], 80, 1)
    lanes = iota((ROWS, 128), 1)
    w0 = jnp.concatenate([jnp.where(lanes < 80, late, now[:, :128]), now[:, 128:]], axis=1)
    windows[0:ROWS] = w0.astype(BF)
    windows[ROWS : 2 * ROWS] = pltpu.roll(x[:, :384], 384 - 80, 1)[:, :256].astype(BF)
    windows[2 * ROWS : 3 * ROWS] = pltpu.roll(x[:, 128:512], 384 - 112, 1)[:, :256].astype(BF)
    windows[3 * ROWS : 4 * ROWS] = pltpu.roll(x[:, 384:], 256 - 16, 1).astype(BF)

    pltpu.make_async_copy(sent, sent, send_sem).wait()
    for k in range(N_SMALL, N_SMALL + N_BIG):
        partner[k].wait()
    band_copy.wait()


def exchange(frames, target, mel, small, big):
    small_full = [jax.ShapeDtypeStruct((a.shape[0], 2 * a.shape[1]), BF) for a in small]
    shapes = [
        jax.ShapeDtypeStruct((4 * ROWS, 256), BF),
        jax.ShapeDtypeStruct((ROWS, 128), F32),
        jax.ShapeDtypeStruct((256, MELS // 2 * CH), BF),
        *small_full,
        *[jax.ShapeDtypeStruct(a.shape, BF) for a in big],
    ]
    out = pl.pallas_call(
        exchange_kernel,
        out_shape=shapes,
        in_specs=[VMEM_SPEC] * (3 + N_SMALL) + [ANY_SPEC] * N_BIG,
        out_specs=[VMEM_SPEC] * 2 + [ANY_SPEC] + [VMEM_SPEC] * N_SMALL + [ANY_SPEC] * N_BIG,
        scratch_shapes=[
            pltpu.VMEM((GROUP // 128, N_DP * SPAN, 128), F32),
            pltpu.VMEM((N_DP, SPAN, GROUP), BF),
            pltpu.VMEM((N_DP, SPAN, GROUP), BF),
            pltpu.VMEM((256, MELS // 2 * CH), BF),
            *[pltpu.VMEM(a.shape, BF) for a in small],
            pltpu.SemaphoreType.DMA((N_SMALL,)),
            pltpu.SemaphoreType.DMA((N_SMALL,)),
            pltpu.SemaphoreType.DMA((N_BIG,)),
            pltpu.SemaphoreType.DMA((N_BIG,)),
            pltpu.SemaphoreType.DMA,
            pltpu.SemaphoreType.DMA,
            pltpu.SemaphoreType.DMA,
        ],
        compiler_params=pltpu.CompilerParams(
            collective_id=0, has_side_effects=True, vmem_limit_bytes=67043328
        ),
        name="exchange",
    )(frames, target, mel, *small, *big)
    return out[0], out[1], out[2], out[3 : 3 + N_SMALL], out[3 + N_SMALL :]


CHUNK = 64
PAD = U_DEV


def depth_rows(load, taps, r):
    total = None
    for i in range(3):
        for j in range(3):
            term = load(i, j, r) * taps[3 * i + j]
            total = term if total is None else total + term
    return total


def subsample_kernel(
    windows, band_in, depth_a, point_a, depth_b, point_b, linear_own, linear_other, out,
    band, first, spread_a, second, spread_b, fourth, linear, sems
):
    core = lax.axis_index("fsdp")
    width = D // 2

    def half(which):
        return linear.at[:, pl.ds(pl.multiple_of(which * width, width), width)]

    early, late = pl.ds(0, 4 * CH), pl.ds(4 * CH, MELS // 2 * CH - 4 * CH)
    loads = [
        pltpu.make_async_copy(band_in.at[:, early], band.at[:, early], sems.at[0]),
        pltpu.make_async_copy(band_in.at[:, late], band.at[:, late], sems.at[1]),
        pltpu.make_async_copy(linear_own, half(core), sems.at[2]),
        pltpu.make_async_copy(linear_other, half(1 - core), sems.at[3]),
    ]
    for copy in loads:
        copy.start()
    inner = slice(PAD, PAD + ROWS)
    first[0, :, 0] = jnp.zeros((4, PAD + ROWS, CH), BF)
    second[:, 0] = jnp.zeros((2, PAD + ROWS, CH), BF)
    for col in range(1, 5):
        for b in range(2):
            first[b, 3, col, 0:PAD] = jnp.zeros((PAD, CH), BF)
    for col in range(1, 3):
        second[1, col, 0:PAD] = jnp.zeros((PAD, CH), BF)
    taps_a = [jnp.broadcast_to(depth_a[k : k + 1], (CHUNK, CH)) for k in range(9)]
    taps_b = [jnp.broadcast_to(depth_b[k : k + 1], (CHUNK, CH)) for k in range(9)]

    def relu(x):
        return jnp.maximum(x.astype(BF), 0)

    def columns(n, b, t, f):
        w = band[:, pl.ds(pl.multiple_of(n * 4 * CH + f * CH, CH), CH)]
        first[b, t, 1 + f, inner] = relu(dot(windows[t * ROWS : (t + 1) * ROWS], w))

    jobs = [(t, f) for f in range(4) for t in range(4)]

    def step(n, b):
        ahead = jnp.minimum(n + 1, 9)
        for t in range(3):
            first[1 - b, t, 0, inner] = first[b, t, 4, inner]
        first[1 - b, 3, 0] = first[b, 3, 4]
        at = 0
        for q in range(4):
            t2, f2 = q // 2, q % 2
            for t, f in jobs[at : at + 3]:
                columns(ahead, 1 - b, t, f)
            at += 3

            def load(i, j, r):
                t = 2 * t2 + i - 1
                if t < 0:
                    return first[b, 3, 2 * f2 + j, r : r + CHUNK]
                return first[b, t, 2 * f2 + j, PAD + r : PAD + r + CHUNK]

            for r in range(0, ROWS, CHUNK):
                spread_a[q, r : r + CHUNK] = depth_rows(load, taps_a, r)
            second[t2, 1 + f2, inner] = relu(dot(spread_a[q], point_a[...]))
        for t, f in jobs[at:]:
            columns(ahead, 1 - b, t, f)

        def load_b(i, j, r):
            if i == 0:
                return second[1, j, r : r + CHUNK]
            return second[i - 1, j, PAD + r : PAD + r + CHUNK]

        for r in range(0, ROWS, CHUNK):
            spread_b[r : r + CHUNK] = depth_rows(load_b, taps_b, r)
        mapped = relu(dot(spread_b[...], point_b[...]))
        fourth[:, pl.ds(pl.multiple_of(n * CH, CH), CH)] = mapped
        for t2 in range(2):
            second[t2, 0] = second[t2, 2]

    loads[0].wait()
    for t, f in jobs:
        columns(0, 0, t, f)
    loads[1].wait()

    def two_steps(m, carry):
        step(2 * m, 0)
        step(2 * m + 1, 1)
        return carry

    lax.fori_loop(0, 5, two_steps, 0)
    loads[2].wait()
    loads[3].wait()
    out[...] = dot(fourth[...], linear[...]).astype(BF)


def subsample(windows, band, depth_a, point_a, depth_b, point_b, linear_own, linear_other):
    return pl.pallas_call(
        subsample_kernel,
        out_shape=jax.ShapeDtypeStruct((ROWS, D), BF),
        in_specs=[VMEM_SPEC, ANY_SPEC] + [VMEM_SPEC] * 4 + [ANY_SPEC] * 2,
        out_specs=VMEM_SPEC,
        scratch_shapes=[
            pltpu.VMEM((256, MELS // 2 * CH), BF),
            pltpu.VMEM((2, 4, 5, PAD + ROWS, CH), BF),
            pltpu.VMEM((4, ROWS, CH), BF),
            pltpu.VMEM((2, 3, PAD + ROWS, CH), BF),
            pltpu.VMEM((ROWS, CH), BF),
            pltpu.VMEM((ROWS, 10 * CH), BF),
            pltpu.VMEM((10 * CH, D), BF),
            pltpu.SemaphoreType.DMA((4,)),
        ],
        compiler_params=pltpu.CompilerParams(vmem_limit_bytes=67043328),
        name="subsample",
    )(windows, band, depth_a, point_a, depth_b, point_b, linear_own, linear_other)


def dot_t(a, b):
    return lax.dot_general(a, b, (((1,), (1,)), ((), ())), preferred_element_type=F32)


def dot_rows(a, b):
    return lax.dot_general(a, b, (((0,), (0,)), ((), ())), preferred_element_type=F32)


def row_mean(x):
    return jnp.sum(x, axis=1, keepdims=True) * (1.0 / D)


KER = 9
BORDER = KER // 2 * U_DEV
HALF_D = D // 2
N_TILE = 256


def lane_tile(n, start=0):
    return pl.ds(pl.multiple_of(start + n * N_TILE, N_TILE), N_TILE)


LANES = ((0, 384), (384, 384), (768, 256))
LINE = 128
OWN = 8


def line_of(me, c):
    x, y, z = me % 4, me // 4 % 4, me // 16
    return ((x, z * 4 + y), (y, z * 4 + x), (z, y * 4 + x))[c]


def device_at(c, a, p):
    if c == 0:
        return p // 4 * 16 + p % 4 * 4 + a
    if c == 1:
        return p // 4 * 16 + a * 4 + p % 4
    return a * 16 + p


def plane_shift(p, step):
    return (p // 4 + step // 4) % 4 * 4 + (p + step) % 4


def module_kernel(
    features, keep, cotangent, gains, depth_kernel,
    up_own, up_other, down_own, down_other,
    layer_out, grad_input, grad_down,
    up, down, normed, stats, gate_a, gate_b, gated, standard_two, slope, hidden, back_out,
    grad_own, to_partner, from_partner, part, shared, big, back_depth, back_proj,
    line_a, line_b, line_c, mid_a, mid_b, mid_c, wide_a, wide_b, wide_c,
    plane_a, plane_b, plane_c, mine_a, mine_b, mine_c,
    load_sems, partner_send, partner_recv, send_sems, recv_sems, own_sems,
):
    me = lax.axis_index("dp")
    core = lax.axis_index("fsdp")
    other = 1 - core
    barrier = pltpu.get_barrier_semaphore()
    pl.semaphore_signal(barrier, inc=1, device_id=(me, other), device_id_type=MESH)

    def greet(step, carry):
        pl.semaphore_signal(
            barrier, inc=1, device_id=(shifted_peer(me, step), core), device_id_type=MESH
        )
        return carry

    lax.fori_loop(1, N_DP, greet, 0)

    def part_of(which, width):
        return pl.ds(pl.multiple_of(which * width, width), width)

    loads = [
        pltpu.make_async_copy(up_own, up.at[:, part_of(core, D)], load_sems.at[0]),
        pltpu.make_async_copy(up_other, up.at[:, part_of(other, D)], load_sems.at[1]),
        pltpu.make_async_copy(down_own, down.at[part_of(core, HALF_D)], load_sems.at[2]),
        pltpu.make_async_copy(down_other, down.at[part_of(other, HALF_D)], load_sems.at[3]),
    ]
    for copy in loads:
        copy.start()

    def rows_of(g, shift=0):
        return pl.ds(pl.multiple_of((g + shift) * U_DEV, U_DEV), U_DEV)

    gain_one = gains[0:1].astype(F32)
    gain_two = gains[1:2].astype(F32)

    def norm_rows(g, carry):
        values = features[rows_of(g)].astype(F32)
        mean = row_mean(values)
        centred = values - mean
        scale = lax.rsqrt(row_mean(centred * centred) + EPSILON)
        normed[rows_of(g)] = (centred * scale * gain_one).astype(BF)
        stats[0, rows_of(g)] = jnp.broadcast_to(mean, (U_DEV, 128))
        stats[1, rows_of(g)] = jnp.broadcast_to(scale, (U_DEV, 128))
        return carry

    lax.fori_loop(0, SPAN, norm_rows, 0)
    gated[0:BORDER] = jnp.zeros((BORDER, D), BF)
    gated[BORDER + ROWS :] = jnp.zeros((BORDER, D), BF)
    back_depth[0:BORDER] = jnp.zeros((BORDER, D), F32)
    back_depth[BORDER + ROWS :] = jnp.zeros((BORDER, D), F32)

    out_row = iota((ROWS, ROWS), 0)
    in_row = iota((ROWS, ROWS), 1)
    to_groups = jnp.where(in_row == (out_row % U_DEV) * SPAN + out_row // U_DEV, 1.0, 0.0)
    to_groups = to_groups.astype(BF)
    to_panels = jnp.where(in_row == (out_row % SPAN) * U_DEV + out_row // SPAN, 1.0, 0.0)
    to_panels = to_panels.astype(BF)

    loads[0].wait()
    loads[1].wait()

    def project(n, carry):
        value = dot(normed[...], up[:, lane_tile(n)])
        gate = jax.nn.sigmoid(dot(normed[...], up[:, lane_tile(n, D)]))
        both = value * gate
        gate_a[:, lane_tile(n)] = gate
        gate_b[:, lane_tile(n)] = both * (1.0 - gate)
        gated[BORDER : BORDER + ROWS, lane_tile(n)] = (keep[:, :1] * both).astype(BF)
        moved = dot(to_groups, cotangent[:, lane_tile(n)])
        back_out[:, lane_tile(n)] = jnp.where(keep[:, :1] > 0, moved, 0.0).astype(BF)
        return carry

    lax.fori_loop(0, D // N_TILE, project, 0)

    def conv_rows(g, carry):
        summed = None
        for k in range(KER):
            tap = depth_kernel[k : k + 1].astype(F32)
            term = gated[rows_of(g, k)].astype(F32) * tap
            summed = term if summed is None else summed + term
        centred = summed - row_mean(summed)
        scale = lax.rsqrt(row_mean(centred * centred) + EPSILON)
        standard = centred * scale
        active = standard * gain_two
        swish = jax.nn.sigmoid(active)
        act = active * swish
        hidden[rows_of(g)] = act.astype(BF)
        standard_two[rows_of(g)] = standard
        slope[rows_of(g)] = (swish + act * (1.0 - swish)) * gain_two
        stats[2, rows_of(g)] = jnp.broadcast_to(scale, (U_DEV, 128))
        return carry

    lax.fori_loop(0, SPAN, conv_rows, 0)

    def grad_rows(which, n):
        mine_rows = hidden[:, part_of(which, HALF_D)]
        return dot_rows(mine_rows, back_out[:, lane_tile(n)])

    def partner_grad(n, carry):
        to_partner[:, lane_tile(n)] = grad_rows(other, n).astype(BF)
        return carry

    lax.fori_loop(0, D // N_TILE, partner_grad, 0)
    pl.semaphore_wait(barrier, N_DP)
    swap = pltpu.make_async_remote_copy(
        src_ref=to_partner,
        dst_ref=from_partner,
        send_sem=partner_send,
        recv_sem=partner_recv,
        device_id=(me, other),
        device_id_type=MESH,
    )
    swap.start()

    def own_grad(n, carry):
        grad_own[:, lane_tile(n)] = grad_rows(core, n)
        return carry

    lax.fori_loop(0, D // N_TILE, own_grad, 0)
    loads[2].wait()
    loads[3].wait()
    swap.wait()

    def add_partner(n, carry):
        rows = pl.ds(pl.multiple_of(n * 64, 64), 64)
        part[rows] = (grad_own[rows] + from_partner[rows].astype(F32)).astype(BF)
        return carry

    lax.fori_loop(0, HALF_D // 64, add_partner, 0)

    line_in = (line_a, line_b, line_c)
    mid = (mid_a, mid_b, mid_c)
    wide = (wide_a, wide_b, wide_c)
    plane_in = (plane_a, plane_b, plane_c)
    mine = (mine_a, mine_b, mine_c)

    def line_rows(a):
        return pl.ds(pl.multiple_of(a * LINE, LINE), LINE)

    def own_rows(a, p):
        return pl.ds(pl.multiple_of(a * LINE + p * OWN, OWN), OWN)

    def push(stage, c, src, dst, peer):
        pltpu.make_async_remote_copy(
            src_ref=src,
            dst_ref=dst,
            send_sem=send_sems.at[stage, c],
            recv_sem=recv_sems.at[stage, c],
            device_id=(peer, core),
            device_id_type=MESH,
        ).start()

    def await_block(block, sem):
        pltpu.make_async_copy(block, block, sem).wait()

    def reduce_lines():
        for c, (at, width) in enumerate(LANES):
            a, p = line_of(me, c)
            for step in range(1, 4):
                to = (a + step) % 4
                push(
                    0, c, part.at[line_rows(to), at : at + width], line_in[c].at[step - 1],
                    device_at(c, to, p),
                )

    def reduce_planes():
        for c, (at, width) in enumerate(LANES):
            a, p = line_of(me, c)
            await_block(line_in[c], recv_sems.at[0, c])
            total = part[line_rows(a), at : at + width].astype(F32)
            for k in range(3):
                total = total + line_in[c][k].astype(F32)
            wide[c][...] = total
            mid[c][...] = total.astype(BF)
        for c, (at, width) in enumerate(LANES):
            a, p = line_of(me, c)

            def send(step, carry, c=c, a=a, p=p):
                to = plane_shift(p, step)
                push(
                    1, c, mid[c].at[pl.ds(pl.multiple_of(to * OWN, OWN), OWN)],
                    plane_in[c].at[step - 1], device_at(c, a, to),
                )
                return carry

            lax.fori_loop(1, 16, send, 0)

    def gather_planes():
        for c, (at, width) in enumerate(LANES):
            a, p = line_of(me, c)
            await_block(plane_in[c], recv_sems.at[1, c])
            total = wide[c][pl.ds(pl.multiple_of(p * OWN, OWN), OWN)]
            for k in range(15):
                total = total + plane_in[c][k].astype(F32)
            mine[c][...] = (total * (1.0 / math.sqrt(ROWS * N_DP * 2))).astype(BF)
        for c, (at, width) in enumerate(LANES):
            a, p = line_of(me, c)
            spot = shared.at[own_rows(a, p), at : at + width]
            pltpu.make_async_copy(mine[c], spot, own_sems.at[c]).start()

            def send(step, carry, c=c, a=a, p=p, spot=spot):
                push(2, c, mine[c], spot, device_at(c, a, plane_shift(p, step)))
                return carry

            lax.fori_loop(1, 16, send, 0)

    def gather_lines():
        for c, (at, width) in enumerate(LANES):
            a, p = line_of(me, c)
            spot = shared.at[own_rows(a, p), at : at + width]
            pltpu.make_async_copy(mine[c], spot, own_sems.at[c]).wait()
            await_block(plane_in[c], recv_sems.at[2, c])
            block = shared.at[line_rows(a), at : at + width]
            for step in range(1, 4):
                push(3, c, block, block, device_at(c, (a + step) % 4, p))

    reduce_lines()

    def output(n, carry):
        mixed = dot(hidden[...], down[:, lane_tile(n)])
        total = features[:, lane_tile(n)].astype(F32) + mixed
        total = (keep[:, :1] * total).astype(BF)
        layer_out[:, lane_tile(n)] = dot(to_panels, total).astype(BF)
        return carry

    lax.fori_loop(0, D // N_TILE, output, 0)

    def back_hidden(n, carry):
        rows = down[pl.ds(pl.multiple_of(n * N_TILE, N_TILE), N_TILE)]
        big[:, lane_tile(n)] = dot_t(back_out[...], rows)
        return carry

    lax.fori_loop(0, D // N_TILE, back_hidden, 0)

    def back_norm(g, carry):
        error = big[rows_of(g)] * slope[rows_of(g)]
        standard = standard_two[rows_of(g)]
        inner = error - row_mean(error) - standard * row_mean(error * standard)
        back_depth[rows_of(g, KER // 2)] = stats[2, rows_of(g), :1] * inner
        return carry

    lax.fori_loop(0, SPAN, back_norm, 0)

    reduce_planes()

    def back_conv(g, carry):
        summed = None
        for k in range(KER):
            tap = depth_kernel[k : k + 1].astype(F32)
            term = back_depth[rows_of(g, KER - 1 - k)] * tap
            summed = term if summed is None else summed + term
        summed = keep[rows_of(g), :1] * summed
        back_proj[rows_of(g), 0:D] = (summed * gate_a[rows_of(g)]).astype(BF)
        back_proj[rows_of(g), D : 2 * D] = (summed * gate_b[rows_of(g)]).astype(BF)
        return carry

    lax.fori_loop(0, SPAN, back_conv, 0)

    gather_planes()

    def back_up(n, carry):
        rows = up[pl.ds(pl.multiple_of(n * N_TILE, N_TILE), N_TILE)]
        big[:, lane_tile(n)] = dot_t(back_proj[...], rows)
        return carry

    lax.fori_loop(0, D // N_TILE, back_up, 0)

    gather_lines()

    def back_first(g, carry):
        front = big[rows_of(g)] * gain_one
        scale = stats[1, rows_of(g), :1]
        standard = (features[rows_of(g)].astype(F32) - stats[0, rows_of(g), :1]) * scale
        inner = front - row_mean(front) - standard * row_mean(front * standard)
        normed[rows_of(g)] = (back_out[rows_of(g)].astype(F32) + scale * inner).astype(BF)
        return carry

    lax.fori_loop(0, SPAN, back_first, 0)

    def reorder(n, carry):
        grad_input[:, lane_tile(n)] = dot(to_panels, normed[:, lane_tile(n)]).astype(BF)
        return carry

    lax.fori_loop(0, D // N_TILE, reorder, 0)
    for c in range(3):
        await_block(line_in[c], recv_sems.at[3, c])

    def place(n, carry):
        rows = pl.ds(pl.multiple_of(n * 64, 64), 64)
        grad_down[rows] = shared[rows].astype(F32)
        return carry

    lax.fori_loop(0, HALF_D // 64, place, 0)
    for c in range(3):
        await_block(line_in[c], send_sems.at[0, c])
        await_block(plane_in[c], send_sems.at[1, c])
        await_block(plane_in[c], send_sems.at[2, c])
        await_block(line_in[c], send_sems.at[3, c])


def module(features, keep, cotangent, gains, depth_kernel, ups, downs):
    rows = (ROWS, D)
    return pl.pallas_call(
        module_kernel,
        out_shape=[
            jax.ShapeDtypeStruct(rows, BF),
            jax.ShapeDtypeStruct(rows, BF),
            jax.ShapeDtypeStruct((HALF_D, D), F32),
        ],
        in_specs=[VMEM_SPEC] * 5 + [ANY_SPEC] * 4,
        out_specs=[VMEM_SPEC] * 3,
        scratch_shapes=[
            pltpu.VMEM((D, 2 * D), BF),
            pltpu.VMEM((D, D), BF),
            pltpu.VMEM(rows, BF),
            pltpu.VMEM((3, ROWS, 128), F32),
            pltpu.VMEM(rows, F32),
            pltpu.VMEM(rows, F32),
            pltpu.VMEM((ROWS + 2 * BORDER, D), BF),
            pltpu.VMEM(rows, F32),
            pltpu.VMEM(rows, F32),
            pltpu.VMEM(rows, BF),
            pltpu.VMEM(rows, BF),
            pltpu.VMEM((HALF_D, D), F32),
            pltpu.VMEM((HALF_D, D), BF),
            pltpu.VMEM((HALF_D, D), BF),
            pltpu.VMEM((HALF_D, D), BF),
            pltpu.VMEM((HALF_D, D), BF),
            pltpu.VMEM(rows, F32),
            pltpu.VMEM((ROWS + 2 * BORDER, D), F32),
            pltpu.VMEM((ROWS, 2 * D), BF),
            *[pltpu.VMEM((3, LINE, width), BF) for _, width in LANES],
            *[pltpu.VMEM((LINE, width), BF) for _, width in LANES],
            *[pltpu.VMEM((LINE, width), F32) for _, width in LANES],
            *[pltpu.VMEM((15, OWN, width), BF) for _, width in LANES],
            *[pltpu.VMEM((OWN, width), BF) for _, width in LANES],
            pltpu.SemaphoreType.DMA((4,)),
            pltpu.SemaphoreType.DMA,
            pltpu.SemaphoreType.DMA,
            pltpu.SemaphoreType.DMA((4, 3)),
            pltpu.SemaphoreType.DMA((4, 3)),
            pltpu.SemaphoreType.DMA((3,)),
        ],
        compiler_params=pltpu.CompilerParams(
            collective_id=1, has_side_effects=True, vmem_limit_bytes=67043328
        ),
        name="module",
    )(features, keep, cotangent, gains, depth_kernel, *ups, *downs)


def local(
    mel_panels,
    frames,
    target,
    conv_first,
    depth_a,
    point_a,
    depth_b,
    point_b,
    linear_weight,
    norm_gain,
    up_weight,
    depth_kernel,
    conv_gain,
    down_weight,
    cotangent,
):
    small = (
        conv_first,
        depth_a,
        point_a,
        depth_b,
        point_b,
        jnp.stack([norm_gain, conv_gain]),
        depth_kernel,
    )
    big = (linear_weight, up_weight, down_weight)
    windows, keep, band, full, other = exchange(frames[None], target[None], mel_panels, small, big)
    features = subsample(windows, band, *full[1:5], linear_weight, other[0])
    return module(
        features,
        keep,
        cotangent,
        full[5],
        full[6],
        (up_weight, other[1]),
        (down_weight, other[2]),
    )


def solution(mesh):
    placed = (
        P(("dp", "fsdp"), None),
        P(("dp", "fsdp")),
        P(("dp", "fsdp")),
        P(None, "fsdp"),
        P(None, "fsdp"),
        P(None, "fsdp"),
        P(None, "fsdp"),
        P(None, "fsdp"),
        P(None, "fsdp"),
        P("fsdp"),
        P(None, "fsdp"),
        P(None, "fsdp"),
        P("fsdp"),
        P("fsdp", None),
        P(("dp", "fsdp"), None),
    )
    return jax.shard_map(
        local,
        mesh=mesh,
        in_specs=placed,
        out_specs=(P(("dp", "fsdp"), None), P(("dp", "fsdp"), None), P("fsdp", None)),
        check_vma=False,
    )
```

```python
import functools
import math

import jax
import jax.numpy as jnp
from jax import lax
from jax.experimental import pallas as pl
from jax.experimental.pallas import tpu as pltpu
from jax.sharding import PartitionSpec as P

MELS = 80
PANEL = 128
EPSILON = 1e-05
SPAN = 16
GROUP = 8 * MELS
N_DP = 64
U_DEV = 32
ROWS = U_DEV * SPAN
D = 1024
CH = 256
HALF = CH // 2
MARK = 64.0
MESH = pl.DeviceIdType.MESH
VMEM_SPEC = pl.BlockSpec(memory_space=pltpu.VMEM)
ANY_SPEC = pl.BlockSpec(memory_space=pl.ANY)
BF = jnp.bfloat16
F32 = jnp.float32


def iota(shape, dim):
    return lax.broadcasted_iota(jnp.int32, shape, dim)


def dot(a, b):
    return jnp.dot(a, b, preferred_element_type=F32)


def shifts(me):
    return tuple([(me // by + k) % 4 for k in range(4)] for by in (1, 4, 16))


def peer_at(moved, step):
    x, y, z = moved
    return z[step // 16] * 16 + y[step // 4 % 4] * 4 + x[step % 4]


def greet_peers(barrier, me, core, moved, steps):
    pl.semaphore_signal(barrier, inc=1, device_id=(me, 1 - core), device_id_type=MESH)
    for step in steps:
        pl.semaphore_signal(
            barrier, inc=1, device_id=(peer_at(moved, step), core), device_id_type=MESH
        )


N_SMALL = 7
N_BIG = 3


def exchange_kernel(*refs):
    frames, target, mel_in = refs[:3]
    small = refs[3 : 3 + N_SMALL]
    big = refs[10:13]
    windows, keep_out, band_out = refs[13:16]
    small_full = refs[16 : 16 + N_SMALL]
    big_other = refs[23:26]
    flat, outgoing, incoming, band_in, mel = refs[26:31]
    small_other = refs[31 : 31 + N_SMALL]
    small_send, small_recv, big_send, big_recv, send_sem, recv_sem, band_sem, mel_sem = refs[38:]

    me = lax.axis_index("dp")
    core = lax.axis_index("fsdp")
    other = 1 - core
    barrier = pltpu.get_barrier_semaphore()
    mel_copy = pltpu.make_async_copy(mel_in, mel, mel_sem)
    mel_copy.start()
    moved = shifts(me)
    greet_peers(barrier, me, core, moved, range(1, N_DP))

    picks = (target[...] == iota((N_DP, 64), 0)) & (frames[...] > 0)
    length = jnp.sum(jnp.where(picks, frames[...], 0), axis=1, keepdims=True)
    chosen = jnp.where(picks, 1.0, 0.0).astype(BF)
    mel_copy.wait()
    for g in range(SPAN):
        rows = dot(chosen, mel[:, g * GROUP : (g + 1) * GROUP])
        rows = jnp.where(length > 8 * g, rows, MARK)
        for k in range(GROUP // 128):
            flat[k, pl.ds(g, N_DP, stride=SPAN), :] = rows[:, k * 128 : (k + 1) * 128]
    for k in range(GROUP // 128):
        outgoing[:, :, k * 128 : (k + 1) * 128] = flat[k].reshape(N_DP, SPAN, 128).astype(BF)

    pl.semaphore_wait(barrier, N_DP)

    partner = []
    for k in range(N_SMALL):
        copy = pltpu.make_async_remote_copy(
            src_ref=small[k],
            dst_ref=small_other[k],
            send_sem=small_send.at[k],
            recv_sem=small_recv.at[k],
            device_id=(me, other),
            device_id_type=MESH,
        )
        copy.start()
        partner.append(copy)

    for step in range(1, N_DP):
        peer = peer_at(moved, step)
        pltpu.make_async_remote_copy(
            src_ref=outgoing.at[peer],
            dst_ref=incoming.at[me],
            send_sem=send_sem,
            recv_sem=recv_sem,
            device_id=(peer, core),
            device_id_type=MESH,
        ).start()
    for k in range(N_BIG):
        copy = pltpu.make_async_remote_copy(
            src_ref=big[k],
            dst_ref=big_other[k],
            send_sem=big_send.at[k],
            recv_sem=big_recv.at[k],
            device_id=(me, other),
            device_id_type=MESH,
        )
        copy.start()
        partner.append(copy)
    incoming[pl.ds(me, 1)] = outgoing[pl.ds(me, 1)]

    for k in range(N_SMALL):
        partner[k].wait()
        width = small[k].shape[1]
        small_full[k][:, pl.ds(pl.multiple_of(core * width, 128), width)] = small[k][...]
        small_full[k][:, pl.ds(pl.multiple_of(other * width, 128), width)] = small_other[k][...]

    taps = small_full[0][...]
    row = iota((256, 9), 0)
    tap = iota((256, 9), 1)
    base = row - 80 * (tap // 3) - tap % 3 + 1

    def band(f, carry):
        b = base + (tap % 3) - 1
        hit = (base == 2 * f) & (b >= 0) & (b < MELS)
        column = dot(jnp.where(hit, 1.0, 0.0).astype(BF), taps)
        band_in[:, pl.ds(pl.multiple_of(f * CH, CH), CH)] = column.astype(BF)
        return carry

    lax.fori_loop(0, MELS // 2, band, 0)
    band_copy = pltpu.make_async_copy(band_in, band_out, band_sem)
    band_copy.start()

    sent = outgoing.at[pl.ds(0, N_DP - 1)]
    got = incoming.at[pl.ds(0, N_DP - 1)]
    pltpu.make_async_copy(got, got, recv_sem).wait()

    total = N_DP * SPAN
    panels = incoming[...].reshape(total, GROUP)
    first_lane = jnp.where(iota((8, GROUP), 1) == 0, 1.0, 0.0).astype(BF)
    heads = lax.dot_general(
        first_lane, panels, (((1,), (1,)), ((), ())), preferred_element_type=F32
    )
    live_row = jnp.where(heads < MARK / 2, 1.0, 0.0).astype(BF)
    pick_heads = jnp.where(iota((total, 64), 0) == SPAN * iota((total, 64), 1), 1.0, 0.0)
    present = dot(live_row, pick_heads.astype(BF)).astype(BF)
    before = jnp.where(iota((64, 64), 0) < iota((64, 64), 1), 1.0, 0.0).astype(BF)
    place = dot(present, before).astype(BF)
    spread = jnp.where(iota((64, total), 1) // SPAN == iota((64, total), 0), 1.0, 0.0).astype(BF)
    present_row = dot(present, spread)[:1]
    place_row = dot(place, spread)[:1].astype(jnp.int32)
    goal = jnp.where(
        present_row > 0.5, (iota((1, total), 1) % SPAN) * U_DEV + place_row, -1
    )
    move = jnp.where(iota((ROWS, total), 0) == goal, 1.0, 0.0).astype(BF)
    x = dot(move, panels)
    keep = x[:, :1] < MARK / 2
    x = jnp.where(keep, x, 0.0)
    keep_out[...] = jnp.broadcast_to(jnp.where(keep, 1.0, 0.0), (ROWS, 128))

    late = jnp.concatenate([jnp.zeros((U_DEV, 128), F32), x[: ROWS - U_DEV, 512:]], axis=0)
    late = pltpu.roll(late, 80, 1)
    now = pltpu.roll(x[:, :256], 80, 1)
    lanes = iota((ROWS, 128), 1)
    w0 = jnp.concatenate([jnp.where(lanes < 80, late, now[:, :128]), now[:, 128:]], axis=1)
    windows[0:ROWS] = w0.astype(BF)
    windows[ROWS : 2 * ROWS] = pltpu.roll(x[:, :384], 384 - 80, 1)[:, :256].astype(BF)
    windows[2 * ROWS : 3 * ROWS] = pltpu.roll(x[:, 128:512], 384 - 112, 1)[:, :256].astype(BF)
    windows[3 * ROWS : 4 * ROWS] = pltpu.roll(x[:, 384:], 256 - 16, 1).astype(BF)

    pltpu.make_async_copy(sent, sent, send_sem).wait()
    for k in range(N_SMALL, N_SMALL + N_BIG):
        partner[k].wait()
    band_copy.wait()


def exchange(frames, target, mel, small, big):
    small_full = [jax.ShapeDtypeStruct((a.shape[0], 2 * a.shape[1]), BF) for a in small]
    shapes = [
        jax.ShapeDtypeStruct((4 * ROWS, 256), BF),
        jax.ShapeDtypeStruct((ROWS, 128), F32),
        jax.ShapeDtypeStruct((256, MELS // 2 * CH), BF),
        *small_full,
        *[jax.ShapeDtypeStruct(a.shape, BF) for a in big],
    ]
    out = pl.pallas_call(
        exchange_kernel,
        out_shape=shapes,
        in_specs=[VMEM_SPEC] * 2 + [ANY_SPEC] + [VMEM_SPEC] * N_SMALL + [ANY_SPEC] * N_BIG,
        out_specs=[VMEM_SPEC] * 2 + [ANY_SPEC] + [VMEM_SPEC] * N_SMALL + [ANY_SPEC] * N_BIG,
        scratch_shapes=[
            pltpu.VMEM((GROUP // 128, N_DP * SPAN, 128), F32),
            pltpu.VMEM((N_DP, SPAN, GROUP), BF),
            pltpu.VMEM((N_DP, SPAN, GROUP), BF),
            pltpu.VMEM((256, MELS // 2 * CH), BF),
            pltpu.VMEM((64, SPAN * GROUP), BF),
            *[pltpu.VMEM(a.shape, BF) for a in small],
            pltpu.SemaphoreType.DMA((N_SMALL,)),
            pltpu.SemaphoreType.DMA((N_SMALL,)),
            pltpu.SemaphoreType.DMA((N_BIG,)),
            pltpu.SemaphoreType.DMA((N_BIG,)),
            pltpu.SemaphoreType.DMA,
            pltpu.SemaphoreType.DMA,
            pltpu.SemaphoreType.DMA,
            pltpu.SemaphoreType.DMA,
        ],
        compiler_params=pltpu.CompilerParams(
            collective_id=0, has_side_effects=True, vmem_limit_bytes=67043328
        ),
        name="exchange",
    )(frames, target, mel, *small, *big)
    return out[0], out[1], out[2], out[3 : 3 + N_SMALL], out[3 + N_SMALL :]


CHUNK = 64
PAD = U_DEV


def depth_rows(load, taps, r):
    total = None
    for i in range(3):
        for j in range(3):
            term = load(i, j, r) * taps[3 * i + j]
            total = term if total is None else total + term
    return total


def subsample_kernel(
    windows, band_in, depth_a, point_a, depth_b, point_b, linear_own, linear_other, out,
    band, first, spread_a, second, spread_b, fourth, linear, sems
):
    core = lax.axis_index("fsdp")
    width = D // 2

    def half(which):
        return linear.at[:, pl.ds(pl.multiple_of(which * width, width), width)]

    early, late = pl.ds(0, 4 * CH), pl.ds(4 * CH, MELS // 2 * CH - 4 * CH)
    loads = [
        pltpu.make_async_copy(band_in.at[:, early], band.at[:, early], sems.at[0]),
        pltpu.make_async_copy(band_in.at[:, late], band.at[:, late], sems.at[1]),
        pltpu.make_async_copy(linear_own, half(core), sems.at[2]),
        pltpu.make_async_copy(linear_other, half(1 - core), sems.at[3]),
    ]
    for copy in loads:
        copy.start()
    inner = slice(PAD, PAD + ROWS)
    first[0, :, 0] = jnp.zeros((4, PAD + ROWS, CH), BF)
    second[:, 0] = jnp.zeros((2, PAD + ROWS, CH), BF)
    for col in range(1, 5):
        for b in range(2):
            first[b, 3, col, 0:PAD] = jnp.zeros((PAD, CH), BF)
    for col in range(1, 3):
        second[1, col, 0:PAD] = jnp.zeros((PAD, CH), BF)
    taps_a = [jnp.broadcast_to(depth_a[k : k + 1], (CHUNK, CH)) for k in range(9)]
    taps_b = [jnp.broadcast_to(depth_b[k : k + 1], (CHUNK, CH)) for k in range(9)]

    def relu(x):
        return jnp.maximum(x.astype(BF), 0)

    def columns(n, b, t, f):
        w = band[:, pl.ds(pl.multiple_of(n * 4 * CH + f * CH, CH), CH)]
        first[b, t, 1 + f, inner] = relu(dot(windows[t * ROWS : (t + 1) * ROWS], w))

    jobs = [(t, f) for f in range(4) for t in range(4)]

    def step(n, b):
        ahead = jnp.minimum(n + 1, 9)
        for t in range(3):
            first[1 - b, t, 0, inner] = first[b, t, 4, inner]
        first[1 - b, 3, 0] = first[b, 3, 4]
        at = 0
        for q in range(4):
            t2, f2 = q // 2, q % 2
            for t, f in jobs[at : at + 3]:
                columns(ahead, 1 - b, t, f)
            at += 3

            def load(i, j, r):
                t = 2 * t2 + i - 1
                if t < 0:
                    return first[b, 3, 2 * f2 + j, r : r + CHUNK]
                return first[b, t, 2 * f2 + j, PAD + r : PAD + r + CHUNK]

            for r in range(0, ROWS, CHUNK):
                spread_a[q, r : r + CHUNK] = depth_rows(load, taps_a, r)
            second[t2, 1 + f2, inner] = relu(dot(spread_a[q], point_a[...]))
        for t, f in jobs[at:]:
            columns(ahead, 1 - b, t, f)

        def load_b(i, j, r):
            if i == 0:
                return second[1, j, r : r + CHUNK]
            return second[i - 1, j, PAD + r : PAD + r + CHUNK]

        for r in range(0, ROWS, CHUNK):
            spread_b[r : r + CHUNK] = depth_rows(load_b, taps_b, r)
        mapped = relu(dot(spread_b[...], point_b[...]))
        fourth[:, pl.ds(pl.multiple_of(n * CH, CH), CH)] = mapped
        for t2 in range(2):
            second[t2, 0] = second[t2, 2]

    loads[0].wait()
    for t, f in jobs:
        columns(0, 0, t, f)
    loads[1].wait()

    def two_steps(m, carry):
        step(2 * m, 0)
        step(2 * m + 1, 1)
        return carry

    lax.fori_loop(0, 5, two_steps, 0)
    loads[2].wait()
    loads[3].wait()
    out[...] = dot(fourth[...], linear[...]).astype(BF)


def subsample(windows, band, depth_a, point_a, depth_b, point_b, linear_own, linear_other):
    return pl.pallas_call(
        subsample_kernel,
        out_shape=jax.ShapeDtypeStruct((ROWS, D), BF),
        in_specs=[VMEM_SPEC, ANY_SPEC] + [VMEM_SPEC] * 4 + [ANY_SPEC] * 2,
        out_specs=VMEM_SPEC,
        scratch_shapes=[
            pltpu.VMEM((256, MELS // 2 * CH), BF),
            pltpu.VMEM((2, 4, 5, PAD + ROWS, CH), BF),
            pltpu.VMEM((4, ROWS, CH), BF),
            pltpu.VMEM((2, 3, PAD + ROWS, CH), BF),
            pltpu.VMEM((ROWS, CH), BF),
            pltpu.VMEM((ROWS, 10 * CH), BF),
            pltpu.VMEM((10 * CH, D), BF),
            pltpu.SemaphoreType.DMA((4,)),
        ],
        compiler_params=pltpu.CompilerParams(vmem_limit_bytes=67043328),
        name="subsample",
    )(windows, band, depth_a, point_a, depth_b, point_b, linear_own, linear_other)


def dot_t(a, b):
    return lax.dot_general(a, b, (((1,), (1,)), ((), ())), preferred_element_type=F32)


def dot_rows(a, b):
    return lax.dot_general(a, b, (((0,), (0,)), ((), ())), preferred_element_type=F32)


def row_mean(x):
    return jnp.sum(x, axis=1, keepdims=True) * (1.0 / D)


KER = 9
BORDER = KER // 2 * U_DEV
HALF_D = D // 2
N_TILE = 256


def lane_tile(n, start=0):
    if isinstance(n, int):
        return pl.ds(start + n * N_TILE, N_TILE)
    return pl.ds(pl.multiple_of(start + n * N_TILE, N_TILE), N_TILE)


LANES = ((0, 384), (384, 384), (768, 256))
LINE = 128
OWN = 8


def placed_at(moved, c, line, plane):
    steps = [(plane // 4, plane % 4)[k] for k in range(2)]
    steps.insert((2, 1, 0)[c], line)
    z, y, x = (moved[2 - k][steps[k]] for k in range(3))
    place = ((x, z * 4 + y), (y, z * 4 + x), (z, y * 4 + x))[c]
    return (z * 16 + y * 4 + x, *place)


def module_kernel(
    features, keep, cotangent, gains, depth_kernel,
    up_own, up_other, down_own, down_other,
    layer_out, grad_input, grad_down,
    up, down, normed, stats, gate_a, gate_b, gated, standard_two, slope, hidden, back_out,
    grad_own, to_partner, from_partner, part, shared, big, back_depth, back_proj,
    line_a, line_b, line_c, mid_a, mid_b, mid_c, wide_a, wide_b, wide_c,
    plane_a, plane_b, plane_c, mine_a, mine_b, mine_c, taps,
    load_sems, partner_send, partner_recv, send_sems, recv_sems, own_sems,
):
    me = lax.axis_index("dp")
    core = lax.axis_index("fsdp")
    other = 1 - core
    barrier = pltpu.get_barrier_semaphore()
    moved = shifts(me)
    near = [k for k in range(1, N_DP) if k < 16 or k % 16 < 4 or k % 4 == 0]
    greet_peers(barrier, me, core, moved, near)

    def part_of(which, width):
        return pl.ds(pl.multiple_of(which * width, width), width)

    loads = [
        pltpu.make_async_copy(up_own, up.at[:, part_of(core, D)], load_sems.at[0]),
        pltpu.make_async_copy(up_other, up.at[:, part_of(other, D)], load_sems.at[1]),
        pltpu.make_async_copy(down_own, down.at[part_of(core, HALF_D)], load_sems.at[2]),
        pltpu.make_async_copy(down_other, down.at[part_of(other, HALF_D)], load_sems.at[3]),
    ]
    for copy in loads:
        copy.start()

    def rows_of(g, shift=0):
        return pl.ds(pl.multiple_of((g + shift) * U_DEV, U_DEV), U_DEV)

    gain_one = gains[0:1].astype(F32)
    gain_two = gains[1:2].astype(F32)

    def norm_rows(g, carry):
        values = features[rows_of(g)].astype(F32)
        mean = row_mean(values)
        centred = values - mean
        scale = lax.rsqrt(row_mean(centred * centred) + EPSILON)
        normed[rows_of(g)] = (centred * scale * gain_one).astype(BF)
        stats[0, rows_of(g)] = jnp.broadcast_to(mean, (U_DEV, 128))
        stats[1, rows_of(g)] = jnp.broadcast_to(scale, (U_DEV, 128))
        return carry

    lax.fori_loop(0, SPAN, norm_rows, 0)
    gated[0:BORDER] = jnp.zeros((BORDER, D), BF)
    gated[BORDER + ROWS :] = jnp.zeros((BORDER, D), BF)
    back_depth[0:BORDER] = jnp.zeros((BORDER, D), F32)
    back_depth[BORDER + ROWS :] = jnp.zeros((BORDER, D), F32)

    out_row = iota((ROWS, ROWS), 0)
    in_row = iota((ROWS, ROWS), 1)
    to_groups = jnp.where(in_row == (out_row % U_DEV) * SPAN + out_row // U_DEV, 1.0, 0.0)
    to_groups = to_groups.astype(BF)

    loads[0].wait()
    loads[1].wait()

    def project(n, carry):
        value = dot(normed[...], up[:, lane_tile(n)])
        gate = jax.nn.sigmoid(dot(normed[...], up[:, lane_tile(n, D)]))
        both = value * gate
        gate_a[:, lane_tile(n)] = gate
        gate_b[:, lane_tile(n)] = both * (1.0 - gate)
        gated[BORDER : BORDER + ROWS, lane_tile(n)] = (keep[:, :1] * both).astype(BF)
        moved = dot(to_groups, cotangent[:, lane_tile(n)])
        back_out[:, lane_tile(n)] = jnp.where(keep[:, :1] > 0, moved, 0.0).astype(BF)
        return carry

    for n in range(D // N_TILE):
        project(n, 0)

    for k in range(KER):
        taps[k] = jnp.broadcast_to(depth_kernel[k : k + 1], (U_DEV, D))

    def conv_rows(g, carry):
        summed = None
        for k in range(0, KER, 3):
            terms = [gated[rows_of(g, k + i)] * taps[k + i] for i in range(3)]
            term = (terms[0] + terms[1] + terms[2]).astype(F32)
            summed = term if summed is None else summed + term
        centred = summed - row_mean(summed)
        scale = lax.rsqrt(row_mean(centred * centred) + EPSILON)
        standard = centred * scale
        active = standard * gain_two
        swish = jax.nn.sigmoid(active)
        act = active * swish
        hidden[rows_of(g)] = act.astype(BF)
        standard_two[rows_of(g)] = standard
        slope[rows_of(g)] = (swish + act * (1.0 - swish)) * gain_two
        stats[2, rows_of(g)] = jnp.broadcast_to(scale, (U_DEV, 128))
        return carry

    lax.fori_loop(0, SPAN, conv_rows, 0)

    def grad_rows(which):
        return dot_rows(hidden[:, part_of(which, HALF_D)], back_out[...])

    to_partner[...] = grad_rows(other).astype(BF)
    pl.semaphore_wait(barrier, 1 + len(near))
    swap = pltpu.make_async_remote_copy(
        src_ref=to_partner,
        dst_ref=from_partner,
        send_sem=partner_send,
        recv_sem=partner_recv,
        device_id=(me, other),
        device_id_type=MESH,
    )
    swap.start()

    grad_own[...] = grad_rows(core)
    loads[2].wait()
    loads[3].wait()
    swap.wait()

    def add_partner(n, carry):
        rows = pl.ds(pl.multiple_of(n * 64, 64), 64)
        part[rows] = (grad_own[rows] + from_partner[rows].astype(F32)).astype(BF)
        return carry

    lax.fori_loop(0, HALF_D // 64, add_partner, 0)

    line_in = (line_a, line_b, line_c)
    mid = (mid_a, mid_b, mid_c)
    wide = (wide_a, wide_b, wide_c)
    plane_in = (plane_a, plane_b, plane_c)
    mine = (mine_a, mine_b, mine_c)

    def line_rows(a):
        return pl.ds(pl.multiple_of(a * LINE, LINE), LINE)

    def own_rows(a, p):
        return pl.ds(pl.multiple_of(a * LINE + p * OWN, OWN), OWN)

    def push(stage, c, src, dst, peer):
        pltpu.make_async_remote_copy(
            src_ref=src,
            dst_ref=dst,
            send_sem=send_sems.at[stage, c],
            recv_sem=recv_sems.at[stage, c],
            device_id=(peer, core),
            device_id_type=MESH,
        ).start()

    def await_block(block, sem):
        pltpu.make_async_copy(block, block, sem).wait()

    def reduce_lines():
        for c, (at, width) in enumerate(LANES):
            for step in range(1, 4):
                peer, a, _ = placed_at(moved, c, step, 0)
                push(
                    0, c, part.at[line_rows(a), at : at + width], line_in[c].at[step - 1], peer
                )

    def reduce_planes():
        for c, (at, width) in enumerate(LANES):
            _, a, _ = placed_at(moved, c, 0, 0)
            await_block(line_in[c], recv_sems.at[0, c])
            total = part[line_rows(a), at : at + width].astype(F32)
            for k in range(3):
                total = total + line_in[c][k].astype(F32)
            wide[c][...] = total
            mid[c][...] = total.astype(BF)
        for c in range(3):
            for step in range(1, 16):
                peer, _, p = placed_at(moved, c, 0, step)
                rows = pl.ds(pl.multiple_of(p * OWN, OWN), OWN)
                push(1, c, mid[c].at[rows], plane_in[c].at[step - 1], peer)

    def spot_of(c):
        at, width = LANES[c]
        _, a, p = placed_at(moved, c, 0, 0)
        return shared.at[own_rows(a, p), at : at + width]

    def gather_planes():
        for c in range(3):
            _, _, p = placed_at(moved, c, 0, 0)
            await_block(plane_in[c], recv_sems.at[1, c])
            total = wide[c][pl.ds(pl.multiple_of(p * OWN, OWN), OWN)]
            for k in range(15):
                total = total + plane_in[c][k].astype(F32)
            mine[c][...] = (total * (1.0 / math.sqrt(ROWS * N_DP * 2))).astype(BF)
        for c in range(3):
            pltpu.make_async_copy(mine[c], spot_of(c), own_sems.at[c]).start()
            for step in range(1, 16):
                push(2, c, mine[c], spot_of(c), placed_at(moved, c, 0, step)[0])

    def gather_lines():
        for c, (at, width) in enumerate(LANES):
            pltpu.make_async_copy(mine[c], spot_of(c), own_sems.at[c]).wait()
            await_block(plane_in[c], recv_sems.at[2, c])
            block = shared.at[line_rows(placed_at(moved, c, 0, 0)[1]), at : at + width]
            for step in range(1, 4):
                push(3, c, block, block, placed_at(moved, c, step, 0)[0])

    reduce_lines()
    to_panels = jnp.where(in_row == (out_row % SPAN) * U_DEV + out_row // SPAN, 1.0, 0.0)
    to_panels = to_panels.astype(BF)

    def output(n, carry):
        mixed = dot(hidden[...], down[:, lane_tile(n)])
        total = features[:, lane_tile(n)].astype(F32) + mixed
        total = (keep[:, :1] * total).astype(BF)
        layer_out[:, lane_tile(n)] = dot(to_panels, total).astype(BF)
        return carry

    lax.fori_loop(0, D // N_TILE, output, 0)

    def back_hidden(n, carry):
        rows = down[pl.ds(pl.multiple_of(n * N_TILE, N_TILE), N_TILE)]
        big[:, lane_tile(n)] = dot_t(back_out[...], rows)
        return carry

    lax.fori_loop(0, D // N_TILE, back_hidden, 0)

    def back_norm(g, carry):
        error = big[rows_of(g)] * slope[rows_of(g)]
        standard = standard_two[rows_of(g)]
        inner = error - row_mean(error) - standard * row_mean(error * standard)
        back_depth[rows_of(g, KER // 2)] = stats[2, rows_of(g), :1] * inner
        return carry

    lax.fori_loop(0, SPAN, back_norm, 0)

    reduce_planes()

    def back_conv(g, carry):
        summed = None
        for k in range(KER):
            tap = depth_kernel[k : k + 1].astype(F32)
            term = back_depth[rows_of(g, KER - 1 - k)] * tap
            summed = term if summed is None else summed + term
        summed = keep[rows_of(g), :1] * summed
        back_proj[rows_of(g), 0:D] = (summed * gate_a[rows_of(g)]).astype(BF)
        back_proj[rows_of(g), D : 2 * D] = (summed * gate_b[rows_of(g)]).astype(BF)
        return carry

    lax.fori_loop(0, SPAN, back_conv, 0)

    gather_planes()

    def back_up(n, carry):
        rows = up[pl.ds(pl.multiple_of(n * N_TILE, N_TILE), N_TILE)]
        big[:, lane_tile(n)] = dot_t(back_proj[...], rows)
        return carry

    lax.fori_loop(0, D // N_TILE, back_up, 0)

    gather_lines()

    def back_first(g, carry):
        front = big[rows_of(g)] * gain_one
        scale = stats[1, rows_of(g), :1]
        standard = (features[rows_of(g)].astype(F32) - stats[0, rows_of(g), :1]) * scale
        inner = front - row_mean(front) - standard * row_mean(front * standard)
        normed[rows_of(g)] = (back_out[rows_of(g)].astype(F32) + scale * inner).astype(BF)
        return carry

    lax.fori_loop(0, SPAN, back_first, 0)

    def reorder(n, carry):
        grad_input[:, lane_tile(n)] = dot(to_panels, normed[:, lane_tile(n)]).astype(BF)
        return carry

    lax.fori_loop(0, D // N_TILE, reorder, 0)
    for c in range(3):
        await_block(line_in[c], recv_sems.at[3, c])

    def place(n, carry):
        rows = pl.ds(pl.multiple_of(n * 64, 64), 64)
        grad_down[rows] = shared[rows].astype(F32)
        return carry

    lax.fori_loop(0, HALF_D // 64, place, 0)
    for c in range(3):
        await_block(line_in[c], send_sems.at[0, c])
        await_block(plane_in[c], send_sems.at[1, c])
        await_block(plane_in[c], send_sems.at[2, c])
        await_block(line_in[c], send_sems.at[3, c])


def module(features, keep, cotangent, gains, depth_kernel, ups, downs):
    rows = (ROWS, D)
    return pl.pallas_call(
        module_kernel,
        out_shape=[
            jax.ShapeDtypeStruct(rows, BF),
            jax.ShapeDtypeStruct(rows, BF),
            jax.ShapeDtypeStruct((HALF_D, D), F32),
        ],
        in_specs=[VMEM_SPEC] * 5 + [ANY_SPEC] * 4,
        out_specs=[VMEM_SPEC] * 3,
        scratch_shapes=[
            pltpu.VMEM((D, 2 * D), BF),
            pltpu.VMEM((D, D), BF),
            pltpu.VMEM(rows, BF),
            pltpu.VMEM((3, ROWS, 128), F32),
            pltpu.VMEM(rows, F32),
            pltpu.VMEM(rows, F32),
            pltpu.VMEM((ROWS + 2 * BORDER, D), BF),
            pltpu.VMEM(rows, F32),
            pltpu.VMEM(rows, F32),
            pltpu.VMEM(rows, BF),
            pltpu.VMEM(rows, BF),
            pltpu.VMEM((HALF_D, D), F32),
            pltpu.VMEM((HALF_D, D), BF),
            pltpu.VMEM((HALF_D, D), BF),
            pltpu.VMEM((HALF_D, D), BF),
            pltpu.VMEM((HALF_D, D), BF),
            pltpu.VMEM(rows, F32),
            pltpu.VMEM((ROWS + 2 * BORDER, D), F32),
            pltpu.VMEM((ROWS, 2 * D), BF),
            *[pltpu.VMEM((3, LINE, width), BF) for _, width in LANES],
            *[pltpu.VMEM((LINE, width), BF) for _, width in LANES],
            *[pltpu.VMEM((LINE, width), F32) for _, width in LANES],
            *[pltpu.VMEM((15, OWN, width), BF) for _, width in LANES],
            *[pltpu.VMEM((OWN, width), BF) for _, width in LANES],
            pltpu.VMEM((KER, U_DEV, D), BF),
            pltpu.SemaphoreType.DMA((4,)),
            pltpu.SemaphoreType.DMA,
            pltpu.SemaphoreType.DMA,
            pltpu.SemaphoreType.DMA((4, 3)),
            pltpu.SemaphoreType.DMA((4, 3)),
            pltpu.SemaphoreType.DMA((3,)),
        ],
        compiler_params=pltpu.CompilerParams(
            collective_id=1, has_side_effects=True, vmem_limit_bytes=67043328
        ),
        name="module",
    )(features, keep, cotangent, gains, depth_kernel, *ups, *downs)


def local(
    mel_panels,
    frames,
    target,
    conv_first,
    depth_a,
    point_a,
    depth_b,
    point_b,
    linear_weight,
    norm_gain,
    up_weight,
    depth_kernel,
    conv_gain,
    down_weight,
    cotangent,
):
    small = (
        conv_first,
        depth_a,
        point_a,
        depth_b,
        point_b,
        jnp.stack([norm_gain, conv_gain]),
        depth_kernel,
    )
    big = (linear_weight, up_weight, down_weight)
    windows, keep, band, full, other = exchange(frames[None], target[None], mel_panels, small, big)
    features = subsample(windows, band, *full[1:5], linear_weight, other[0])
    return module(
        features,
        keep,
        cotangent,
        full[5],
        full[6],
        (up_weight, other[1]),
        (down_weight, other[2]),
    )


def solution(mesh):
    placed = (
        P(("dp", "fsdp"), None),
        P(("dp", "fsdp")),
        P(("dp", "fsdp")),
        P(None, "fsdp"),
        P(None, "fsdp"),
        P(None, "fsdp"),
        P(None, "fsdp"),
        P(None, "fsdp"),
        P(None, "fsdp"),
        P("fsdp"),
        P(None, "fsdp"),
        P(None, "fsdp"),
        P("fsdp"),
        P("fsdp", None),
        P(("dp", "fsdp"), None),
    )
    return jax.shard_map(
        local,
        mesh=mesh,
        in_specs=placed,
        out_specs=(P(("dp", "fsdp"), None), P(("dp", "fsdp"), None), P("fsdp", None)),
        check_vma=False,
    )
```

```python
import functools
import math

import jax
import jax.numpy as jnp
from jax import lax
from jax.experimental import pallas as pl
from jax.experimental.pallas import tpu as pltpu
from jax.sharding import PartitionSpec as P

MELS = 80
PANEL = 128
EPSILON = 1e-05
SPAN = 16
GROUP = 8 * MELS
N_DP = 64
U_DEV = 32
ROWS = U_DEV * SPAN
D = 1024
CH = 256
HALF = CH // 2
MARK = 64.0
MESH = pl.DeviceIdType.MESH
VMEM_SPEC = pl.BlockSpec(memory_space=pltpu.VMEM)
ANY_SPEC = pl.BlockSpec(memory_space=pl.ANY)
BF = jnp.bfloat16
F32 = jnp.float32


def iota(shape, dim):
    return lax.broadcasted_iota(jnp.int32, shape, dim)


def dot(a, b):
    return jnp.dot(a, b, preferred_element_type=F32)


def shifts(me):
    return tuple([(me // by + k) % 4 for k in range(4)] for by in (1, 4, 16))


def peer_at(moved, step):
    x, y, z = moved
    return z[step // 16] * 16 + y[step // 4 % 4] * 4 + x[step % 4]


def greet_peers(barrier, me, core, moved, steps):
    pl.semaphore_signal(barrier, inc=1, device_id=(me, 1 - core), device_id_type=MESH)
    for step in steps:
        pl.semaphore_signal(
            barrier, inc=1, device_id=(peer_at(moved, step), core), device_id_type=MESH
        )


N_SMALL = 8
GAINS = (5, 6)
N_BIG = 3


def exchange_kernel(*refs):
    frames, target, mel_in = refs[:3]
    small = refs[3 : 3 + N_SMALL]
    big = refs[11:14]
    windows, keep_out, band_out = refs[14:17]
    small_full = refs[17 : 17 + N_SMALL]
    big_other = refs[25:28]
    flat, outgoing, incoming, band_in, mel = refs[28:33]
    small_other = refs[33 : 33 + N_SMALL]
    small_send, small_recv, big_send, big_recv, send_sem, recv_sem, band_sem, mel_sem = refs[41:]

    me = lax.axis_index("dp")
    core = lax.axis_index("fsdp")
    other = 1 - core
    barrier = pltpu.get_barrier_semaphore()
    mel_copy = pltpu.make_async_copy(mel_in, mel, mel_sem)
    mel_copy.start()
    moved = shifts(me)
    greet_peers(barrier, me, core, moved, range(1, N_DP))

    picks = (target[...] == iota((N_DP, 64), 0)) & (frames[...] > 0)
    length = jnp.sum(jnp.where(picks, frames[...], 0), axis=1, keepdims=True)
    chosen = jnp.where(picks, 1.0, 0.0).astype(BF)
    mel_copy.wait()
    for g in range(SPAN):
        rows = dot(chosen, mel[:, g * GROUP : (g + 1) * GROUP])
        rows = jnp.where(length > 8 * g, rows, MARK)
        for k in range(GROUP // 128):
            flat[k, pl.ds(g, N_DP, stride=SPAN), :] = rows[:, k * 128 : (k + 1) * 128]
    for k in range(GROUP // 128):
        outgoing[:, :, k * 128 : (k + 1) * 128] = flat[k].reshape(N_DP, SPAN, 128).astype(BF)

    pl.semaphore_wait(barrier, N_DP)

    partner = []
    for k in range(N_SMALL):
        copy = pltpu.make_async_remote_copy(
            src_ref=small[k],
            dst_ref=small_other[k],
            send_sem=small_send.at[k],
            recv_sem=small_recv.at[k],
            device_id=(me, other),
            device_id_type=MESH,
        )
        copy.start()
        partner.append(copy)

    for step in range(1, N_DP):
        peer = peer_at(moved, step)
        pltpu.make_async_remote_copy(
            src_ref=outgoing.at[peer],
            dst_ref=incoming.at[me],
            send_sem=send_sem,
            recv_sem=recv_sem,
            device_id=(peer, core),
            device_id_type=MESH,
        ).start()
    for k in range(N_BIG):
        copy = pltpu.make_async_remote_copy(
            src_ref=big[k],
            dst_ref=big_other[k],
            send_sem=big_send.at[k],
            recv_sem=big_recv.at[k],
            device_id=(me, other),
            device_id_type=MESH,
        )
        copy.start()
        partner.append(copy)
    incoming[pl.ds(me, 1)] = outgoing[pl.ds(me, 1)]

    for k in range(N_SMALL):
        partner[k].wait()
        for which, ref in ((core, small[k]), (other, small_other[k])):
            if k in GAINS:
                lines = ref[...].astype(F32)
                for i in range(D // 2 // 128):
                    at = pl.multiple_of(which * (D // 2) + i * 128, 128)
                    small_full[k][:, pl.ds(at, 128)] = lines[i : i + 1].astype(BF)
            else:
                width = ref.shape[1]
                small_full[k][:, pl.ds(pl.multiple_of(which * width, 128), width)] = ref[...]

    taps = small_full[0][...]
    row = iota((256, 9), 0)
    tap = iota((256, 9), 1)
    base = row - 80 * (tap // 3) - tap % 3 + 1

    def band(f, carry):
        b = base + (tap % 3) - 1
        hit = (base == 2 * f) & (b >= 0) & (b < MELS)
        column = dot(jnp.where(hit, 1.0, 0.0).astype(BF), taps)
        band_in[:, pl.ds(pl.multiple_of(f * CH, CH), CH)] = column.astype(BF)
        return carry

    lax.fori_loop(0, MELS // 2, band, 0)
    band_copy = pltpu.make_async_copy(band_in, band_out, band_sem)
    band_copy.start()

    sent = outgoing.at[pl.ds(0, N_DP - 1)]
    got = incoming.at[pl.ds(0, N_DP - 1)]
    pltpu.make_async_copy(got, got, recv_sem).wait()

    total = N_DP * SPAN
    panels = incoming[...].reshape(total, GROUP)
    first_lane = jnp.where(iota((8, GROUP), 1) == 0, 1.0, 0.0).astype(BF)
    heads = lax.dot_general(
        first_lane, panels, (((1,), (1,)), ((), ())), preferred_element_type=F32
    )
    live_row = jnp.where(heads < MARK / 2, 1.0, 0.0).astype(BF)
    pick_heads = jnp.where(iota((total, 64), 0) == SPAN * iota((total, 64), 1), 1.0, 0.0)
    present = dot(live_row, pick_heads.astype(BF)).astype(BF)
    before = jnp.where(iota((64, 64), 0) < iota((64, 64), 1), 1.0, 0.0).astype(BF)
    place = dot(present, before).astype(BF)
    spread = jnp.where(iota((64, total), 1) // SPAN == iota((64, total), 0), 1.0, 0.0).astype(BF)
    present_row = dot(present, spread)[:1]
    place_row = dot(place, spread)[:1].astype(jnp.int32)
    goal = jnp.where(
        present_row > 0.5, (iota((1, total), 1) % SPAN) * U_DEV + place_row, -1
    )
    move = jnp.where(iota((ROWS, total), 0) == goal, 1.0, 0.0).astype(BF)
    x = dot(move, panels)
    keep = x[:, :1] < MARK / 2
    x = jnp.where(keep, x, 0.0)
    keep_out[...] = jnp.broadcast_to(jnp.where(keep, 1.0, 0.0), (ROWS, 128))

    late = jnp.concatenate([jnp.zeros((U_DEV, 128), F32), x[: ROWS - U_DEV, 512:]], axis=0)
    late = pltpu.roll(late, 80, 1)
    now = pltpu.roll(x[:, :256], 80, 1)
    lanes = iota((ROWS, 128), 1)
    w0 = jnp.concatenate([jnp.where(lanes < 80, late, now[:, :128]), now[:, 128:]], axis=1)
    windows[0:ROWS] = w0.astype(BF)
    windows[ROWS : 2 * ROWS] = pltpu.roll(x[:, :384], 384 - 80, 1)[:, :256].astype(BF)
    windows[2 * ROWS : 3 * ROWS] = pltpu.roll(x[:, 128:512], 384 - 112, 1)[:, :256].astype(BF)
    windows[3 * ROWS : 4 * ROWS] = pltpu.roll(x[:, 384:], 256 - 16, 1).astype(BF)

    pltpu.make_async_copy(sent, sent, send_sem).wait()
    for k in range(N_SMALL, N_SMALL + N_BIG):
        partner[k].wait()
    band_copy.wait()


def exchange(frames, target, mel, small, big):
    small_full = [
        jax.ShapeDtypeStruct((1, D) if k in GAINS else (a.shape[0], 2 * a.shape[1]), BF)
        for k, a in enumerate(small)
    ]
    shapes = [
        jax.ShapeDtypeStruct((4 * ROWS, 256), BF),
        jax.ShapeDtypeStruct((ROWS, 128), F32),
        jax.ShapeDtypeStruct((256, MELS // 2 * CH), BF),
        *small_full,
        *[jax.ShapeDtypeStruct(a.shape, BF) for a in big],
    ]
    out = pl.pallas_call(
        exchange_kernel,
        out_shape=shapes,
        in_specs=[VMEM_SPEC] * 2 + [ANY_SPEC] + [VMEM_SPEC] * N_SMALL + [ANY_SPEC] * N_BIG,
        out_specs=[VMEM_SPEC] * 2 + [ANY_SPEC] + [VMEM_SPEC] * N_SMALL + [ANY_SPEC] * N_BIG,
        scratch_shapes=[
            pltpu.VMEM((GROUP // 128, N_DP * SPAN, 128), F32),
            pltpu.VMEM((N_DP, SPAN, GROUP), BF),
            pltpu.VMEM((N_DP, SPAN, GROUP), BF),
            pltpu.VMEM((256, MELS // 2 * CH), BF),
            pltpu.VMEM((64, SPAN * GROUP), BF),
            *[pltpu.VMEM(a.shape, BF) for a in small],
            pltpu.SemaphoreType.DMA((N_SMALL,)),
            pltpu.SemaphoreType.DMA((N_SMALL,)),
            pltpu.SemaphoreType.DMA((N_BIG,)),
            pltpu.SemaphoreType.DMA((N_BIG,)),
            pltpu.SemaphoreType.DMA,
            pltpu.SemaphoreType.DMA,
            pltpu.SemaphoreType.DMA,
            pltpu.SemaphoreType.DMA,
        ],
        compiler_params=pltpu.CompilerParams(
            collective_id=0, has_side_effects=True, vmem_limit_bytes=67043328
        ),
        name="exchange",
    )(frames, target, mel, *small, *big)
    return out[0], out[1], out[2], out[3 : 3 + N_SMALL], out[3 + N_SMALL :]


CHUNK = 64
PAD = U_DEV


def depth_rows(load, taps, r):
    total = None
    for i in range(3):
        for j in range(3):
            term = load(i, j, r) * taps[3 * i + j]
            total = term if total is None else total + term
    return total


def subsample_kernel(
    windows, band_in, depth_a, point_a, depth_b, point_b, linear_own, linear_other, out,
    band, first, spread_a, second, spread_b, fourth, linear, sems
):
    core = lax.axis_index("fsdp")
    width = D // 2

    def half(which):
        return linear.at[:, pl.ds(pl.multiple_of(which * width, width), width)]

    early, late = pl.ds(0, 4 * CH), pl.ds(4 * CH, MELS // 2 * CH - 4 * CH)
    loads = [
        pltpu.make_async_copy(band_in.at[:, early], band.at[:, early], sems.at[0]),
        pltpu.make_async_copy(band_in.at[:, late], band.at[:, late], sems.at[1]),
        pltpu.make_async_copy(linear_own, half(core), sems.at[2]),
        pltpu.make_async_copy(linear_other, half(1 - core), sems.at[3]),
    ]
    for copy in loads:
        copy.start()
    inner = slice(PAD, PAD + ROWS)
    first[0, :, 0] = jnp.zeros((4, PAD + ROWS, CH), BF)
    second[:, 0] = jnp.zeros((2, PAD + ROWS, CH), BF)
    for col in range(1, 5):
        for b in range(2):
            first[b, 3, col, 0:PAD] = jnp.zeros((PAD, CH), BF)
    for col in range(1, 3):
        second[1, col, 0:PAD] = jnp.zeros((PAD, CH), BF)
    taps_a = [jnp.broadcast_to(depth_a[k : k + 1], (CHUNK, CH)) for k in range(9)]
    taps_b = [jnp.broadcast_to(depth_b[k : k + 1], (CHUNK, CH)) for k in range(9)]

    def relu(x):
        return jnp.maximum(x.astype(BF), 0)

    def columns(n, b, t, f):
        w = band[:, pl.ds(pl.multiple_of(n * 4 * CH + f * CH, CH), CH)]
        first[b, t, 1 + f, inner] = relu(dot(windows[t * ROWS : (t + 1) * ROWS], w))

    jobs = [(t, f) for f in range(4) for t in range(4)]

    def step(n, b):
        ahead = jnp.minimum(n + 1, 9)
        for t in range(3):
            first[1 - b, t, 0, inner] = first[b, t, 4, inner]
        first[1 - b, 3, 0] = first[b, 3, 4]
        at = 0
        for q in range(4):
            t2, f2 = q // 2, q % 2
            for t, f in jobs[at : at + 3]:
                columns(ahead, 1 - b, t, f)
            at += 3

            def load(i, j, r):
                t = 2 * t2 + i - 1
                if t < 0:
                    return first[b, 3, 2 * f2 + j, r : r + CHUNK]
                return first[b, t, 2 * f2 + j, PAD + r : PAD + r + CHUNK]

            for r in range(0, ROWS, CHUNK):
                spread_a[q, r : r + CHUNK] = depth_rows(load, taps_a, r)
            second[t2, 1 + f2, inner] = relu(dot(spread_a[q], point_a[...]))
        for t, f in jobs[at:]:
            columns(ahead, 1 - b, t, f)

        def load_b(i, j, r):
            if i == 0:
                return second[1, j, r : r + CHUNK]
            return second[i - 1, j, PAD + r : PAD + r + CHUNK]

        for r in range(0, ROWS, CHUNK):
            spread_b[r : r + CHUNK] = depth_rows(load_b, taps_b, r)
        mapped = relu(dot(spread_b[...], point_b[...]))
        fourth[:, pl.ds(pl.multiple_of(n * CH, CH), CH)] = mapped
        for t2 in range(2):
            second[t2, 0] = second[t2, 2]

    loads[0].wait()
    for t, f in jobs:
        columns(0, 0, t, f)
    loads[1].wait()

    def two_steps(m, carry):
        step(2 * m, 0)
        step(2 * m + 1, 1)
        return carry

    lax.fori_loop(0, 5, two_steps, 0)
    loads[2].wait()
    loads[3].wait()
    out[...] = dot(fourth[...], linear[...]).astype(BF)


def subsample(windows, band, depth_a, point_a, depth_b, point_b, linear_own, linear_other):
    return pl.pallas_call(
        subsample_kernel,
        out_shape=jax.ShapeDtypeStruct((ROWS, D), BF),
        in_specs=[VMEM_SPEC, ANY_SPEC] + [VMEM_SPEC] * 4 + [ANY_SPEC] * 2,
        out_specs=VMEM_SPEC,
        scratch_shapes=[
            pltpu.VMEM((256, MELS // 2 * CH), BF),
            pltpu.VMEM((2, 4, 5, PAD + ROWS, CH), BF),
            pltpu.VMEM((4, ROWS, CH), BF),
            pltpu.VMEM((2, 3, PAD + ROWS, CH), BF),
            pltpu.VMEM((ROWS, CH), BF),
            pltpu.VMEM((ROWS, 10 * CH), BF),
            pltpu.VMEM((10 * CH, D), BF),
            pltpu.SemaphoreType.DMA((4,)),
        ],
        compiler_params=pltpu.CompilerParams(vmem_limit_bytes=67043328),
        name="subsample",
    )(windows, band, depth_a, point_a, depth_b, point_b, linear_own, linear_other)


def dot_t(a, b):
    return lax.dot_general(a, b, (((1,), (1,)), ((), ())), preferred_element_type=F32)


def dot_rows(a, b):
    return lax.dot_general(a, b, (((0,), (0,)), ((), ())), preferred_element_type=F32)


def row_mean(x):
    return jnp.sum(x, axis=1, keepdims=True) * (1.0 / D)


KER = 9
BORDER = KER // 2 * U_DEV
HALF_D = D // 2
N_TILE = 256


def lane_tile(n, start=0):
    if isinstance(n, int):
        return pl.ds(start + n * N_TILE, N_TILE)
    return pl.ds(pl.multiple_of(start + n * N_TILE, N_TILE), N_TILE)


LANES = ((0, 384), (384, 384), (768, 256))
LINE = 128
OWN = 8


def placed_at(moved, c, line, plane):
    steps = [(plane // 4, plane % 4)[k] for k in range(2)]
    steps.insert((2, 1, 0)[c], line)
    z, y, x = (moved[2 - k][steps[k]] for k in range(3))
    place = ((x, z * 4 + y), (y, z * 4 + x), (z, y * 4 + x))[c]
    return (z * 16 + y * 4 + x, *place)


def module_kernel(
    features, keep, cotangent, norm_gain, conv_gain, depth_kernel,
    up_own, up_other, down_own, down_other,
    layer_out, grad_input, shared,
    up, down, normed, stats, gate_a, gate_b, gated, standard_two, slope, hidden, back_out,
    grad_own, to_partner, from_partner, part, big, back_depth, back_proj,
    line_a, line_b, line_c, mid_a, mid_b, mid_c, wide_a, wide_b, wide_c,
    plane_a, plane_b, plane_c, mine_a, mine_b, mine_c, taps,
    load_sems, partner_send, partner_recv, send_sems, recv_sems, own_sems,
):
    me = lax.axis_index("dp")
    core = lax.axis_index("fsdp")
    other = 1 - core
    barrier = pltpu.get_barrier_semaphore()
    moved = shifts(me)
    near = [k for k in range(1, N_DP) if k < 16 or k % 16 < 4 or k % 4 == 0]
    greet_peers(barrier, me, core, moved, near)

    def part_of(which, width):
        return pl.ds(pl.multiple_of(which * width, width), width)

    loads = [
        pltpu.make_async_copy(up_own, up.at[:, part_of(core, D)], load_sems.at[0]),
        pltpu.make_async_copy(up_other, up.at[:, part_of(other, D)], load_sems.at[1]),
        pltpu.make_async_copy(down_own, down.at[part_of(core, HALF_D)], load_sems.at[2]),
        pltpu.make_async_copy(down_other, down.at[part_of(other, HALF_D)], load_sems.at[3]),
    ]
    for copy in loads:
        copy.start()

    def rows_of(g, shift=0):
        return pl.ds(pl.multiple_of((g + shift) * U_DEV, U_DEV), U_DEV)

    gain_one = norm_gain[...].astype(F32)
    gain_two = conv_gain[...].astype(F32)

    def norm_rows(g, carry):
        values = features[rows_of(g)].astype(F32)
        mean = row_mean(values)
        centred = values - mean
        scale = lax.rsqrt(row_mean(centred * centred) + EPSILON)
        normed[rows_of(g)] = (centred * scale * gain_one).astype(BF)
        stats[0, rows_of(g)] = jnp.broadcast_to(mean, (U_DEV, 128))
        stats[1, rows_of(g)] = jnp.broadcast_to(scale, (U_DEV, 128))
        return carry

    lax.fori_loop(0, SPAN, norm_rows, 0)
    gated[0:BORDER] = jnp.zeros((BORDER, D), BF)
    gated[BORDER + ROWS :] = jnp.zeros((BORDER, D), BF)
    back_depth[0:BORDER] = jnp.zeros((BORDER, D), F32)
    back_depth[BORDER + ROWS :] = jnp.zeros((BORDER, D), F32)

    out_row = iota((ROWS, ROWS), 0)
    in_row = iota((ROWS, ROWS), 1)
    to_groups = jnp.where(in_row == (out_row % U_DEV) * SPAN + out_row // U_DEV, 1.0, 0.0)
    to_groups = to_groups.astype(BF)

    loads[0].wait()
    loads[1].wait()

    def project(n, carry):
        value = dot(normed[...], up[:, lane_tile(n)])
        gate = jax.nn.sigmoid(dot(normed[...], up[:, lane_tile(n, D)]))
        both = value * gate
        gate_a[:, lane_tile(n)] = gate
        gate_b[:, lane_tile(n)] = both * (1.0 - gate)
        gated[BORDER : BORDER + ROWS, lane_tile(n)] = (keep[:, :1] * both).astype(BF)
        moved = dot(to_groups, cotangent[:, lane_tile(n)])
        back_out[:, lane_tile(n)] = jnp.where(keep[:, :1] > 0, moved, 0.0).astype(BF)
        return carry

    for n in range(D // N_TILE):
        project(n, 0)

    for k in range(KER):
        taps[k] = jnp.broadcast_to(depth_kernel[k : k + 1], (U_DEV, D))

    def conv_rows(g, carry):
        summed = None
        for k in range(0, KER, 3):
            terms = [gated[rows_of(g, k + i)] * taps[k + i] for i in range(3)]
            term = (terms[0] + terms[1] + terms[2]).astype(F32)
            summed = term if summed is None else summed + term
        centred = summed - row_mean(summed)
        scale = lax.rsqrt(row_mean(centred * centred) + EPSILON)
        standard = centred * scale
        active = standard * gain_two
        swish = jax.nn.sigmoid(active)
        act = active * swish
        hidden[rows_of(g)] = act.astype(BF)
        standard_two[rows_of(g)] = standard
        slope[rows_of(g)] = (swish + act * (1.0 - swish)) * gain_two
        stats[2, rows_of(g)] = jnp.broadcast_to(scale, (U_DEV, 128))
        return carry

    lax.fori_loop(0, SPAN, conv_rows, 0)

    def grad_rows(which):
        return dot_rows(hidden[:, part_of(which, HALF_D)], back_out[...])

    to_partner[...] = grad_rows(other).astype(BF)
    pl.semaphore_wait(barrier, 1 + len(near))
    swaps = []
    for c, (at, width) in enumerate(LANES):
        copy = pltpu.make_async_remote_copy(
            src_ref=to_partner.at[:, at : at + width],
            dst_ref=from_partner.at[:, at : at + width],
            send_sem=partner_send.at[c],
            recv_sem=partner_recv.at[c],
            device_id=(me, other),
            device_id_type=MESH,
        )
        copy.start()
        swaps.append(copy)
    grad_own[...] = grad_rows(core)

    line_in = (line_a, line_b, line_c)
    mid = (mid_a, mid_b, mid_c)
    wide = (wide_a, wide_b, wide_c)
    plane_in = (plane_a, plane_b, plane_c)
    mine = (mine_a, mine_b, mine_c)

    def line_rows(a):
        return pl.ds(pl.multiple_of(a * LINE, LINE), LINE)

    def own_rows(a, p):
        return pl.ds(pl.multiple_of(a * LINE + p * OWN, OWN), OWN)

    def push(stage, c, src, dst, peer):
        pltpu.make_async_remote_copy(
            src_ref=src,
            dst_ref=dst,
            send_sem=send_sems.at[stage, c],
            recv_sem=recv_sems.at[stage, c],
            device_id=(peer, core),
            device_id_type=MESH,
        ).start()

    def await_block(block, sem):
        pltpu.make_async_copy(block, block, sem).wait()

    def reduce_lines():
        for c, (at, width) in enumerate(LANES):
            swaps[c].wait()
            lanes = slice(at, at + width)
            part[:, lanes] = (grad_own[:, lanes] + from_partner[:, lanes].astype(F32)).astype(BF)
            for step in range(1, 4):
                peer, a, _ = placed_at(moved, c, step, 0)
                push(
                    0, c, part.at[line_rows(a), at : at + width], line_in[c].at[step - 1], peer
                )

    def reduce_planes():
        for c, (at, width) in enumerate(LANES):
            _, a, _ = placed_at(moved, c, 0, 0)
            await_block(line_in[c], recv_sems.at[0, c])
            total = part[line_rows(a), at : at + width].astype(F32)
            for k in range(3):
                total = total + line_in[c][k].astype(F32)
            wide[c][...] = total
            mid[c][...] = total.astype(BF)
        for c in range(3):
            for step in range(1, 16):
                peer, _, p = placed_at(moved, c, 0, step)
                rows = pl.ds(pl.multiple_of(p * OWN, OWN), OWN)
                push(1, c, mid[c].at[rows], plane_in[c].at[step - 1], peer)

    def spot_of(c):
        at, width = LANES[c]
        _, a, p = placed_at(moved, c, 0, 0)
        return shared.at[own_rows(a, p), at : at + width]

    def gather_planes():
        for c in range(3):
            _, _, p = placed_at(moved, c, 0, 0)
            await_block(plane_in[c], recv_sems.at[1, c])
            total = wide[c][pl.ds(pl.multiple_of(p * OWN, OWN), OWN)]
            for k in range(15):
                total = total + plane_in[c][k].astype(F32)
            mine[c][...] = (total * (1.0 / math.sqrt(ROWS * N_DP * 2))).astype(BF)
        for c in range(3):
            pltpu.make_async_copy(mine[c], spot_of(c), own_sems.at[c]).start()
            for step in range(1, 16):
                push(2, c, mine[c], spot_of(c), placed_at(moved, c, 0, step)[0])

    def gather_lines():
        for c, (at, width) in enumerate(LANES):
            pltpu.make_async_copy(mine[c], spot_of(c), own_sems.at[c]).wait()
            await_block(plane_in[c], recv_sems.at[2, c])
            block = shared.at[line_rows(placed_at(moved, c, 0, 0)[1]), at : at + width]
            for step in range(1, 4):
                push(3, c, block, block, placed_at(moved, c, step, 0)[0])

    reduce_lines()
    loads[2].wait()
    loads[3].wait()
    to_panels = jnp.where(in_row == (out_row % SPAN) * U_DEV + out_row // SPAN, 1.0, 0.0)
    to_panels = to_panels.astype(BF)

    def output(n, carry):
        mixed = dot(hidden[...], down[:, lane_tile(n)])
        total = features[:, lane_tile(n)].astype(F32) + mixed
        total = (keep[:, :1] * total).astype(BF)
        layer_out[:, lane_tile(n)] = dot(to_panels, total).astype(BF)
        return carry

    lax.fori_loop(0, D // N_TILE, output, 0)

    def back_hidden(n, carry):
        rows = down[pl.ds(pl.multiple_of(n * N_TILE, N_TILE), N_TILE)]
        big[:, lane_tile(n)] = dot_t(back_out[...], rows)
        return carry

    lax.fori_loop(0, D // N_TILE, back_hidden, 0)

    def back_norm(g, carry):
        error = big[rows_of(g)] * slope[rows_of(g)]
        standard = standard_two[rows_of(g)]
        inner = error - row_mean(error) - standard * row_mean(error * standard)
        back_depth[rows_of(g, KER // 2)] = stats[2, rows_of(g), :1] * inner
        return carry

    lax.fori_loop(0, SPAN, back_norm, 0)

    reduce_planes()

    def back_conv(g, carry):
        summed = None
        for k in range(KER):
            tap = depth_kernel[k : k + 1].astype(F32)
            term = back_depth[rows_of(g, KER - 1 - k)] * tap
            summed = term if summed is None else summed + term
        summed = keep[rows_of(g), :1] * summed
        back_proj[rows_of(g), 0:D] = (summed * gate_a[rows_of(g)]).astype(BF)
        back_proj[rows_of(g), D : 2 * D] = (summed * gate_b[rows_of(g)]).astype(BF)
        return carry

    lax.fori_loop(0, SPAN, back_conv, 0)

    gather_planes()

    def back_up(n, carry):
        rows = up[pl.ds(pl.multiple_of(n * N_TILE, N_TILE), N_TILE)]
        big[:, lane_tile(n)] = dot_t(back_proj[...], rows)
        return carry

    lax.fori_loop(0, D // N_TILE, back_up, 0)

    gather_lines()

    def back_first(g, carry):
        front = big[rows_of(g)] * gain_one
        scale = stats[1, rows_of(g), :1]
        standard = (features[rows_of(g)].astype(F32) - stats[0, rows_of(g), :1]) * scale
        inner = front - row_mean(front) - standard * row_mean(front * standard)
        normed[rows_of(g)] = (back_out[rows_of(g)].astype(F32) + scale * inner).astype(BF)
        return carry

    lax.fori_loop(0, SPAN, back_first, 0)

    def reorder(n, carry):
        grad_input[:, lane_tile(n)] = dot(to_panels, normed[:, lane_tile(n)]).astype(BF)
        return carry

    lax.fori_loop(0, D // N_TILE, reorder, 0)
    for c in range(3):
        await_block(line_in[c], recv_sems.at[3, c])

    for c in range(3):
        await_block(line_in[c], send_sems.at[0, c])
        await_block(plane_in[c], send_sems.at[1, c])
        await_block(plane_in[c], send_sems.at[2, c])
        await_block(line_in[c], send_sems.at[3, c])


def module(features, keep, cotangent, norm_gain, conv_gain, depth_kernel, ups, downs):
    rows = (ROWS, D)
    return pl.pallas_call(
        module_kernel,
        out_shape=[
            jax.ShapeDtypeStruct(rows, BF),
            jax.ShapeDtypeStruct(rows, BF),
            jax.ShapeDtypeStruct((HALF_D, D), BF),
        ],
        in_specs=[VMEM_SPEC] * 6 + [ANY_SPEC] * 4,
        out_specs=[VMEM_SPEC] * 3,
        scratch_shapes=[
            pltpu.VMEM((D, 2 * D), BF),
            pltpu.VMEM((D, D), BF),
            pltpu.VMEM(rows, BF),
            pltpu.VMEM((3, ROWS, 128), F32),
            pltpu.VMEM(rows, F32),
            pltpu.VMEM(rows, F32),
            pltpu.VMEM((ROWS + 2 * BORDER, D), BF),
            pltpu.VMEM(rows, F32),
            pltpu.VMEM(rows, F32),
            pltpu.VMEM(rows, BF),
            pltpu.VMEM(rows, BF),
            pltpu.VMEM((HALF_D, D), F32),
            pltpu.VMEM((HALF_D, D), BF),
            pltpu.VMEM((HALF_D, D), BF),
            pltpu.VMEM((HALF_D, D), BF),
            pltpu.VMEM(rows, F32),
            pltpu.VMEM((ROWS + 2 * BORDER, D), F32),
            pltpu.VMEM((ROWS, 2 * D), BF),
            *[pltpu.VMEM((3, LINE, width), BF) for _, width in LANES],
            *[pltpu.VMEM((LINE, width), BF) for _, width in LANES],
            *[pltpu.VMEM((LINE, width), F32) for _, width in LANES],
            *[pltpu.VMEM((15, OWN, width), BF) for _, width in LANES],
            *[pltpu.VMEM((OWN, width), BF) for _, width in LANES],
            pltpu.VMEM((KER, U_DEV, D), BF),
            pltpu.SemaphoreType.DMA((4,)),
            pltpu.SemaphoreType.DMA((3,)),
            pltpu.SemaphoreType.DMA((3,)),
            pltpu.SemaphoreType.DMA((4, 3)),
            pltpu.SemaphoreType.DMA((4, 3)),
            pltpu.SemaphoreType.DMA((3,)),
        ],
        compiler_params=pltpu.CompilerParams(
            collective_id=1, has_side_effects=True, vmem_limit_bytes=67043328
        ),
        name="module",
    )(features, keep, cotangent, norm_gain, conv_gain, depth_kernel, *ups, *downs)


def finish_kernel(layer_in, grad_in, down_in, layer_out, grad_input, grad_down):
    layer_out[...] = layer_in[...]
    grad_input[...] = grad_in[...]
    grad_down[...] = down_in[...].astype(F32)


def finish(layer_out, grad_input, grad_down):
    block = pl.BlockSpec((128, D), lambda i: (i, 0))
    return pl.pallas_call(
        finish_kernel,
        grid=(ROWS // 128,),
        out_shape=[
            jax.ShapeDtypeStruct((ROWS, D), BF),
            jax.ShapeDtypeStruct((ROWS, D), BF),
            jax.ShapeDtypeStruct((HALF_D, D), F32),
        ],
        in_specs=[block] * 3,
        out_specs=[block] * 3,
        compiler_params=pltpu.CompilerParams(vmem_limit_bytes=67043328),
        name="finish",
    )(layer_out, grad_input, grad_down)


def local(
    mel_panels,
    frames,
    target,
    conv_first,
    depth_a,
    point_a,
    depth_b,
    point_b,
    linear_weight,
    norm_gain,
    up_weight,
    depth_kernel,
    conv_gain,
    down_weight,
    cotangent,
):
    small = (
        conv_first,
        depth_a,
        point_a,
        depth_b,
        point_b,
        norm_gain.reshape(-1, 128),
        conv_gain.reshape(-1, 128),
        depth_kernel,
    )
    big = (linear_weight, up_weight, down_weight)
    windows, keep, band, full, other = exchange(frames[None], target[None], mel_panels, small, big)
    features = subsample(windows, band, *full[1:5], linear_weight, other[0])
    results = module(
        features,
        keep,
        cotangent,
        full[5],
        full[6],
        full[7],
        (up_weight, other[1]),
        (down_weight, other[2]),
    )
    return tuple(finish(*results))


def solution(mesh):
    placed = (
        P(("dp", "fsdp"), None),
        P(("dp", "fsdp")),
        P(("dp", "fsdp")),
        P(None, "fsdp"),
        P(None, "fsdp"),
        P(None, "fsdp"),
        P(None, "fsdp"),
        P(None, "fsdp"),
        P(None, "fsdp"),
        P("fsdp"),
        P(None, "fsdp"),
        P(None, "fsdp"),
        P("fsdp"),
        P("fsdp", None),
        P(("dp", "fsdp"), None),
    )
    return jax.shard_map(
        local,
        mesh=mesh,
        in_specs=placed,
        out_specs=(P(("dp", "fsdp"), None), P(("dp", "fsdp"), None), P("fsdp", None)),
        check_vma=False,
    )
```

```python
import functools
import math

import jax
import jax.numpy as jnp
from jax import lax
from jax.experimental import pallas as pl
from jax.experimental.pallas import tpu as pltpu
from jax.sharding import PartitionSpec as P

MELS = 80
PANEL = 128
EPSILON = 1e-05
SPAN = 16
GROUP = 8 * MELS
N_DP = 64
U_DEV = 32
ROWS = U_DEV * SPAN
D = 1024
CH = 256
HALF = CH // 2
MARK = 64.0
MESH = pl.DeviceIdType.MESH
VMEM_SPEC = pl.BlockSpec(memory_space=pltpu.VMEM)
ANY_SPEC = pl.BlockSpec(memory_space=pl.ANY)
BF = jnp.bfloat16
F32 = jnp.float32


def iota(shape, dim):
    return lax.broadcasted_iota(jnp.int32, shape, dim)


def dot(a, b):
    return jnp.dot(a, b, preferred_element_type=F32)


def shifts(me):
    return tuple([(me // by + k) % 4 for k in range(4)] for by in (1, 4, 16))


def hops(step):
    return sum((0, 1, 2, 1)[step // by % 4] for by in (1, 4, 16))


FAR_FIRST = sorted(range(1, N_DP), key=lambda step: -hops(step))
PLANE_STEPS = sorted(range(1, 16), key=lambda step: -hops(step))


def peer_at(moved, step):
    x, y, z = moved
    return z[step // 16] * 16 + y[step // 4 % 4] * 4 + x[step % 4]


def greet_peers(barrier, me, core, moved, steps):
    pl.semaphore_signal(barrier, inc=1, device_id=(me, 1 - core), device_id_type=MESH)
    for step in steps:
        pl.semaphore_signal(
            barrier, inc=1, device_id=(peer_at(moved, step), core), device_id_type=MESH
        )


N_SMALL = 8
GAINS = (5, 6)
N_BIG = 3


def exchange_kernel(*refs):
    frames, target, mel_in = refs[:3]
    small = refs[3 : 3 + N_SMALL]
    big = refs[11:14]
    windows, keep_out, band_out = refs[14:17]
    small_full = refs[17 : 17 + N_SMALL]
    big_other = refs[25:28]
    flat, outgoing, incoming, band_in, mel = refs[28:33]
    small_other = refs[33 : 33 + N_SMALL]
    small_send, small_recv, big_send, big_recv, send_sem, recv_sem, band_sem, mel_sem = refs[41:]

    me = lax.axis_index("dp")
    core = lax.axis_index("fsdp")
    other = 1 - core
    barrier = pltpu.get_barrier_semaphore()
    mel_copy = pltpu.make_async_copy(mel_in, mel, mel_sem)
    mel_copy.start()
    moved = shifts(me)
    greet_peers(barrier, me, core, moved, range(1, N_DP))

    picks = (target[...] == iota((N_DP, 64), 0)) & (frames[...] > 0)
    length = jnp.sum(jnp.where(picks, frames[...], 0), axis=1, keepdims=True)
    chosen = jnp.where(picks, 1.0, 0.0).astype(BF)
    mel_copy.wait()
    for g in range(SPAN):
        rows = dot(chosen, mel[:, g * GROUP : (g + 1) * GROUP])
        rows = jnp.where(length > 8 * g, rows, MARK)
        for k in range(GROUP // 128):
            flat[k, pl.ds(g, N_DP, stride=SPAN), :] = rows[:, k * 128 : (k + 1) * 128]
    for k in range(GROUP // 128):
        outgoing[:, :, k * 128 : (k + 1) * 128] = flat[k].reshape(N_DP, SPAN, 128).astype(BF)

    pl.semaphore_wait(barrier, N_DP)

    partner = []
    for k in range(N_SMALL):
        copy = pltpu.make_async_remote_copy(
            src_ref=small[k],
            dst_ref=small_other[k],
            send_sem=small_send.at[k],
            recv_sem=small_recv.at[k],
            device_id=(me, other),
            device_id_type=MESH,
        )
        copy.start()
        partner.append(copy)

    for step in FAR_FIRST:
        peer = peer_at(moved, step)
        pltpu.make_async_remote_copy(
            src_ref=outgoing.at[peer],
            dst_ref=incoming.at[me],
            send_sem=send_sem,
            recv_sem=recv_sem,
            device_id=(peer, core),
            device_id_type=MESH,
        ).start()
    for k in range(N_BIG):
        copy = pltpu.make_async_remote_copy(
            src_ref=big[k],
            dst_ref=big_other[k],
            send_sem=big_send.at[k],
            recv_sem=big_recv.at[k],
            device_id=(me, other),
            device_id_type=MESH,
        )
        copy.start()
        partner.append(copy)
    incoming[pl.ds(me, 1)] = outgoing[pl.ds(me, 1)]

    for k in range(N_SMALL):
        partner[k].wait()
        for which, ref in ((core, small[k]), (other, small_other[k])):
            if k in GAINS:
                lines = ref[...].astype(F32)
                for i in range(D // 2 // 128):
                    at = pl.multiple_of(which * (D // 2) + i * 128, 128)
                    small_full[k][:, pl.ds(at, 128)] = lines[i : i + 1].astype(BF)
            else:
                width = ref.shape[1]
                small_full[k][:, pl.ds(pl.multiple_of(which * width, 128), width)] = ref[...]

    taps = small_full[0][...]
    row = iota((256, 9), 0)
    tap = iota((256, 9), 1)
    base = row - 80 * (tap // 3) - tap % 3 + 1

    def band(f, carry):
        b = base + (tap % 3) - 1
        hit = (base == 2 * f) & (b >= 0) & (b < MELS)
        column = dot(jnp.where(hit, 1.0, 0.0).astype(BF), taps)
        band_in[:, pl.ds(pl.multiple_of(f * CH, CH), CH)] = column.astype(BF)
        return carry

    lax.fori_loop(0, MELS // 2, band, 0)
    band_copy = pltpu.make_async_copy(band_in, band_out, band_sem)
    band_copy.start()

    sent = outgoing.at[pl.ds(0, N_DP - 1)]
    got = incoming.at[pl.ds(0, N_DP - 1)]
    pltpu.make_async_copy(got, got, recv_sem).wait()

    total = N_DP * SPAN
    panels = incoming[...].reshape(total, GROUP)
    first_lane = jnp.where(iota((8, GROUP), 1) == 0, 1.0, 0.0).astype(BF)
    heads = lax.dot_general(
        first_lane, panels, (((1,), (1,)), ((), ())), preferred_element_type=F32
    )
    live_row = jnp.where(heads < MARK / 2, 1.0, 0.0).astype(BF)
    pick_heads = jnp.where(iota((total, 64), 0) == SPAN * iota((total, 64), 1), 1.0, 0.0)
    present = dot(live_row, pick_heads.astype(BF)).astype(BF)
    before = jnp.where(iota((64, 64), 0) < iota((64, 64), 1), 1.0, 0.0).astype(BF)
    place = dot(present, before).astype(BF)
    spread = jnp.where(iota((64, total), 1) // SPAN == iota((64, total), 0), 1.0, 0.0).astype(BF)
    present_row = dot(present, spread)[:1]
    place_row = dot(place, spread)[:1].astype(jnp.int32)
    goal = jnp.where(
        present_row > 0.5, (iota((1, total), 1) % SPAN) * U_DEV + place_row, -1
    )
    move = jnp.where(iota((ROWS, total), 0) == goal, 1.0, 0.0).astype(BF)
    x = dot(move, panels)
    keep = x[:, :1] < MARK / 2
    x = jnp.where(keep, x, 0.0)
    keep_out[...] = jnp.broadcast_to(jnp.where(keep, 1.0, 0.0), (ROWS, 128))

    late = jnp.concatenate([jnp.zeros((U_DEV, 128), F32), x[: ROWS - U_DEV, 512:]], axis=0)
    late = pltpu.roll(late, 80, 1)
    now = pltpu.roll(x[:, :256], 80, 1)
    lanes = iota((ROWS, 128), 1)
    w0 = jnp.concatenate([jnp.where(lanes < 80, late, now[:, :128]), now[:, 128:]], axis=1)
    windows[0:ROWS] = w0.astype(BF)
    windows[ROWS : 2 * ROWS] = pltpu.roll(x[:, :384], 384 - 80, 1)[:, :256].astype(BF)
    windows[2 * ROWS : 3 * ROWS] = pltpu.roll(x[:, 128:512], 384 - 112, 1)[:, :256].astype(BF)
    windows[3 * ROWS : 4 * ROWS] = pltpu.roll(x[:, 384:], 256 - 16, 1).astype(BF)

    pltpu.make_async_copy(sent, sent, send_sem).wait()
    for k in range(N_SMALL, N_SMALL + N_BIG):
        partner[k].wait()
    band_copy.wait()


def exchange(frames, target, mel, small, big):
    small_full = [
        jax.ShapeDtypeStruct((1, D) if k in GAINS else (a.shape[0], 2 * a.shape[1]), BF)
        for k, a in enumerate(small)
    ]
    shapes = [
        jax.ShapeDtypeStruct((4 * ROWS, 256), BF),
        jax.ShapeDtypeStruct((ROWS, 128), F32),
        jax.ShapeDtypeStruct((256, MELS // 2 * CH), BF),
        *small_full,
        *[jax.ShapeDtypeStruct(a.shape, BF) for a in big],
    ]
    out = pl.pallas_call(
        exchange_kernel,
        out_shape=shapes,
        in_specs=[VMEM_SPEC] * 2 + [ANY_SPEC] + [VMEM_SPEC] * N_SMALL + [ANY_SPEC] * N_BIG,
        out_specs=[VMEM_SPEC] * 2 + [ANY_SPEC] + [VMEM_SPEC] * N_SMALL + [ANY_SPEC] * N_BIG,
        scratch_shapes=[
            pltpu.VMEM((GROUP // 128, N_DP * SPAN, 128), F32),
            pltpu.VMEM((N_DP, SPAN, GROUP), BF),
            pltpu.VMEM((N_DP, SPAN, GROUP), BF),
            pltpu.VMEM((256, MELS // 2 * CH), BF),
            pltpu.VMEM((64, SPAN * GROUP), BF),
            *[pltpu.VMEM(a.shape, BF) for a in small],
            pltpu.SemaphoreType.DMA((N_SMALL,)),
            pltpu.SemaphoreType.DMA((N_SMALL,)),
            pltpu.SemaphoreType.DMA((N_BIG,)),
            pltpu.SemaphoreType.DMA((N_BIG,)),
            pltpu.SemaphoreType.DMA,
            pltpu.SemaphoreType.DMA,
            pltpu.SemaphoreType.DMA,
            pltpu.SemaphoreType.DMA,
        ],
        compiler_params=pltpu.CompilerParams(
            collective_id=0, has_side_effects=True, vmem_limit_bytes=67043328
        ),
        name="exchange",
    )(frames, target, mel, *small, *big)
    return out[0], out[1], out[2], out[3 : 3 + N_SMALL], out[3 + N_SMALL :]


CHUNK = 64
PAD = U_DEV


def depth_rows(load, taps, r):
    total = None
    for i in range(3):
        for j in range(3):
            term = load(i, j, r) * taps[3 * i + j]
            total = term if total is None else total + term
    return total


def subsample_kernel(
    windows, band_in, depth_a, point_a, depth_b, point_b, linear_own, linear_other, out,
    band, first, spread_a, second, spread_b, fourth, linear, sems
):
    core = lax.axis_index("fsdp")
    width = D // 2

    def half(which):
        return linear.at[:, pl.ds(pl.multiple_of(which * width, width), width)]

    early, late = pl.ds(0, 4 * CH), pl.ds(4 * CH, MELS // 2 * CH - 4 * CH)
    loads = [
        pltpu.make_async_copy(band_in.at[:, early], band.at[:, early], sems.at[0]),
        pltpu.make_async_copy(band_in.at[:, late], band.at[:, late], sems.at[1]),
        pltpu.make_async_copy(linear_own, half(core), sems.at[2]),
        pltpu.make_async_copy(linear_other, half(1 - core), sems.at[3]),
    ]
    for copy in loads:
        copy.start()
    inner = slice(PAD, PAD + ROWS)
    first[0, :, 0] = jnp.zeros((4, PAD + ROWS, CH), BF)
    second[:, 0] = jnp.zeros((2, PAD + ROWS, CH), BF)
    for col in range(1, 5):
        for b in range(2):
            first[b, 3, col, 0:PAD] = jnp.zeros((PAD, CH), BF)
    for col in range(1, 3):
        second[1, col, 0:PAD] = jnp.zeros((PAD, CH), BF)
    taps_a = [jnp.broadcast_to(depth_a[k : k + 1], (CHUNK, CH)) for k in range(9)]
    taps_b = [jnp.broadcast_to(depth_b[k : k + 1], (CHUNK, CH)) for k in range(9)]

    def relu(x):
        return jnp.maximum(x.astype(BF), 0)

    def columns(n, b, t, f):
        w = band[:, pl.ds(pl.multiple_of(n * 4 * CH + f * CH, CH), CH)]
        first[b, t, 1 + f, inner] = relu(dot(windows[t * ROWS : (t + 1) * ROWS], w))

    jobs = [(t, f) for f in range(4) for t in range(4)]

    def step(n, b):
        ahead = jnp.minimum(n + 1, 9)
        for t in range(3):
            first[1 - b, t, 0, inner] = first[b, t, 4, inner]
        first[1 - b, 3, 0] = first[b, 3, 4]
        at = 0
        for q in range(4):
            t2, f2 = q // 2, q % 2
            for t, f in jobs[at : at + 3]:
                columns(ahead, 1 - b, t, f)
            at += 3

            def load(i, j, r):
                t = 2 * t2 + i - 1
                if t < 0:
                    return first[b, 3, 2 * f2 + j, r : r + CHUNK]
                return first[b, t, 2 * f2 + j, PAD + r : PAD + r + CHUNK]

            for r in range(0, ROWS, CHUNK):
                spread_a[q, r : r + CHUNK] = depth_rows(load, taps_a, r)
            second[t2, 1 + f2, inner] = relu(dot(spread_a[q], point_a[...]))
        for t, f in jobs[at:]:
            columns(ahead, 1 - b, t, f)

        def load_b(i, j, r):
            if i == 0:
                return second[1, j, r : r + CHUNK]
            return second[i - 1, j, PAD + r : PAD + r + CHUNK]

        for r in range(0, ROWS, CHUNK):
            spread_b[r : r + CHUNK] = depth_rows(load_b, taps_b, r)
        mapped = relu(dot(spread_b[...], point_b[...]))
        fourth[:, pl.ds(pl.multiple_of(n * CH, CH), CH)] = mapped
        for t2 in range(2):
            second[t2, 0] = second[t2, 2]

    loads[0].wait()
    for t, f in jobs:
        columns(0, 0, t, f)
    loads[1].wait()

    def two_steps(m, carry):
        step(2 * m, 0)
        step(2 * m + 1, 1)
        return carry

    lax.fori_loop(0, 5, two_steps, 0)
    loads[2].wait()
    loads[3].wait()
    out[...] = dot(fourth[...], linear[...]).astype(BF)


def subsample(windows, band, depth_a, point_a, depth_b, point_b, linear_own, linear_other):
    return pl.pallas_call(
        subsample_kernel,
        out_shape=jax.ShapeDtypeStruct((ROWS, D), BF),
        in_specs=[VMEM_SPEC, ANY_SPEC] + [VMEM_SPEC] * 4 + [ANY_SPEC] * 2,
        out_specs=VMEM_SPEC,
        scratch_shapes=[
            pltpu.VMEM((256, MELS // 2 * CH), BF),
            pltpu.VMEM((2, 4, 5, PAD + ROWS, CH), BF),
            pltpu.VMEM((4, ROWS, CH), BF),
            pltpu.VMEM((2, 3, PAD + ROWS, CH), BF),
            pltpu.VMEM((ROWS, CH), BF),
            pltpu.VMEM((ROWS, 10 * CH), BF),
            pltpu.VMEM((10 * CH, D), BF),
            pltpu.SemaphoreType.DMA((4,)),
        ],
        compiler_params=pltpu.CompilerParams(vmem_limit_bytes=67043328),
        name="subsample",
    )(windows, band, depth_a, point_a, depth_b, point_b, linear_own, linear_other)


def dot_t(a, b):
    return lax.dot_general(a, b, (((1,), (1,)), ((), ())), preferred_element_type=F32)


def dot_rows(a, b):
    return lax.dot_general(a, b, (((0,), (0,)), ((), ())), preferred_element_type=F32)


def row_mean(x):
    return jnp.sum(x, axis=1, keepdims=True) * (1.0 / D)


KER = 9
BORDER = KER // 2 * U_DEV
HALF_D = D // 2
N_TILE = 256


def lane_tile(n, start=0):
    if isinstance(n, int):
        return pl.ds(start + n * N_TILE, N_TILE)
    return pl.ds(pl.multiple_of(start + n * N_TILE, N_TILE), N_TILE)


LANES = ((0, 384), (384, 384), (768, 256))
LINE = 128
OWN = 8


def placed_at(moved, c, line, plane):
    steps = [(plane // 4, plane % 4)[k] for k in range(2)]
    steps.insert((2, 1, 0)[c], line)
    z, y, x = (moved[2 - k][steps[k]] for k in range(3))
    place = ((x, z * 4 + y), (y, z * 4 + x), (z, y * 4 + x))[c]
    return (z * 16 + y * 4 + x, *place)


def module_kernel(
    features, keep, cotangent, norm_gain, conv_gain, depth_kernel,
    up_own, up_other, down_own, down_other,
    layer_out, grad_input, shared,
    up, down, normed, stats, gate_a, gate_b, gated, standard_two, hidden, back_out,
    grad_own, to_partner, from_partner, part, big, back_depth, back_proj,
    line_a, line_b, line_c, mid_a, mid_b, mid_c, wide_a, wide_b, wide_c,
    plane_a, plane_b, plane_c, mine_a, mine_b, mine_c, taps,
    load_sems, partner_send, partner_recv, send_sems, recv_sems, own_sems,
):
    me = lax.axis_index("dp")
    core = lax.axis_index("fsdp")
    other = 1 - core
    barrier = pltpu.get_barrier_semaphore()
    moved = shifts(me)
    near = [k for k in range(1, N_DP) if k < 16 or k % 16 < 4 or k % 4 == 0]
    greet_peers(barrier, me, core, moved, near)

    def part_of(which, width):
        return pl.ds(pl.multiple_of(which * width, width), width)

    loads = [
        pltpu.make_async_copy(up_own, up.at[:, part_of(core, D)], load_sems.at[0]),
        pltpu.make_async_copy(up_other, up.at[:, part_of(other, D)], load_sems.at[1]),
        pltpu.make_async_copy(down_own, down.at[part_of(core, HALF_D)], load_sems.at[2]),
        pltpu.make_async_copy(down_other, down.at[part_of(other, HALF_D)], load_sems.at[3]),
    ]
    for copy in loads:
        copy.start()

    def rows_of(g, shift=0):
        return pl.ds(pl.multiple_of((g + shift) * U_DEV, U_DEV), U_DEV)

    gain_one = norm_gain[...].astype(F32)
    gain_two = conv_gain[...].astype(F32)

    def norm_rows(g, carry):
        values = features[rows_of(g)].astype(F32)
        mean = row_mean(values)
        centred = values - mean
        scale = lax.rsqrt(row_mean(centred * centred) + EPSILON)
        normed[rows_of(g)] = (centred * scale * gain_one).astype(BF)
        stats[0, rows_of(g)] = jnp.broadcast_to(mean, (U_DEV, 128))
        stats[1, rows_of(g)] = jnp.broadcast_to(scale, (U_DEV, 128))
        return carry

    lax.fori_loop(0, SPAN, norm_rows, 0)
    gated[0:BORDER] = jnp.zeros((BORDER, D), BF)
    gated[BORDER + ROWS :] = jnp.zeros((BORDER, D), BF)
    back_depth[0:BORDER] = jnp.zeros((BORDER, D), F32)
    back_depth[BORDER + ROWS :] = jnp.zeros((BORDER, D), F32)

    out_row = iota((ROWS, ROWS), 0)
    in_row = iota((ROWS, ROWS), 1)
    to_groups = jnp.where(in_row == (out_row % U_DEV) * SPAN + out_row // U_DEV, 1.0, 0.0)
    to_groups = to_groups.astype(BF)

    loads[0].wait()
    loads[1].wait()

    def project(n, carry):
        value = dot(normed[...], up[:, lane_tile(n)])
        gate = jax.nn.sigmoid(dot(normed[...], up[:, lane_tile(n, D)]))
        both = value * gate
        gate_a[:, lane_tile(n)] = gate
        gate_b[:, lane_tile(n)] = both
        gated[BORDER : BORDER + ROWS, lane_tile(n)] = (keep[:, :1] * both).astype(BF)
        moved = dot(to_groups, cotangent[:, lane_tile(n)])
        back_out[:, lane_tile(n)] = jnp.where(keep[:, :1] > 0, moved, 0.0).astype(BF)
        return carry

    for n in range(D // N_TILE):
        project(n, 0)

    for k in range(KER):
        taps[k] = jnp.broadcast_to(depth_kernel[k : k + 1], (U_DEV, D))

    def conv_rows(g, carry):
        summed = None
        for k in range(0, KER, 3):
            terms = [gated[rows_of(g, k + i)] * taps[k + i] for i in range(3)]
            term = (terms[0] + terms[1] + terms[2]).astype(F32)
            summed = term if summed is None else summed + term
        centred = summed - row_mean(summed)
        scale = lax.rsqrt(row_mean(centred * centred) + EPSILON)
        standard = centred * scale
        active = standard * gain_two
        swish = jax.nn.sigmoid(active)
        act = active * swish
        hidden[rows_of(g)] = act.astype(BF)
        standard_two[rows_of(g)] = standard
        stats[2, rows_of(g)] = jnp.broadcast_to(scale, (U_DEV, 128))
        return carry

    lax.fori_loop(0, SPAN, conv_rows, 0)

    def grad_rows(which):
        return dot_rows(hidden[:, part_of(which, HALF_D)], back_out[...])

    to_partner[...] = grad_rows(other).astype(BF)
    pl.semaphore_wait(barrier, 1 + len(near))
    swaps = []
    for c, (at, width) in enumerate(LANES):
        copy = pltpu.make_async_remote_copy(
            src_ref=to_partner.at[:, at : at + width],
            dst_ref=from_partner.at[:, at : at + width],
            send_sem=partner_send.at[c],
            recv_sem=partner_recv.at[c],
            device_id=(me, other),
            device_id_type=MESH,
        )
        copy.start()
        swaps.append(copy)
    grad_own[...] = grad_rows(core)

    line_in = (line_a, line_b, line_c)
    mid = (mid_a, mid_b, mid_c)
    wide = (wide_a, wide_b, wide_c)
    plane_in = (plane_a, plane_b, plane_c)
    mine = (mine_a, mine_b, mine_c)

    def line_rows(a):
        return pl.ds(pl.multiple_of(a * LINE, LINE), LINE)

    def own_rows(a, p):
        return pl.ds(pl.multiple_of(a * LINE + p * OWN, OWN), OWN)

    def push(stage, c, src, dst, peer):
        pltpu.make_async_remote_copy(
            src_ref=src,
            dst_ref=dst,
            send_sem=send_sems.at[stage, c],
            recv_sem=recv_sems.at[stage, c],
            device_id=(peer, core),
            device_id_type=MESH,
        ).start()

    def await_block(block, sem):
        pltpu.make_async_copy(block, block, sem).wait()

    def reduce_lines():
        for c, (at, width) in enumerate(LANES):
            swaps[c].wait()
            lanes = slice(at, at + width)
            part[:, lanes] = (grad_own[:, lanes] + from_partner[:, lanes].astype(F32)).astype(BF)
            for step in range(1, 4):
                peer, a, _ = placed_at(moved, c, step, 0)
                push(
                    0, c, part.at[line_rows(a), at : at + width], line_in[c].at[step - 1], peer
                )

    def reduce_planes():
        for c, (at, width) in enumerate(LANES):
            _, a, _ = placed_at(moved, c, 0, 0)
            await_block(line_in[c], recv_sems.at[0, c])
            total = part[line_rows(a), at : at + width].astype(F32)
            for k in range(3):
                total = total + line_in[c][k].astype(F32)
            wide[c][...] = total
            mid[c][...] = total.astype(BF)
        for c in range(3):
            for step in PLANE_STEPS:
                peer, _, p = placed_at(moved, c, 0, step)
                rows = pl.ds(pl.multiple_of(p * OWN, OWN), OWN)
                push(1, c, mid[c].at[rows], plane_in[c].at[step - 1], peer)

    def spot_of(c):
        at, width = LANES[c]
        _, a, p = placed_at(moved, c, 0, 0)
        return shared.at[own_rows(a, p), at : at + width]

    def gather_planes():
        for c in range(3):
            _, _, p = placed_at(moved, c, 0, 0)
            await_block(plane_in[c], recv_sems.at[1, c])
            total = wide[c][pl.ds(pl.multiple_of(p * OWN, OWN), OWN)]
            for k in range(15):
                total = total + plane_in[c][k].astype(F32)
            mine[c][...] = (total * (1.0 / math.sqrt(ROWS * N_DP * 2))).astype(BF)
        for c in range(3):
            pltpu.make_async_copy(mine[c], spot_of(c), own_sems.at[c]).start()
            for step in PLANE_STEPS:
                push(2, c, mine[c], spot_of(c), placed_at(moved, c, 0, step)[0])

    def gather_lines():
        for c, (at, width) in enumerate(LANES):
            pltpu.make_async_copy(mine[c], spot_of(c), own_sems.at[c]).wait()
            await_block(plane_in[c], recv_sems.at[2, c])
            block = shared.at[line_rows(placed_at(moved, c, 0, 0)[1]), at : at + width]
            for step in range(1, 4):
                push(3, c, block, block, placed_at(moved, c, step, 0)[0])

    reduce_lines()
    loads[2].wait()
    loads[3].wait()
    to_panels = jnp.where(in_row == (out_row % SPAN) * U_DEV + out_row // SPAN, 1.0, 0.0)
    to_panels = to_panels.astype(BF)

    def output(n, carry):
        mixed = dot(hidden[...], down[:, lane_tile(n)])
        total = features[:, lane_tile(n)].astype(F32) + mixed
        total = (keep[:, :1] * total).astype(BF)
        layer_out[:, lane_tile(n)] = dot(to_panels, total).astype(BF)
        return carry

    lax.fori_loop(0, D // N_TILE, output, 0)

    def back_hidden(n, carry):
        rows = down[pl.ds(pl.multiple_of(n * N_TILE, N_TILE), N_TILE)]
        big[:, lane_tile(n)] = dot_t(back_out[...], rows)
        return carry

    lax.fori_loop(0, D // N_TILE, back_hidden, 0)

    def back_norm(g, carry):
        standard = standard_two[rows_of(g)]
        active = standard * gain_two
        swish = jax.nn.sigmoid(active)
        error = big[rows_of(g)] * ((swish + active * swish * (1.0 - swish)) * gain_two)
        inner = error - row_mean(error) - standard * row_mean(error * standard)
        back_depth[rows_of(g, KER // 2)] = stats[2, rows_of(g), :1] * inner
        return carry

    lax.fori_loop(0, SPAN, back_norm, 0)

    reduce_planes()

    def back_conv(g, carry):
        summed = None
        for k in range(KER):
            tap = depth_kernel[k : k + 1].astype(F32)
            term = back_depth[rows_of(g, KER - 1 - k)] * tap
            summed = term if summed is None else summed + term
        summed = keep[rows_of(g), :1] * summed
        gate = gate_a[rows_of(g)]
        back_proj[rows_of(g), 0:D] = (summed * gate).astype(BF)
        inner = summed * gate_b[rows_of(g)] * (1.0 - gate)
        back_proj[rows_of(g), D : 2 * D] = inner.astype(BF)
        return carry

    lax.fori_loop(0, SPAN, back_conv, 0)

    gather_planes()

    def back_up(n, carry):
        rows = up[pl.ds(pl.multiple_of(n * N_TILE, N_TILE), N_TILE)]
        big[:, lane_tile(n)] = dot_t(back_proj[...], rows)
        return carry

    lax.fori_loop(0, D // N_TILE, back_up, 0)

    gather_lines()

    def back_first(g, carry):
        front = big[rows_of(g)] * gain_one
        scale = stats[1, rows_of(g), :1]
        standard = (features[rows_of(g)].astype(F32) - stats[0, rows_of(g), :1]) * scale
        inner = front - row_mean(front) - standard * row_mean(front * standard)
        normed[rows_of(g)] = (back_out[rows_of(g)].astype(F32) + scale * inner).astype(BF)
        return carry

    lax.fori_loop(0, SPAN, back_first, 0)

    def reorder(n, carry):
        grad_input[:, lane_tile(n)] = dot(to_panels, normed[:, lane_tile(n)]).astype(BF)
        return carry

    lax.fori_loop(0, D // N_TILE, reorder, 0)
    for c in range(3):
        await_block(line_in[c], recv_sems.at[3, c])

    for c in range(3):
        await_block(line_in[c], send_sems.at[0, c])
        await_block(plane_in[c], send_sems.at[1, c])
        await_block(plane_in[c], send_sems.at[2, c])
        await_block(line_in[c], send_sems.at[3, c])


def module(features, keep, cotangent, norm_gain, conv_gain, depth_kernel, ups, downs):
    rows = (ROWS, D)
    return pl.pallas_call(
        module_kernel,
        out_shape=[
            jax.ShapeDtypeStruct(rows, BF),
            jax.ShapeDtypeStruct(rows, BF),
            jax.ShapeDtypeStruct((HALF_D, D), BF),
        ],
        in_specs=[VMEM_SPEC] * 6 + [ANY_SPEC] * 4,
        out_specs=[VMEM_SPEC] * 3,
        scratch_shapes=[
            pltpu.VMEM((D, 2 * D), BF),
            pltpu.VMEM((D, D), BF),
            pltpu.VMEM(rows, BF),
            pltpu.VMEM((3, ROWS, 128), F32),
            pltpu.VMEM(rows, F32),
            pltpu.VMEM(rows, F32),
            pltpu.VMEM((ROWS + 2 * BORDER, D), BF),
            pltpu.VMEM(rows, F32),
            pltpu.VMEM(rows, BF),
            pltpu.VMEM(rows, BF),
            pltpu.VMEM((HALF_D, D), F32),
            pltpu.VMEM((HALF_D, D), BF),
            pltpu.VMEM((HALF_D, D), BF),
            pltpu.VMEM((HALF_D, D), BF),
            pltpu.VMEM(rows, F32),
            pltpu.VMEM((ROWS + 2 * BORDER, D), F32),
            pltpu.VMEM((ROWS, 2 * D), BF),
            *[pltpu.VMEM((3, LINE, width), BF) for _, width in LANES],
            *[pltpu.VMEM((LINE, width), BF) for _, width in LANES],
            *[pltpu.VMEM((LINE, width), F32) for _, width in LANES],
            *[pltpu.VMEM((15, OWN, width), BF) for _, width in LANES],
            *[pltpu.VMEM((OWN, width), BF) for _, width in LANES],
            pltpu.VMEM((KER, U_DEV, D), BF),
            pltpu.SemaphoreType.DMA((4,)),
            pltpu.SemaphoreType.DMA((3,)),
            pltpu.SemaphoreType.DMA((3,)),
            pltpu.SemaphoreType.DMA((4, 3)),
            pltpu.SemaphoreType.DMA((4, 3)),
            pltpu.SemaphoreType.DMA((3,)),
        ],
        compiler_params=pltpu.CompilerParams(
            collective_id=1, has_side_effects=True, vmem_limit_bytes=67043328
        ),
        name="module",
    )(features, keep, cotangent, norm_gain, conv_gain, depth_kernel, *ups, *downs)


def finish_kernel(
    layer_in, grad_in, down_in, layer_out, grad_input, grad_down, held, wide, in_sems, out_sems
):
    blocks = [slice(k * 128, (k + 1) * 128) for k in range(ROWS // 128)]
    pairs = ((down_in, grad_down), (layer_in, layer_out), (grad_in, grad_input))

    def arriving(k, n):
        rows = blocks[n]
        return pltpu.make_async_copy(pairs[k][0].at[rows], held.at[k, rows], in_sems.at[k, n])

    def leaving(k, n):
        rows = blocks[n]
        source = wide.at[rows] if k == 0 else held.at[k, rows]
        return pltpu.make_async_copy(source, pairs[k][1].at[rows], out_sems.at[k, n])

    order = [(k, n) for n in range(len(blocks)) for k in range(3)]
    for k, n in order:
        arriving(k, n).start()
    for k, n in order:
        arriving(k, n).wait()
        if k == 0:
            wide[blocks[n]] = held[0, blocks[n]].astype(F32)
        leaving(k, n).start()
    for k, n in order:
        leaving(k, n).wait()


def finish(layer_out, grad_input, grad_down):
    return pl.pallas_call(
        finish_kernel,
        out_shape=[
            jax.ShapeDtypeStruct((ROWS, D), BF),
            jax.ShapeDtypeStruct((ROWS, D), BF),
            jax.ShapeDtypeStruct((HALF_D, D), F32),
        ],
        in_specs=[ANY_SPEC] * 3,
        out_specs=[ANY_SPEC] * 3,
        scratch_shapes=[
            pltpu.VMEM((3, ROWS, D), BF),
            pltpu.VMEM((HALF_D, D), F32),
            pltpu.SemaphoreType.DMA((3, 4)),
            pltpu.SemaphoreType.DMA((3, 4)),
        ],
        compiler_params=pltpu.CompilerParams(vmem_limit_bytes=67043328),
        name="finish",
    )(layer_out, grad_input, grad_down)


def local(
    mel_panels,
    frames,
    target,
    conv_first,
    depth_a,
    point_a,
    depth_b,
    point_b,
    linear_weight,
    norm_gain,
    up_weight,
    depth_kernel,
    conv_gain,
    down_weight,
    cotangent,
):
    small = (
        conv_first,
        depth_a,
        point_a,
        depth_b,
        point_b,
        norm_gain.reshape(-1, 128),
        conv_gain.reshape(-1, 128),
        depth_kernel,
    )
    big = (linear_weight, up_weight, down_weight)
    windows, keep, band, full, other = exchange(frames[None], target[None], mel_panels, small, big)
    features = subsample(windows, band, *full[1:5], linear_weight, other[0])
    results = module(
        features,
        keep,
        cotangent,
        full[5],
        full[6],
        full[7],
        (up_weight, other[1]),
        (down_weight, other[2]),
    )
    return tuple(finish(*results))


def solution(mesh):
    placed = (
        P(("dp", "fsdp"), None),
        P(("dp", "fsdp")),
        P(("dp", "fsdp")),
        P(None, "fsdp"),
        P(None, "fsdp"),
        P(None, "fsdp"),
        P(None, "fsdp"),
        P(None, "fsdp"),
        P(None, "fsdp"),
        P("fsdp"),
        P(None, "fsdp"),
        P(None, "fsdp"),
        P("fsdp"),
        P("fsdp", None),
        P(("dp", "fsdp"), None),
    )
    return jax.shard_map(
        local,
        mesh=mesh,
        in_specs=placed,
        out_specs=(P(("dp", "fsdp"), None), P(("dp", "fsdp"), None), P("fsdp", None)),
        check_vma=False,
    )
```
